32 devices in a mesh: groups: 2 (over y), ctx: 4 (over z), heads: 4 (over x, core).
Axes of the slice: x: 2, y: 2, z: 4, core: 2. Of those that a mesh axis runs over, the one named last changes fastest.
Arguments:
- queries: bfloat16 [4096, 2048], P(('groups', 'ctx'), 'heads'), parts along dimension 0, may hold values from -6 to 6
- key_rows: bfloat16 [4096, 2048], P(('groups', 'ctx'), 'heads'), parts along dimension 0, may hold values from -6 to 6
- values: bfloat16 [4096, 2048], P(('groups', 'ctx'), 'heads'), parts along dimension 0, may hold values from -6 to 6
- memory_in: float32 [32, 128, 128], P(('groups', 'heads')), parts along dimension 0, may hold values from -1024 to 1024
- norm_in: float32 [32, 128], P(('groups', 'heads')), parts along dimension 0, may hold values from 256 to 1024
- decays: float32 [8, 16], P(('groups', 'ctx'), 'heads'), parts along dimension 0, may hold values from 0.05 to 1
- gate_bias: float32 [16], P('heads'), may hold values from -1.5 to 1.5
- out_weight: bfloat16 [2048, 2048], P('heads'), may hold values from -0.125 to 0.125
- out_grad: bfloat16 [4096, 2048], P(('groups', 'ctx'), 'heads'), parts along dimension 0, may hold values from -1.5 to 1.5
Outputs:
- output: bfloat16 [4096, 2048], P(('groups', 'ctx'), 'heads'), parts along dimension 0
- grad_query: bfloat16 [4096, 2048], P(('groups', 'ctx'), 'heads'), parts along dimension 0
- grad_key: bfloat16 [4096, 2048], P(('groups', 'ctx'), 'heads'), parts along dimension 0
- grad_value: bfloat16 [4096, 2048], P(('groups', 'ctx'), 'heads'), parts along dimension 0
- grad_weight: float32 [4096, 2048], P(('groups', 'heads'), 'ctx'), parts along dimension 0
The draws below stay inside these ranges and needn't reach their ends.
There are 2 independent parts, one for each index of `groups`. The reference program is written for one: setup_inputs(seed, part) draws one part's arguments, and reference() takes and returns one part's arrays. A program takes and returns all parts, laid end to end along the dimension named above; an argument that names none is the same for every part. Nothing has to cross between parts.
All inputs are finite; a program needn't handle non-finite values.
Results may differ from the reference program's by a relative error of at most 0.012.
Values may be sent and summed in bfloat16 or wider, within the bound.
A program may use at most 64 MiB of HBM per device.

```python
import math
import jax
import jax.numpy as jnp
from jax import lax

D = 2048
ATTENTION_HEADS = 16
HEAD = 128
SEG = 512
STREAM_SEGMENTS = 4
TOKENS = 2048
HD = 2048
N_HEADS = 4


def query_key_pair(key):
    base_key = jax.random.fold_in(key, 11)
    first, second = jax.random.split(base_key, 2)
    query_out = jax.random.truncated_normal(first, -5.0, 5.0, (TOKENS, HD), jnp.float32)
    key_out = jax.random.truncated_normal(second, -5.0, 5.0, (TOKENS, HD), jnp.float32)
    return (query_out, key_out)


def draw_queries(key, part):
    return query_key_pair(key)[0].astype(jnp.bfloat16)


def draw_key_rows(key, part):
    return query_key_pair(key)[1].astype(jnp.bfloat16)


def draw_values(key, part):
    first, second = jax.random.split(jax.random.fold_in(key, 23))
    offsets = jax.random.uniform(second, (STREAM_SEGMENTS, 1, HD), minval=-1.5, maxval=1.5)
    noise = jax.random.truncated_normal(first, -4.0, 4.0, (STREAM_SEGMENTS, SEG, HD), jnp.float32)
    return (noise + offsets).reshape(TOKENS, HD).astype(jnp.bfloat16)


def memory_pair(key):
    first, second = jax.random.split(jax.random.fold_in(key, 53))
    low = jnp.log(0.5 * SEG)
    high = jnp.log(2.0 * SEG)
    norm_out = jnp.exp(jax.random.uniform(first, (ATTENTION_HEADS, HEAD), minval=low, maxval=high))
    mem_out = norm_out[:, :, None] * jax.random.uniform(second, (ATTENTION_HEADS, HEAD, HEAD), minval=-1.0, maxval=1.0)
    return (mem_out, norm_out)


def draw_memory_in(key, part):
    return memory_pair(key)[0].astype(jnp.float32)


def draw_norm_in(key, part):
    return memory_pair(key)[1].astype(jnp.float32)


def draw_decays(key, part):
    first, second, third_portion, fourth, fifth = jax.random.split(jax.random.fold_in(key, 37), 5)
    fast = jax.random.bernoulli(first, 0.5, (1, ATTENTION_HEADS))
    gradual_decay_rate = jnp.exp(-jax.random.uniform(second, (STREAM_SEGMENTS, ATTENTION_HEADS), minval=0.3, maxval=2.0) / STREAM_SEGMENTS)
    sudden_spike = jax.random.bernoulli(third_portion, 2.0 / STREAM_SEGMENTS, (STREAM_SEGMENTS, ATTENTION_HEADS))
    split_point = jax.random.uniform(fourth, (STREAM_SEGMENTS, ATTENTION_HEADS), minval=0.5, maxval=0.8)
    gradual_decay = jnp.where(sudden_spike, gradual_decay_rate * split_point, gradual_decay_rate)
    quick = jax.random.uniform(fifth, (STREAM_SEGMENTS, ATTENTION_HEADS), minval=0.05, maxval=0.35)
    return jnp.where(fast, quick, gradual_decay).astype(jnp.float32)


def strengthened(entries, key, source, target, parts, factor):
    owner, partner = [(jnp.arange(entries.shape[dim]) // (entries.shape[dim] // parts)).reshape([-1 if axis == dim else 1 for axis in range(entries.ndim)]) for dim in (source, target)]
    chosen = jax.random.permutation(key, parts)[partner]
    strong = (owner == chosen) | (owner == (partner + parts // 2) % parts)
    return jnp.where(strong, factor * entries, entries)


def steps_of(key, extent, cuts, low, high):
    gain, own = 1.0, jax.random.fold_in(key, 6)
    for position, parts in cuts:
        draws = jnp.exp(jax.random.uniform(jax.random.fold_in(own, position), (parts,), jnp.float32, low / len(cuts), high / len(cuts)))
        gain = gain * jnp.repeat(draws, extent[position] // parts).reshape([-1 if axis == position else 1 for axis in range(len(extent))])
    return gain


def scatter_about(stream_key, extent, scale, limit, shards=(), kind=jnp.bfloat16):
    factor_of = steps_of(stream_key, extent, shards, -0.22, 0.18) if shards else 1.0
    drawn = jax.random.normal(stream_key, extent, jnp.float32) * scale * factor_of
    return jnp.minimum(jnp.maximum(drawn, -limit), limit).astype(kind)


def gaussian_with(key, shape, scale, most, cuts, heavy, kind=jnp.bfloat16):
    values = scale * jax.random.normal(key, shape, jnp.float32)
    if cuts:
        values = values * steps_of(key, shape, cuts, -0.22, 0.18)
    return jnp.clip(strengthened(values, jax.random.fold_in(key, 3), *heavy), -most, most).astype(kind)


def setup_inputs(seed: int = 0, part: int = 0) -> dict:
    arg_keys = jax.random.split(jax.random.key(seed), 10)
    part_keys = jax.random.split(jax.random.fold_in(arg_keys[9], part), 10)
    queries = draw_queries(jax.random.fold_in(jax.random.fold_in(arg_keys[9], part), 71), part)
    key_rows = draw_key_rows(jax.random.fold_in(jax.random.fold_in(arg_keys[9], part), 71), part)
    values = draw_values(jax.random.fold_in(jax.random.fold_in(arg_keys[9], part), 71), part)
    memory_in = draw_memory_in(jax.random.fold_in(jax.random.fold_in(arg_keys[9], part), 71), part)
    norm_in = draw_norm_in(jax.random.fold_in(jax.random.fold_in(arg_keys[9], part), 71), part)
    decays = draw_decays(jax.random.fold_in(jax.random.fold_in(arg_keys[9], part), 71), part)
    gate_bias = jnp.clip(jax.random.uniform(arg_keys[6], (ATTENTION_HEADS,), jnp.float32, -1.5, 1.5) * steps_of(arg_keys[6], (ATTENTION_HEADS,), ((0, 4),), -0.4, 0.0), -1.5, 1.5)
    out_weight = scatter_about(arg_keys[7], (HD, D), HD ** -0.5, 0.125, ((0, 4),))
    out_grad = gaussian_with(part_keys[8], (TOKENS, D), 0.25, 1.5, ((0, 4), (1, 4)), (0, 1, 4, 2.0))
    return {"queries": queries, "key_rows": key_rows, "values": values, "memory_in": memory_in, "norm_in": norm_in, "decays": decays, "gate_bias": gate_bias, "out_weight": out_weight, "out_grad": out_grad}


HIGH = lax.Precision.HIGHEST

def feature(inner):
    return jnp.where(inner > 0, inner + 1.0, jnp.exp(jnp.minimum(inner, 0.0)))

def feature_slope(inner):
    return jnp.where(inner > 0, 1.0, jnp.exp(jnp.minimum(inner, 0.0)))

def segment_pieces(query_seg, key_seg, value_seg, state_mem, state_norm, gate_bias):
    scale = 1.0 / math.sqrt(HEAD)
    query_f = query_seg.astype(jnp.float32)
    key_f = key_seg.astype(jnp.float32)
    value_f = value_seg.astype(jnp.float32)
    query_feat = feature(query_f)
    numer = jnp.einsum('thi,hij->thj', query_feat, state_mem, precision=HIGH)
    denom = jnp.einsum('thi,hi->th', query_feat, state_norm, precision=HIGH)
    recall = numer / denom[..., None]
    scores = jnp.einsum('thd,shd->hts', query_f, key_f, precision=HIGH) * scale
    places = jnp.arange(SEG, dtype=jnp.int32)
    causal = (places[:, None] >= places[None, :])[None]
    peak = lax.optimization_barrier(jnp.max(jnp.where(causal, scores, -jnp.inf), axis=-1, keepdims=True))
    expo = jnp.where(causal, jnp.exp(scores - peak), 0.0)
    probs = expo / lax.optimization_barrier(jnp.sum(expo, axis=-1, keepdims=True))
    probs_half = probs.astype(jnp.bfloat16)
    local_out = jnp.einsum('hts,shd->thd', probs_half.astype(jnp.float32), value_f, precision=HIGH)
    mix = jax.nn.sigmoid(gate_bias)[None, :, None]
    mixed = (mix * recall + (1.0 - mix) * local_out).astype(jnp.bfloat16)
    return (mixed, probs, probs_half, recall, denom, query_feat)

def reference(queries, key_rows, values, memory_in, norm_in, decays, gate_bias, out_weight, out_grad):
    shape_four = (STREAM_SEGMENTS, SEG, ATTENTION_HEADS, HEAD)
    query_all = queries.reshape(shape_four)
    key_all = key_rows.reshape(shape_four)
    value_all = values.reshape(shape_four)
    key_feat = feature(key_all.astype(jnp.float32)).astype(jnp.bfloat16)
    upd_mem = jnp.einsum('sthi,sthj->shij', key_feat.astype(jnp.float32), value_all.astype(jnp.float32), precision=HIGH)
    upd_norm = lax.optimization_barrier(jnp.sum(key_feat.astype(jnp.float32), axis=1))

    def advance(carry, inputs):
        mem_now, norm_now = carry
        gate_now, upd_m, upd_n = inputs
        return ((gate_now[:, None, None] * mem_now + upd_m, gate_now[:, None] * norm_now + upd_n), (mem_now, norm_now))
    _, (mem_before, norm_before) = lax.scan(advance, (memory_in, norm_in), (decays, upd_mem, upd_norm))

    def forward_one(inputs):
        query_seg, key_seg, value_seg, state_mem, state_norm = inputs
        return segment_pieces(query_seg, key_seg, value_seg, state_mem, state_norm, gate_bias)[0]
    mixed = lax.map(forward_one, (query_all, key_all, value_all, mem_before, norm_before))
    mixed_flat = mixed.reshape(TOKENS, HD)
    group = HD // N_HEADS
    total = jnp.zeros((TOKENS, D), jnp.float32)
    for member in range(N_HEADS):
        partial_sum = jnp.dot(mixed_flat[:, member * group:(member + 1) * group], out_weight[member * group:(member + 1) * group], preferred_element_type=jnp.float32)
        total = total + partial_sum.astype(jnp.bfloat16).astype(jnp.float32)
    output = total.astype(jnp.bfloat16)
    grad_mixed = jnp.dot(out_grad, out_weight.T, preferred_element_type=jnp.float32)
    grad_weight = jnp.dot(mixed_flat.T, out_grad, preferred_element_type=jnp.float32)
    grad_mixed_all = grad_mixed.reshape(shape_four)
    scale = 1.0 / math.sqrt(HEAD)

    def backward_one(inputs):
        query_seg, key_seg, value_seg, state_mem, state_norm, grad_seg = inputs
        mixed_seg, probs, probs_half, recall, denom, query_feat = segment_pieces(query_seg, key_seg, value_seg, state_mem, state_norm, gate_bias)
        query_f = query_seg.astype(jnp.float32)
        key_f = key_seg.astype(jnp.float32)
        value_f = value_seg.astype(jnp.float32)
        mix = jax.nn.sigmoid(gate_bias)[None, :, None]
        grad_recall = mix * grad_seg
        grad_local = ((1.0 - mix) * grad_seg).astype(jnp.bfloat16).astype(jnp.float32)
        grad_probs = jnp.einsum('thd,shd->hts', grad_local, value_f, precision=HIGH)
        grad_value_att = jnp.einsum('hts,thd->shd', probs_half.astype(jnp.float32), grad_local, precision=HIGH)
        delta = lax.optimization_barrier(jnp.sum(probs * grad_probs, axis=-1, keepdims=True))
        grad_scores = (probs * (grad_probs - delta) * scale).astype(jnp.bfloat16).astype(jnp.float32)
        grad_query_att = jnp.einsum('hts,shd->thd', grad_scores, key_f, precision=HIGH)
        grad_key_att = jnp.einsum('hts,thd->shd', grad_scores, query_f, precision=HIGH)
        grad_numer = grad_recall / denom[..., None]
        grad_denom = -lax.optimization_barrier(jnp.sum(grad_recall * recall, axis=-1)) / denom
        grad_qfeat = jnp.einsum('thj,hij->thi', grad_numer, state_mem, precision=HIGH) + grad_denom[..., None] * state_norm[None]
        local_mem = jnp.einsum('thi,thj->hij', query_feat, grad_numer, precision=HIGH)
        local_norm = jnp.einsum('thi,th->hi', query_feat, grad_denom, precision=HIGH)
        grad_query = (grad_query_att + grad_qfeat * feature_slope(query_f)).astype(jnp.bfloat16)
        return (grad_query, grad_key_att, grad_value_att, local_mem, local_norm)
    grad_query, grad_key_att, grad_value_att, local_mem, local_norm = lax.map(backward_one, (query_all, key_all, value_all, mem_before, norm_before, grad_mixed_all))

    def retreat(carry, inputs):
        after_m, after_n = carry
        gate_now, loc_m, loc_n = inputs
        return ((loc_m + gate_now[:, None, None] * after_m, loc_n + gate_now[:, None] * after_n), (after_m, after_n))
    zero_state = (jnp.zeros((ATTENTION_HEADS, HEAD, HEAD), jnp.float32), jnp.zeros((ATTENTION_HEADS, HEAD), jnp.float32))
    _, (after_mem, after_norm) = lax.scan(retreat, zero_state, (decays, local_mem, local_norm), reverse=True)
    key_f = key_all.astype(jnp.float32)
    grad_kfeat = jnp.einsum('sthj,shij->sthi', value_all.astype(jnp.float32), after_mem, precision=HIGH) + after_norm[:, None]
    grad_key = (grad_key_att + grad_kfeat * feature_slope(key_f)).astype(jnp.bfloat16)
    grad_value = (grad_value_att + jnp.einsum('sthi,shij->sthj', key_feat.astype(jnp.float32), after_mem, precision=HIGH)).astype(jnp.bfloat16)
    return (output, grad_query.reshape(TOKENS, HD), grad_key.reshape(TOKENS, HD), grad_value.reshape(TOKENS, HD), grad_weight)
```

```python
import math

import jax
import jax.numpy as jnp
from jax import lax
from jax.experimental import pallas as pl
from jax.experimental.pallas import tpu as pltpu
from jax.sharding import PartitionSpec as P

HIGH = lax.Precision.HIGHEST


def shortened(value):

    def short(part):
        return part.astype(jnp.bfloat16) if part.dtype == jnp.float32 else part

    return jax.tree.map(short, value)


def feature(inner):
    return jnp.where(inner > 0, inner + 1.0, jnp.exp(jnp.minimum(inner, 0.0)))


def feature_slope(inner):
    return jnp.where(inner > 0, 1.0, jnp.exp(jnp.minimum(inner, 0.0)))


def gathered_prefix(stacked_gate, stacked_mem, stacked_norm, own_index, count, upward):
    order = jnp.arange(count, dtype=jnp.int32)
    term_pos = order[:, None]
    inner_pos = order[None, :]
    if upward:
        between = (inner_pos > term_pos) & (inner_pos < own_index)
        active = order < own_index
    else:
        between = (inner_pos < term_pos) & (inner_pos > own_index)
        active = order > own_index
    factor = jnp.prod(jnp.where(between[:, :, None], stacked_gate[None, :, :], 1.0), axis=1)
    weight = jnp.where(active[:, None], factor, 0.0)
    total_mem = jnp.einsum("th,thij->hij", weight, stacked_mem, precision=HIGH)
    total_norm = jnp.einsum("th,thi->hi", weight, stacked_norm, precision=HIGH)
    leading = jnp.prod(jnp.where(active[:, None], stacked_gate, 1.0), axis=0)
    return (leading, total_mem, total_norm)


def plain(queries, key_rows, values, memory_in, norm_in, decays, gate_bias, out_weight, out_grad):
    rows = queries.shape[0]
    heads_here = memory_in.shape[0]
    width = memory_in.shape[1]
    scale = 1.0 / math.sqrt(width)
    shape_three = (rows, heads_here, width)
    query_blk = queries.reshape(shape_three)
    key_blk = key_rows.reshape(shape_three)
    value_blk = values.reshape(shape_three)
    gate_now = decays[0]
    key_f = key_blk.astype(jnp.float32)
    key_feat = feature(key_f).astype(jnp.bfloat16)
    upd_mem = jnp.einsum("thi,thj->hij", key_feat, value_blk, preferred_element_type=jnp.float32)
    upd_norm = jnp.sum(key_feat.astype(jnp.float32), axis=0)
    all_gate, all_mem, all_norm = (
        lax.all_gather(gate_now[None].astype(jnp.bfloat16), "ctx", axis=0, tiled=True).astype(
            jnp.float32
        ),
        lax.all_gather(upd_mem[None].astype(jnp.bfloat16), "ctx", axis=0, tiled=True).astype(
            jnp.float32
        ),
        lax.all_gather(upd_norm[None].astype(jnp.bfloat16), "ctx", axis=0, tiled=True).astype(
            jnp.float32
        ),
    )
    leading, prior_mem, prior_norm = gathered_prefix(
        all_gate, all_mem, all_norm, lax.axis_index("ctx"), lax.axis_size("ctx"), True
    )
    state_mem = leading[:, None, None] * memory_in + prior_mem
    state_norm = leading[:, None] * norm_in + prior_norm
    query_f = query_blk.astype(jnp.float32)
    query_feat = feature(query_f)
    numer = jnp.einsum("thi,hij->thj", query_feat, state_mem, precision=HIGH)
    denom = jnp.einsum("thi,hi->th", query_feat, state_norm, precision=HIGH)
    recall = numer / denom[..., None]
    scores = (
        jnp.einsum("thd,shd->hts", query_blk, key_blk, preferred_element_type=jnp.float32) * scale
    )
    places = jnp.arange(rows, dtype=jnp.int32)
    causal = (places[:, None] >= places[None, :])[None]
    peak = jnp.max(jnp.where(causal, scores, -jnp.inf), axis=-1, keepdims=True)
    expo = jnp.where(causal, jnp.exp(scores - peak), 0.0)
    probs = expo / jnp.sum(expo, axis=-1, keepdims=True)
    probs_half = probs.astype(jnp.bfloat16)
    local_out = jnp.einsum(
        "hts,shd->thd", probs_half, value_blk, preferred_element_type=jnp.float32
    )
    mix = jax.nn.sigmoid(gate_bias)[None, :, None]
    mixed = (
        (mix * recall + (1.0 - mix) * local_out)
        .astype(jnp.bfloat16)
        .reshape(rows, heads_here * width)
    )
    partial_sum = jnp.dot(mixed, out_weight, preferred_element_type=jnp.float32)
    output = lax.psum_scatter(
        partial_sum.astype(jnp.bfloat16), "heads", scatter_dimension=1, tiled=True
    )
    piece = lax.all_gather(out_grad, "heads", axis=1, tiled=True)
    grad_mix = lax.dot_general(
        piece, out_weight, (((1,), (1,)), ((), ())), preferred_element_type=jnp.float32
    )
    block = lax.dot_general(
        mixed, piece, (((0,), (0,)), ((), ())), preferred_element_type=jnp.float32
    )
    grad_mix, collected = (grad_mix, block)
    grad_weight = lax.psum_scatter(
        collected.astype(jnp.bfloat16), "ctx", scatter_dimension=1, tiled=True
    ).astype(jnp.float32)
    grad_seg = grad_mix.reshape(shape_three)
    grad_recall = mix * grad_seg
    grad_local = ((1.0 - mix) * grad_seg).astype(jnp.bfloat16)
    grad_probs = jnp.einsum(
        "thd,shd->hts", grad_local, value_blk, preferred_element_type=jnp.float32
    )
    grad_value_att = jnp.einsum(
        "hts,thd->shd", probs_half, grad_local, preferred_element_type=jnp.float32
    )
    delta = jnp.sum(probs * grad_probs, axis=-1, keepdims=True)
    grad_scores = (probs * (grad_probs - delta) * scale).astype(jnp.bfloat16)
    grad_query_att = jnp.einsum(
        "hts,shd->thd", grad_scores, key_blk, preferred_element_type=jnp.float32
    )
    grad_key_att = jnp.einsum(
        "hts,thd->shd", grad_scores, query_blk, preferred_element_type=jnp.float32
    )
    grad_numer = grad_recall / denom[..., None]
    grad_denom = -jnp.sum(grad_recall * recall, axis=-1) / denom
    grad_qfeat = (
        jnp.einsum("thj,hij->thi", grad_numer, state_mem, precision=HIGH)
        + grad_denom[..., None] * state_norm[None]
    )
    local_mem = jnp.einsum("thi,thj->hij", query_feat, grad_numer, precision=HIGH)
    local_norm = jnp.einsum("thi,th->hi", query_feat, grad_denom, precision=HIGH)
    grad_query = (
        (grad_query_att + grad_qfeat * feature_slope(query_f))
        .astype(jnp.bfloat16)
        .reshape(rows, heads_here * width)
    )
    back_gate, back_mem, back_norm = (
        lax.all_gather(gate_now[None].astype(jnp.bfloat16), "ctx", axis=0, tiled=True).astype(
            jnp.float32
        ),
        lax.all_gather(shortened(local_mem[None]), "ctx", axis=0, tiled=True),
        lax.all_gather(shortened(local_norm[None]), "ctx", axis=0, tiled=True),
    )
    unused_lead, after_mem, after_norm = gathered_prefix(
        back_gate, back_mem, back_norm, lax.axis_index("ctx"), lax.axis_size("ctx"), False
    )
    value_f = value_blk.astype(jnp.float32)
    grad_kfeat = jnp.einsum("thj,hij->thi", value_f, after_mem, precision=HIGH) + after_norm[None]
    grad_key = (
        (grad_key_att + grad_kfeat * feature_slope(key_f))
        .astype(jnp.bfloat16)
        .reshape(rows, heads_here * width)
    )
    grad_value = (
        (
            grad_value_att
            + jnp.einsum("thi,hij->thj", key_feat.astype(jnp.float32), after_mem, precision=HIGH)
        )
        .astype(jnp.bfloat16)
        .reshape(rows, heads_here * width)
    )
    return (output, grad_query, grad_key, grad_value, grad_weight)


MESH = pl.DeviceIdType.MESH
F32 = jnp.float32
BF16 = jnp.bfloat16
HALF = 256
PAD = 16


def mm(left, right):
    return jnp.dot(left, right, preferred_element_type=F32)


def nt(left, right):
    return lax.dot_general(left, right, (((1,), (1,)), ((), ())), preferred_element_type=F32)


def fused(
    q_in, k_in, v_in, mem_in, norm_in, decay_in, gate_in, w_in, og_ref,
    out_ref, gq_ref, gk_ref, gv_ref, gw_ref,
    q_ref, k_ref, v_ref, mem_ref, norm_ref, w_ref, decay_ref, gate_ref,
    og_all, upd, state, local, after, up_send, up_recv, down_send, down_recv,
    probs, out_t, recall, own_out, grad_mix, mixed, mixed_t, grad_feat, gk_att, gv_att,
    rs_send, rs_recv, rs_merge, o_send, o_recv,
    og_s, og_r, up_s, up_r, down_s, down_r, rs_s, rs_r, merge_r, o_s, o_r, load_s,
):
    rows, cols = q_ref.shape
    heads_here, width = mem_ref.shape[0], mem_ref.shape[1]
    scale = 1.0 / math.sqrt(width)
    me = lax.axis_index("heads")
    place = lax.axis_index("ctx")
    partner = me + 1 - 2 * lax.rem(me, 2)
    cross = lax.rem(me + 2, 4)
    far = lax.rem(partner + 2, 4)
    low = 1 - lax.div(place, 2)
    is_end = (place == 0) | (place == 3)
    is_mid = (place == 1) | (place == 2)
    near = 1 + lax.div(place, 2)

    def lanes(h):
        return pl.ds(pl.multiple_of(h * width, width), width)

    def block(j):
        return pl.ds(pl.multiple_of(j * cols, cols), cols)

    def send(src, dst, s, r, **where):
        return pltpu.make_async_remote_copy(
            src_ref=src, dst_ref=dst, send_sem=s, recv_sem=r, device_id=where, device_id_type=MESH
        )

    def mix_of(h):
        return 1.0 / (1.0 + jnp.exp(-jnp.full((1, width), gate_ref[0, h], F32)))

    loads = [
        pltpu.make_async_copy(src, dst, load_s.at[i])
        for i, (src, dst) in enumerate(
            (
                (k_in, k_ref), (v_in, v_ref), (q_in, q_ref), (mem_in, mem_ref),
                (norm_in, norm_ref), (w_in, w_ref), (og_ref, og_all.at[:, block(me)]),
                (decay_in, decay_ref), (gate_in, gate_ref),
            )
        )
    ]
    for i in (6, 0, 1, 2, 3, 4, 7, 8, 5):
        loads[i].start()

    barrier = pltpu.get_barrier_semaphore()
    for peer in (partner, cross):
        pl.semaphore_signal(barrier, inc=1, device_id={"heads": peer}, device_id_type=MESH)
    for step in (1, 2, 3):
        pl.semaphore_signal(
            barrier, inc=1, device_id={"ctx": lax.rem(place + step, 4)}, device_id_type=MESH
        )
    pl.semaphore_wait(barrier, 5)

    def rows_of(c):
        return pl.ds(c * HALF, HALF)

    og_cross, og_pair, og_relay = [], [], []
    for c in range(rows // HALF):
        mine = og_all.at[rows_of(c), block(me)]
        theirs = og_all.at[rows_of(c), block(cross)]
        og_cross.append(
            send(mine, mine, og_s.at[0, c], og_r.at[0, c], heads=cross)
        )
        og_pair.append(
            send(mine, mine, og_s.at[1, c], og_r.at[1, c], heads=partner)
        )
        og_relay.append(send(theirs, theirs, og_s.at[2, c], og_r.at[2, c], heads=partner))
    loads[6].wait()
    for copy in og_cross + og_pair:
        copy.start()
    loads[0].wait()
    loads[1].wait()

    def update(h, carry):
        key_feat = feature(k_ref[:, lanes(h)].astype(F32)).astype(BF16)
        upd[h, :width] = mm(key_feat.T, v_ref[:, lanes(h)])
        total = jnp.sum(key_feat.astype(F32), axis=0, keepdims=True)
        upd[h, width:] = jnp.broadcast_to(total, (PAD, width))
        return carry

    lax.fori_loop(0, heads_here, update, 0)

    def up_copy(h, target):
        return send(up_send.at[h], up_recv.at[h], up_s.at[h], up_r.at[h], ctx=target)

    def up_step(index):
        @pl.when(place == index)
        def _():
            for h in range(heads_here):
                if index == 0:
                    state[h, :width] = mem_ref[h]
                    state[h, width:] = jnp.broadcast_to(norm_ref[h : h + 1, :], (PAD, width))
                else:
                    up_copy(h, index - 1).wait_recv()
                    state[h] = up_recv[h].astype(F32)
                if index < 3:
                    up_send[h] = (decay_ref[0, h] * state[h] + upd[h]).astype(BF16)
                    up_copy(h, index + 1).start()

    def down_copy(h, target):
        return send(down_send.at[h], down_recv.at[h], down_s.at[h], down_r.at[h], ctx=target)

    def down_step(index):
        @pl.when(place == index)
        def _():
            if index == 3:
                after[...] = jnp.zeros_like(after)
            for h in range(heads_here):
                if index < 3:
                    down_copy(h, index + 1).wait_recv()
                    after[h] = down_recv[h].astype(F32)
                if index > 0:
                    down_send[h] = (decay_ref[0, h] * after[h] + local[h]).astype(BF16)
                    down_copy(h, index - 1).start()

    keep = lax.broadcasted_iota(jnp.int32, (HALF, HALF), 0) <= lax.broadcasted_iota(
        jnp.int32, (HALF, HALF), 1
    )
    factor = scale * math.log2(math.e)
    parts = rows // HALF

    def span(j):
        return slice(j * HALF, (j + 1) * HALF)

    def forward(h, carry):
        values_t = v_ref[:, lanes(h)].T
        for b in range(parts):
            query = q_ref[span(b), lanes(h)]
            scores = [nt(k_ref[span(j), lanes(h)], query) for j in range(b + 1)]
            scores[b] = jnp.where(keep, scores[b], -1e30)
            peak = jnp.max(scores[0], axis=0, keepdims=True)
            for piece in scores[1:]:
                peak = jnp.maximum(peak, jnp.max(piece, axis=0, keepdims=True))
            expo = [jnp.exp2((piece - peak) * factor) for piece in scores]
            total = sum(jnp.sum(piece, axis=0, keepdims=True) for piece in expo)
            inverse = 1.0 / total
            acc = None
            for j in range(b + 1):
                prob = (expo[j] * inverse).astype(BF16)
                probs[h, span(j), span(b)] = prob
                term = mm(values_t[:, span(j)], prob)
                acc = term if acc is None else acc + term
            out_t[h, :, span(b)] = acc
        return carry

    for i in (3, 4, 7, 8):
        loads[i].wait()
    up_step(0)
    loads[2].wait()
    lax.fori_loop(0, 2, forward, 0)
    up_step(1)
    lax.fori_loop(2, heads_here, forward, 0)
    up_step(2)
    og_cross[0].wait_recv()
    og_relay[0].start()
    up_step(3)

    def recall_step(h, carry):
        mem = state[h, :width].astype(BF16)
        norm = state[h, width : width + 1]
        query_feat = feature(q_ref[:, lanes(h)].astype(F32))
        inverse = 1.0 / jnp.sum(query_feat * norm, axis=1, keepdims=True)
        recalled = mm(query_feat.astype(BF16), mem) * inverse
        recall[:, lanes(h)] = recalled
        mix = mix_of(h)
        both = (mix * recalled + (1.0 - mix) * out_t[h].T).astype(BF16)
        mixed[:, lanes(h)] = both
        mixed_t[pl.ds(pl.multiple_of(h * width, width), width), :] = both.T
        return carry

    lax.fori_loop(0, heads_here, recall_step, 0)
    og_cross[1].wait_recv()
    og_relay[1].start()
    for c in range(rows // HALF):
        og_pair[c].wait_recv()
        og_relay[c].wait_recv()

    def grad_block(j, carry):
        here = pl.ds(pl.multiple_of(j * HALF, HALF), HALF)
        grad_mix[:, here] = nt(og_all[...], w_ref[here, :])
        return carry

    loads[5].wait()
    lax.fori_loop(0, cols // HALF, grad_block, 0)

    def memory_step(h, carry):
        mem = state[h, :width].astype(BF16)
        norm = state[h, width : width + 1]
        query = q_ref[:, lanes(h)].astype(F32)
        query_feat = feature(query)
        inverse = 1.0 / jnp.sum(query_feat * norm, axis=1, keepdims=True)
        grad_recall = mix_of(h) * grad_mix[:, lanes(h)]
        grad_numer = (grad_recall * inverse).astype(BF16)
        grad_denom = -jnp.sum(grad_recall * recall[:, lanes(h)], axis=1, keepdims=True) * inverse
        grad_feat[:, lanes(h)] = (nt(grad_numer, mem) + grad_denom * norm) * feature_slope(query)
        local[h, :width] = mm(query_feat.astype(BF16).T, grad_numer)
        total = jnp.sum(query_feat * grad_denom, axis=0, keepdims=True)
        local[h, width:] = jnp.broadcast_to(total, (PAD, width))
        return carry

    lax.fori_loop(0, heads_here, memory_step, 0)
    down_step(3)

    def rs_copy(i, target):
        return send(rs_send.at[i], rs_recv.at[place], rs_s.at[i], rs_r.at[place], ctx=target)

    def merge_copy(target):
        return send(rs_send.at[0], rs_merge, rs_s.at[0], merge_r.at[0], ctx=target)

    def target_of(i):
        return i * (1 - low) + (3 - i) * low

    for i in range(4):
        value = mm(mixed_t[...], og_all[:, block(target_of(i))])
        if i == 0:
            rs_send[0] = value.astype(BF16)

            @pl.when(is_end)
            def _():
                merge_copy(near).start()

        elif i == 1:
            rs_send[1] = value.astype(BF16)

            @pl.when(place == 1)
            def _():
                rs_copy(1, target_of(1)).start()

        else:
            own = is_mid if i == 2 else is_end
            other = is_end if i == 2 else is_mid

            @pl.when(own)
            def _():
                gw_ref[...] = value

            @pl.when(other)
            def _():
                rs_send[i] = value.astype(BF16)

            if i == 3:

                @pl.when(place == 2)
                def _():
                    rs_copy(3, target_of(3)).start()

    down_step(2)

    @pl.when(place == 2)
    def _():
        rs_copy(1, target_of(1)).start()

    o_far = send(o_send.at[0], o_recv.at[0], o_s.at[0], o_r.at[0], heads=partner)
    o_pair = send(o_send.at[1], o_recv.at[1], o_s.at[1], o_r.at[1], heads=partner)
    o_cross = send(o_send.at[2], o_recv.at[2], o_s.at[2], o_r.at[2], heads=cross)
    o_send[0] = mm(mixed[...], w_ref[:, block(far)]).astype(BF16)
    o_far.start()
    o_send[1] = mm(mixed[...], w_ref[:, block(partner)]).astype(BF16)
    o_pair.start()
    value = mm(mixed[...], w_ref[:, block(cross)])
    down_step(1)

    @pl.when(place == 1)
    def _():
        rs_copy(3, target_of(3)).start()

    o_far.wait_recv()
    o_send[2] = (value + o_recv[0].astype(F32)).astype(BF16)
    o_cross.start()
    own_out[...] = mm(mixed[...], w_ref[:, block(me)])

    def backward(h, carry):
        mix = mix_of(h)
        grad_local = ((1.0 - mix) * grad_mix[:, lanes(h)]).astype(BF16)
        grad_t = grad_local.T
        delta = jnp.sum(grad_t.astype(F32) * out_t[h], axis=0, keepdims=True)
        keys_t = k_ref[:, lanes(h)].T
        for b in range(parts):
            query = q_ref[span(b), lanes(h)]
            acc = None
            for j in range(b + 1):
                prob = probs[h, span(j), span(b)]
                grad_prob = mm(v_ref[span(j), lanes(h)], grad_t[:, span(b)])
                grad_score = (prob.astype(F32) * (grad_prob - delta[:, span(b)]) * scale).astype(
                    BF16
                )
                term = mm(keys_t[:, span(j)], grad_score)
                acc = term if acc is None else acc + term
                key_term = mm(grad_score, query)
                value_term = mm(prob, grad_local[span(b), :])
                if b == j:
                    gk_att[span(j), lanes(h)] = key_term
                    gv_att[span(j), lanes(h)] = value_term
                else:
                    gk_att[span(j), lanes(h)] += key_term
                    gv_att[span(j), lanes(h)] += value_term
            gq_ref[span(b), lanes(h)] = (acc.T + grad_feat[span(b), lanes(h)]).astype(BF16)
        return carry

    def merge_step():
        @pl.when(is_mid)
        def _():
            merge_copy(near).wait_recv()
            rs_send[0] = (rs_send[0].astype(F32) + rs_merge[...].astype(F32)).astype(BF16)
            rs_copy(0, target_of(0)).start()

        @pl.when(is_end)
        def _():
            merge_copy(near).wait_send()
            rs_copy(1, target_of(1)).start()
            rs_copy(2, target_of(2)).start()

    lax.fori_loop(0, 2, backward, 0)
    merge_step()
    lax.fori_loop(2, heads_here, backward, 0)
    o_pair.wait_recv()
    o_cross.wait_recv()
    out_ref[...] = (own_out[...] + o_recv[1].astype(F32) + o_recv[2].astype(F32)).astype(BF16)
    down_step(0)

    def finish(h, carry):
        mem = after[h, :width].astype(BF16)
        key = k_ref[:, lanes(h)].astype(F32)
        value = v_ref[:, lanes(h)]
        grad_kfeat = nt(value, mem) + after[h, width : width + 1]
        gk_ref[:, lanes(h)] = (gk_att[:, lanes(h)] + grad_kfeat * feature_slope(key)).astype(BF16)
        key_feat = feature(key).astype(BF16)
        gv_ref[:, lanes(h)] = (gv_att[:, lanes(h)] + mm(key_feat, mem)).astype(BF16)
        return carry

    lax.fori_loop(0, heads_here, finish, 0)

    def collect(sources):
        for source in sources:
            pltpu.make_async_remote_copy(
                src_ref=rs_send.at[1], dst_ref=rs_recv.at[source], send_sem=rs_s.at[1],
                recv_sem=rs_r.at[source], device_id={"ctx": near}, device_id_type=MESH,
            ).wait_recv()
        gw_ref[...] += sum(rs_recv[source].astype(F32) for source in sources)

    @pl.when(is_end)
    def _():
        collect((1, 2))

    @pl.when(place == 1)
    def _():
        collect((0, 2, 3))

    @pl.when(place == 2)
    def _():
        collect((0, 1, 3))

    for copy in (*og_cross, *og_pair, *og_relay, o_far, o_pair, o_cross):
        copy.wait_send()

    @pl.when(place < 3)
    def _():
        for h in range(heads_here):
            up_copy(h, near).wait_send()

    @pl.when(place > 0)
    def _():
        for h in range(heads_here):
            down_copy(h, near).wait_send()

    for i in range(3):
        if i == 2:
            @pl.when(is_end)
            def _():
                rs_copy(2, near).wait_send()

            @pl.when(is_mid)
            def _():
                rs_copy(3, near).wait_send()
        elif i == 1:
            rs_copy(1, near).wait_send()
        else:

            @pl.when(is_mid)
            def _():
                rs_copy(0, near).wait_send()


def settle(*refs):
    sems = refs[-1]
    count = len(refs) // 2
    copies = [
        pltpu.make_async_copy(refs[i], refs[count + i], sems.at[i]) for i in range(count)
    ]
    for copy in copies:
        copy.start()
    for copy in copies:
        copy.wait()


def shards(queries, key_rows, values, memory_in, norm_in, decays, gate_bias, out_weight, out_grad):
    rows, cols = queries.shape
    heads_here, width = memory_in.shape[0], memory_in.shape[1]
    if (
        lax.axis_size("ctx") != 4
        or lax.axis_size("heads") != 4
        or rows != 2 * HALF
        or cols != rows
        or heads_here != 4
        or width != 128
    ):
        return plain(
            queries, key_rows, values, memory_in, norm_in, decays, gate_bias, out_weight, out_grad
        )
    wide = out_weight.shape[1]
    free = pl.BlockSpec(memory_space=pl.ANY)
    small = (heads_here, width + PAD, width)
    half = jax.ShapeDtypeStruct((rows, cols), BF16)
    dma = pltpu.SemaphoreType.DMA
    shapes = (half, half, half, half, jax.ShapeDtypeStruct((cols, cols), F32))
    held = tuple(pltpu.VMEM(x.shape, x.dtype) for x in shapes)
    results = pl.pallas_call(
        fused,
        out_shape=held,
        in_specs=[free] * 9,
        out_specs=(pl.BlockSpec(memory_space=pltpu.VMEM),) * 5,
        scratch_shapes=[
            pltpu.VMEM((rows, cols), BF16),
            pltpu.VMEM((rows, cols), BF16),
            pltpu.VMEM((rows, cols), BF16),
            pltpu.VMEM((heads_here, width, width), F32),
            pltpu.VMEM((heads_here, width), F32),
            pltpu.VMEM((cols, wide), BF16),
            pltpu.SMEM((1, heads_here), F32),
            pltpu.SMEM((1, heads_here), F32),
            pltpu.VMEM((rows, wide), BF16),
            pltpu.VMEM(small, F32),
            pltpu.VMEM(small, F32),
            pltpu.VMEM(small, F32),
            pltpu.VMEM(small, F32),
            pltpu.VMEM(small, BF16),
            pltpu.VMEM(small, BF16),
            pltpu.VMEM(small, BF16),
            pltpu.VMEM(small, BF16),
            pltpu.VMEM((heads_here, rows, rows), BF16),
            pltpu.VMEM((heads_here, width, rows), F32),
            pltpu.VMEM((rows, cols), F32),
            pltpu.VMEM((rows, cols), F32),
            pltpu.VMEM((rows, cols), F32),
            pltpu.VMEM((rows, cols), BF16),
            pltpu.VMEM((cols, rows), BF16),
            pltpu.VMEM((rows, cols), F32),
            pltpu.VMEM((rows, cols), F32),
            pltpu.VMEM((rows, cols), F32),
            pltpu.VMEM((4, cols, cols), BF16),
            pltpu.VMEM((4, cols, cols), BF16),
            pltpu.VMEM((cols, cols), BF16),
            pltpu.VMEM((3, rows, cols), BF16),
            pltpu.VMEM((3, rows, cols), BF16),
            dma((3, 2)), dma((3, 2)),
            dma((4,)), dma((4,)),
            dma((4,)), dma((4,)),
            dma((4,)), dma((4,)), dma((1,)),
            dma((3,)), dma((3,)), dma((9,)),
        ],
        compiler_params=pltpu.CompilerParams(
            collective_id=0, has_side_effects=True, vmem_limit_bytes=48 << 20
        ),
    )(
        *(
            pltpu.with_memory_space_constraint(x, pltpu.HBM)
            for x in (
                queries, key_rows, values, memory_in, norm_in, decays,
                gate_bias.reshape(1, heads_here), out_weight, out_grad,
            )
        )
    )
    results = [pltpu.with_memory_space_constraint(x, pltpu.VMEM) for x in results]
    return pl.pallas_call(
        settle,
        out_shape=shapes,
        in_specs=[pl.BlockSpec(memory_space=pltpu.VMEM)] * 5,
        out_specs=(free,) * 5,
        scratch_shapes=[dma((5,))],
    )(*results)


def solution(mesh):
    return jax.shard_map(
        shards,
        mesh=mesh,
        in_specs=(
            P(("groups", "ctx"), "heads"),
            P(("groups", "ctx"), "heads"),
            P(("groups", "ctx"), "heads"),
            P(("groups", "heads"), None, None),
            P(("groups", "heads"), None),
            P(("groups", "ctx"), "heads"),
            P("heads"),
            P("heads", None),
            P(("groups", "ctx"), "heads"),
        ),
        out_specs=(
            P(("groups", "ctx"), "heads"),
            P(("groups", "ctx"), "heads"),
            P(("groups", "ctx"), "heads"),
            P(("groups", "ctx"), "heads"),
            P(("groups", "heads"), "ctx"),
        ),
        check_vma=False,
    )
```

```python
import math

import jax
import jax.numpy as jnp
from jax import lax
from jax.experimental import pallas as pl
from jax.experimental.pallas import tpu as pltpu
from jax.sharding import PartitionSpec as P

HIGH = lax.Precision.HIGHEST


def shortened(value):

    def short(part):
        return part.astype(jnp.bfloat16) if part.dtype == jnp.float32 else part

    return jax.tree.map(short, value)


def feature(inner):
    return jnp.where(inner > 0, inner + 1.0, jnp.exp(jnp.minimum(inner, 0.0)))


def feature_slope(inner):
    return jnp.where(inner > 0, 1.0, jnp.exp(jnp.minimum(inner, 0.0)))


def gathered_prefix(stacked_gate, stacked_mem, stacked_norm, own_index, count, upward):
    order = jnp.arange(count, dtype=jnp.int32)
    term_pos = order[:, None]
    inner_pos = order[None, :]
    if upward:
        between = (inner_pos > term_pos) & (inner_pos < own_index)
        active = order < own_index
    else:
        between = (inner_pos < term_pos) & (inner_pos > own_index)
        active = order > own_index
    factor = jnp.prod(jnp.where(between[:, :, None], stacked_gate[None, :, :], 1.0), axis=1)
    weight = jnp.where(active[:, None], factor, 0.0)
    total_mem = jnp.einsum("th,thij->hij", weight, stacked_mem, precision=HIGH)
    total_norm = jnp.einsum("th,thi->hi", weight, stacked_norm, precision=HIGH)
    leading = jnp.prod(jnp.where(active[:, None], stacked_gate, 1.0), axis=0)
    return (leading, total_mem, total_norm)


def plain(queries, key_rows, values, memory_in, norm_in, decays, gate_bias, out_weight, out_grad):
    rows = queries.shape[0]
    heads_here = memory_in.shape[0]
    width = memory_in.shape[1]
    scale = 1.0 / math.sqrt(width)
    shape_three = (rows, heads_here, width)
    query_blk = queries.reshape(shape_three)
    key_blk = key_rows.reshape(shape_three)
    value_blk = values.reshape(shape_three)
    gate_now = decays[0]
    key_f = key_blk.astype(jnp.float32)
    key_feat = feature(key_f).astype(jnp.bfloat16)
    upd_mem = jnp.einsum("thi,thj->hij", key_feat, value_blk, preferred_element_type=jnp.float32)
    upd_norm = jnp.sum(key_feat.astype(jnp.float32), axis=0)
    all_gate, all_mem, all_norm = (
        lax.all_gather(gate_now[None].astype(jnp.bfloat16), "ctx", axis=0, tiled=True).astype(
            jnp.float32
        ),
        lax.all_gather(upd_mem[None].astype(jnp.bfloat16), "ctx", axis=0, tiled=True).astype(
            jnp.float32
        ),
        lax.all_gather(upd_norm[None].astype(jnp.bfloat16), "ctx", axis=0, tiled=True).astype(
            jnp.float32
        ),
    )
    leading, prior_mem, prior_norm = gathered_prefix(
        all_gate, all_mem, all_norm, lax.axis_index("ctx"), lax.axis_size("ctx"), True
    )
    state_mem = leading[:, None, None] * memory_in + prior_mem
    state_norm = leading[:, None] * norm_in + prior_norm
    query_f = query_blk.astype(jnp.float32)
    query_feat = feature(query_f)
    numer = jnp.einsum("thi,hij->thj", query_feat, state_mem, precision=HIGH)
    denom = jnp.einsum("thi,hi->th", query_feat, state_norm, precision=HIGH)
    recall = numer / denom[..., None]
    scores = (
        jnp.einsum("thd,shd->hts", query_blk, key_blk, preferred_element_type=jnp.float32) * scale
    )
    places = jnp.arange(rows, dtype=jnp.int32)
    causal = (places[:, None] >= places[None, :])[None]
    peak = jnp.max(jnp.where(causal, scores, -jnp.inf), axis=-1, keepdims=True)
    expo = jnp.where(causal, jnp.exp(scores - peak), 0.0)
    probs = expo / jnp.sum(expo, axis=-1, keepdims=True)
    probs_half = probs.astype(jnp.bfloat16)
    local_out = jnp.einsum(
        "hts,shd->thd", probs_half, value_blk, preferred_element_type=jnp.float32
    )
    mix = jax.nn.sigmoid(gate_bias)[None, :, None]
    mixed = (
        (mix * recall + (1.0 - mix) * local_out)
        .astype(jnp.bfloat16)
        .reshape(rows, heads_here * width)
    )
    partial_sum = jnp.dot(mixed, out_weight, preferred_element_type=jnp.float32)
    output = lax.psum_scatter(
        partial_sum.astype(jnp.bfloat16), "heads", scatter_dimension=1, tiled=True
    )
    piece = lax.all_gather(out_grad, "heads", axis=1, tiled=True)
    grad_mix = lax.dot_general(
        piece, out_weight, (((1,), (1,)), ((), ())), preferred_element_type=jnp.float32
    )
    block = lax.dot_general(
        mixed, piece, (((0,), (0,)), ((), ())), preferred_element_type=jnp.float32
    )
    grad_mix, collected = (grad_mix, block)
    grad_weight = lax.psum_scatter(
        collected.astype(jnp.bfloat16), "ctx", scatter_dimension=1, tiled=True
    ).astype(jnp.float32)
    grad_seg = grad_mix.reshape(shape_three)
    grad_recall = mix * grad_seg
    grad_local = ((1.0 - mix) * grad_seg).astype(jnp.bfloat16)
    grad_probs = jnp.einsum(
        "thd,shd->hts", grad_local, value_blk, preferred_element_type=jnp.float32
    )
    grad_value_att = jnp.einsum(
        "hts,thd->shd", probs_half, grad_local, preferred_element_type=jnp.float32
    )
    delta = jnp.sum(probs * grad_probs, axis=-1, keepdims=True)
    grad_scores = (probs * (grad_probs - delta) * scale).astype(jnp.bfloat16)
    grad_query_att = jnp.einsum(
        "hts,shd->thd", grad_scores, key_blk, preferred_element_type=jnp.float32
    )
    grad_key_att = jnp.einsum(
        "hts,thd->shd", grad_scores, query_blk, preferred_element_type=jnp.float32
    )
    grad_numer = grad_recall / denom[..., None]
    grad_denom = -jnp.sum(grad_recall * recall, axis=-1) / denom
    grad_qfeat = (
        jnp.einsum("thj,hij->thi", grad_numer, state_mem, precision=HIGH)
        + grad_denom[..., None] * state_norm[None]
    )
    local_mem = jnp.einsum("thi,thj->hij", query_feat, grad_numer, precision=HIGH)
    local_norm = jnp.einsum("thi,th->hi", query_feat, grad_denom, precision=HIGH)
    grad_query = (
        (grad_query_att + grad_qfeat * feature_slope(query_f))
        .astype(jnp.bfloat16)
        .reshape(rows, heads_here * width)
    )
    back_gate, back_mem, back_norm = (
        lax.all_gather(gate_now[None].astype(jnp.bfloat16), "ctx", axis=0, tiled=True).astype(
            jnp.float32
        ),
        lax.all_gather(shortened(local_mem[None]), "ctx", axis=0, tiled=True),
        lax.all_gather(shortened(local_norm[None]), "ctx", axis=0, tiled=True),
    )
    unused_lead, after_mem, after_norm = gathered_prefix(
        back_gate, back_mem, back_norm, lax.axis_index("ctx"), lax.axis_size("ctx"), False
    )
    value_f = value_blk.astype(jnp.float32)
    grad_kfeat = jnp.einsum("thj,hij->thi", value_f, after_mem, precision=HIGH) + after_norm[None]
    grad_key = (
        (grad_key_att + grad_kfeat * feature_slope(key_f))
        .astype(jnp.bfloat16)
        .reshape(rows, heads_here * width)
    )
    grad_value = (
        (
            grad_value_att
            + jnp.einsum("thi,hij->thj", key_feat.astype(jnp.float32), after_mem, precision=HIGH)
        )
        .astype(jnp.bfloat16)
        .reshape(rows, heads_here * width)
    )
    return (output, grad_query, grad_key, grad_value, grad_weight)


MESH = pl.DeviceIdType.MESH
F32 = jnp.float32
BF16 = jnp.bfloat16
HALF = 256
PAD = 16


def mm(left, right):
    return jnp.dot(left, right, preferred_element_type=F32)


def nt(left, right):
    return lax.dot_general(left, right, (((1,), (1,)), ((), ())), preferred_element_type=F32)


def fused(
    q_in, k_in, v_in, mem_in, norm_in, decay_in, gate_in, w_in, og_ref,
    out_ref, gq_ref, gk_ref, gv_ref, gw_ref,
    q_ref, k_ref, v_ref, mem_ref, norm_ref, w_ref, decay_ref, gate_ref,
    og_all, og_end, upd, state, local, after, up_send, up_recv, down_send, down_recv,
    probs, out_t, recall, own_out, grad_mix, mixed, mixed_t, mixed_end, grad_feat, gk_att, gv_att,
    sum_send, sum_recv, fin_send, o_send, o_recv,
    og_s, og_r, end_s, end_r, mix_s, mix_r, up_s, up_r, down_s, down_r, sum_s, sum_r, fin_s, fin_r,
    o_s, o_r, load_s,
):
    rows, cols = q_ref.shape
    heads_here, width = mem_ref.shape[0], mem_ref.shape[1]
    scale = 1.0 / math.sqrt(width)
    me = lax.axis_index("heads")
    place = lax.axis_index("ctx")
    partner = me + 1 - 2 * lax.rem(me, 2)
    cross = lax.rem(me + 2, 4)
    far = lax.rem(partner + 2, 4)
    is_end = (place == 0) | (place == 3)
    is_mid = (place == 1) | (place == 2)
    near = 1 + lax.div(place, 2)
    edge = 3 * lax.div(place, 2)
    side = lax.div(me, 2)
    holds_outer = (me == 0) | (me == 3)
    holds_inner = (me == 1) | (me == 2)
    ours = (3 * side, 1 + side)
    theirs = (3 - 3 * side, 2 - side)
    part = pl.ds(pl.multiple_of(lax.rem(me, 2) * HALF, HALF), HALF)

    def lanes(h):
        return pl.ds(pl.multiple_of(h * width, width), width)

    def block(j):
        return pl.ds(pl.multiple_of(j * cols, cols), cols)

    def send(src, dst, s, r, **where):
        return pltpu.make_async_remote_copy(
            src_ref=src, dst_ref=dst, send_sem=s, recv_sem=r, device_id=where, device_id_type=MESH
        )

    def mix_of(h):
        return 1.0 / (1.0 + jnp.exp(-jnp.full((1, width), gate_ref[0, h], F32)))

    loads = [
        pltpu.make_async_copy(src, dst, load_s.at[i])
        for i, (src, dst) in enumerate(
            (
                (k_in, k_ref), (v_in, v_ref), (q_in, q_ref), (mem_in, mem_ref),
                (norm_in, norm_ref), (w_in, w_ref), (og_ref, og_all.at[:, block(me)]),
                (decay_in, decay_ref), (gate_in, gate_ref),
            )
        )
    ]
    for i in (6, 0, 1, 2, 3, 4, 7, 8, 5):
        loads[i].start()

    barrier = pltpu.get_barrier_semaphore()
    for peer in (partner, cross):
        pl.semaphore_signal(barrier, inc=1, device_id={"heads": peer}, device_id_type=MESH)
    for step in (-1, 1):

        @pl.when((place + step >= 0) & (place + step <= 3))
        def _():
            pl.semaphore_signal(
                barrier, inc=1, device_id={"ctx": place + step}, device_id_type=MESH
            )

    def piece(ref, j):
        return ref.at[part, block(j)]

    own_block = og_all.at[:, block(me)]
    og_pair = send(own_block, own_block, og_s.at[0], og_r.at[0], heads=partner)
    og_cross = [
        send(piece(og_all, ours[i]), piece(og_all, ours[i]), og_s.at[1 + i], og_r.at[1 + i],
             heads=cross)
        for i in range(2)
    ]
    og_relay = [
        send(piece(og_all, theirs[i]), piece(og_all, theirs[i]), og_s.at[3 + i], og_r.at[3 + i],
             heads=partner)
        for i in range(2)
    ]
    end_ship = [
        send(piece(og_all, ours[i]), piece(og_end, ours[i]), end_s.at[i], end_r.at[i], ctx=near)
        for i in range(2)
    ]
    end_pair = [
        send(piece(og_end, ours[i]), piece(og_end, ours[i]), end_s.at[2 + i], end_r.at[2 + i],
             heads=partner)
        for i in range(2)
    ]
    end_cross = [
        send(piece(og_end, ours[i]), piece(og_end, ours[i]), end_s.at[4 + i], end_r.at[4 + i],
             heads=cross)
        for i in range(2)
    ]
    end_relay = [
        send(piece(og_end, theirs[i]), piece(og_end, theirs[i]), end_s.at[6 + i], end_r.at[6 + i],
             heads=partner)
        for i in range(2)
    ]

    def strip(h):
        return pl.ds(pl.multiple_of(h * width, width), width)

    def mix_copy(h):
        return send(
            mixed_t.at[strip(h)], mixed_end.at[strip(h)], mix_s.at[h], mix_r.at[h], ctx=near
        )

    def sum_copy(i, h):
        return send(
            sum_send.at[i, strip(h)], sum_recv.at[i, strip(h)], sum_s.at[i, h], sum_r.at[i, h],
            ctx=3 - near,
        )

    def fin_copy(h):
        return send(
            fin_send.at[strip(h)], sum_recv.at[0, strip(h)], fin_s.at[h], fin_r.at[h], ctx=edge
        )

    loads[0].wait()
    loads[1].wait()

    def update(h, carry):
        key_feat = feature(k_ref[:, lanes(h)].astype(F32)).astype(BF16)
        upd[h, :width] = mm(key_feat.T, v_ref[:, lanes(h)])
        total = jnp.sum(key_feat.astype(F32), axis=0, keepdims=True)
        upd[h, width:] = jnp.broadcast_to(total, (PAD, width))
        return carry

    lax.fori_loop(0, heads_here, update, 0)

    def up_copy(h, target):
        return send(up_send.at[h], up_recv.at[h], up_s.at[h], up_r.at[h], ctx=target)

    def up_step(index):
        @pl.when(place == index)
        def _():
            for h in range(heads_here):
                if index == 0:
                    state[h, :width] = mem_ref[h]
                    state[h, width:] = jnp.broadcast_to(norm_ref[h : h + 1, :], (PAD, width))
                else:
                    up_copy(h, index - 1).wait_recv()
                    state[h] = up_recv[h].astype(F32)
                if index < 3:
                    up_send[h] = (decay_ref[0, h] * state[h] + upd[h]).astype(BF16)
                    up_copy(h, index + 1).start()

    def down_copy(h, target):
        return send(down_send.at[h], down_recv.at[h], down_s.at[h], down_r.at[h], ctx=target)

    def down_step(index):
        @pl.when(place == index)
        def _():
            if index == 3:
                after[...] = jnp.zeros_like(after)
            for h in range(heads_here):
                if index < 3:
                    down_copy(h, index + 1).wait_recv()
                    after[h] = down_recv[h].astype(F32)
                if index > 0:
                    down_send[h] = (decay_ref[0, h] * after[h] + local[h]).astype(BF16)
                    down_copy(h, index - 1).start()

    keep = lax.broadcasted_iota(jnp.int32, (HALF, HALF), 0) <= lax.broadcasted_iota(
        jnp.int32, (HALF, HALF), 1
    )
    factor = scale * math.log2(math.e)
    parts = rows // HALF

    def span(j):
        return slice(j * HALF, (j + 1) * HALF)

    def forward(h, carry):
        values_t = v_ref[:, lanes(h)].T
        for b in range(parts):
            query = q_ref[span(b), lanes(h)]
            scores = [nt(k_ref[span(j), lanes(h)], query) for j in range(b + 1)]
            scores[b] = jnp.where(keep, scores[b], -1e30)
            peak = jnp.max(scores[0], axis=0, keepdims=True)
            for piece in scores[1:]:
                peak = jnp.maximum(peak, jnp.max(piece, axis=0, keepdims=True))
            expo = [jnp.exp2((piece - peak) * factor) for piece in scores]
            total = sum(jnp.sum(piece, axis=0, keepdims=True) for piece in expo)
            inverse = 1.0 / total
            acc = None
            for j in range(b + 1):
                prob = (expo[j] * inverse).astype(BF16)
                probs[h, span(j), span(b)] = prob
                term = mm(values_t[:, span(j)], prob)
                acc = term if acc is None else acc + term
            out_t[h, :, span(b)] = acc
        return carry

    loads[2].wait()
    lax.fori_loop(0, 1, forward, 0)
    for i in (3, 4, 7, 8):
        loads[i].wait()
    pl.semaphore_wait(barrier, 3 + is_mid.astype(jnp.int32))
    up_step(0)
    loads[6].wait()
    og_pair.start()

    def launch():
        og_cross[0].start()

        @pl.when(is_end)
        def _():
            end_ship[0].start()

    @pl.when(holds_outer)
    def _():
        launch()

    lax.fori_loop(1, 2, forward, 0)
    og_pair.wait_recv()

    @pl.when(holds_inner)
    def _():
        launch()

    @pl.when(is_end)
    def _():
        og_cross[1].start()

    up_step(1)
    lax.fori_loop(2, heads_here, forward, 0)
    up_step(2)
    og_cross[0].wait_recv()
    og_relay[0].start()

    @pl.when(is_end)
    def _():
        end_ship[0].wait_send()
        end_ship[1].start()

    @pl.when(is_mid)
    def _():
        end_ship[0].wait_recv()
        end_pair[0].start()
        end_cross[0].start()

    up_step(3)

    def recall_step(h, carry):
        mem = state[h, :width].astype(BF16)
        norm = state[h, width : width + 1]
        query_feat = feature(q_ref[:, lanes(h)].astype(F32))
        inverse = 1.0 / jnp.sum(query_feat * norm, axis=1, keepdims=True)
        recalled = mm(query_feat.astype(BF16), mem) * inverse
        recall[:, lanes(h)] = recalled
        mix = mix_of(h)
        both = (mix * recalled + (1.0 - mix) * out_t[h].T).astype(BF16)
        mixed[:, lanes(h)] = both
        mixed_t[pl.ds(pl.multiple_of(h * width, width), width), :] = both.T
        return carry

    lax.fori_loop(0, heads_here, recall_step, 0)
    loads[5].wait()
    o_far = send(o_send.at[0], o_recv.at[0], o_s.at[0], o_r.at[0], heads=partner)
    o_pair = send(o_send.at[1], o_recv.at[1], o_s.at[1], o_r.at[1], heads=partner)
    o_cross = send(o_send.at[2], o_recv.at[2], o_s.at[2], o_r.at[2], heads=cross)
    o_send[0] = mm(mixed[...], w_ref[:, block(far)]).astype(BF16)
    o_far.start()
    o_send[1] = mm(mixed[...], w_ref[:, block(partner)]).astype(BF16)
    o_pair.start()
    value = mm(mixed[...], w_ref[:, block(cross)])
    o_far.wait_recv()
    o_send[2] = (value + o_recv[0].astype(F32)).astype(BF16)
    own_out[...] = mm(mixed[...], w_ref[:, block(me)])

    def both_terms(h, j):
        return mm(mixed_t[strip(h), :], og_all[:, block(j)]) + mm(
            mixed_end[strip(h), :], og_end[:, block(j)]
        )

    def sum_step(i, j):
        def step(h):
            if i == 0:
                mix_copy(h).wait_recv()
            sum_send[i, strip(h)] = both_terms(h, j).astype(BF16)
            sum_copy(i, h).start()

        return step

    @pl.when(is_mid)
    def _():
        end_cross[0].wait_send()
        og_cross[1].start()
        end_ship[1].wait_recv()
        end_pair[1].start()
        end_cross[0].wait_recv()
        end_relay[0].start()
        og_relay[0].wait_recv()
        end_pair[0].wait_recv()
        end_relay[0].wait_recv()
        for h in range(2):
            sum_step(0, 3 - edge)(h)

    @pl.when(is_end)
    def _():
        end_ship[1].wait_send()
        for h in range(heads_here):
            mix_copy(h).start()

    og_cross[1].wait_recv()
    og_relay[1].start()

    @pl.when(is_mid)
    def _():
        og_cross[1].wait_send()
        end_cross[1].start()

    @pl.when(is_end)
    def _():
        o_cross.start()
        og_relay[0].wait_recv()

    og_relay[1].wait_recv()

    def grad_block(j, carry):
        here = pl.ds(pl.multiple_of(j * HALF, HALF), HALF)
        grad_mix[:, here] = nt(og_all[...], w_ref[here, :])
        return carry

    lax.fori_loop(0, cols // HALF, grad_block, 0)

    def memory_step(h, carry):
        mem = state[h, :width].astype(BF16)
        norm = state[h, width : width + 1]
        query = q_ref[:, lanes(h)].astype(F32)
        query_feat = feature(query)
        inverse = 1.0 / jnp.sum(query_feat * norm, axis=1, keepdims=True)
        grad_recall = mix_of(h) * grad_mix[:, lanes(h)]
        grad_numer = (grad_recall * inverse).astype(BF16)
        grad_denom = -jnp.sum(grad_recall * recall[:, lanes(h)], axis=1, keepdims=True) * inverse
        grad_feat[:, lanes(h)] = (nt(grad_numer, mem) + grad_denom * norm) * feature_slope(query)
        local[h, :width] = mm(query_feat.astype(BF16).T, grad_numer)
        total = jnp.sum(query_feat * grad_denom, axis=0, keepdims=True)
        local[h, width:] = jnp.broadcast_to(total, (PAD, width))
        return carry

    lax.fori_loop(0, heads_here, memory_step, 0)
    down_step(3)

    down_step(2)

    @pl.when(is_mid)
    def _():
        for h in range(2, heads_here):
            sum_step(0, 3 - edge)(h)
        end_cross[1].wait_send()
        o_cross.start()
        end_cross[1].wait_recv()
        end_relay[1].start()
        end_pair[1].wait_recv()
        end_relay[1].wait_recv()
        for h in range(heads_here):
            sum_step(1, 3 - near)(h)

    down_step(1)
    gw_ref[...] = mm(mixed_t[...], og_all[:, block(place)])

    @pl.when(is_mid)
    def _():
        gw_ref[...] += mm(mixed_end[...], og_end[:, block(place)])

    def backward(h, carry):
        mix = mix_of(h)
        grad_local = ((1.0 - mix) * grad_mix[:, lanes(h)]).astype(BF16)
        grad_t = grad_local.T
        delta = jnp.sum(grad_t.astype(F32) * out_t[h], axis=0, keepdims=True)
        keys_t = k_ref[:, lanes(h)].T
        for b in range(parts):
            query = q_ref[span(b), lanes(h)]
            acc = None
            for j in range(b + 1):
                prob = probs[h, span(j), span(b)]
                grad_prob = mm(v_ref[span(j), lanes(h)], grad_t[:, span(b)])
                grad_score = (prob.astype(F32) * (grad_prob - delta[:, span(b)]) * scale).astype(
                    BF16
                )
                term = mm(keys_t[:, span(j)], grad_score)
                acc = term if acc is None else acc + term
                key_term = mm(grad_score, query)
                value_term = mm(prob, grad_local[span(b), :])
                if b == j:
                    gk_att[span(j), lanes(h)] = key_term
                    gv_att[span(j), lanes(h)] = value_term
                else:
                    gk_att[span(j), lanes(h)] += key_term
                    gv_att[span(j), lanes(h)] += value_term
            gq_ref[span(b), lanes(h)] = (acc.T + grad_feat[span(b), lanes(h)]).astype(BF16)
        return carry

    def backward_step(h, carry):
        backward(h, carry)

        @pl.when(is_mid)
        def _():
            sum_copy(0, h).wait_recv()
            fin_send[strip(h)] = (
                mm(mixed_t[strip(h), :], og_all[:, block(edge)])
                + sum_recv[0, strip(h)].astype(F32)
            ).astype(BF16)
            fin_copy(h).start()

        return carry

    lax.fori_loop(0, heads_here, backward_step, 0)
    o_pair.wait_recv()
    o_cross.wait_recv()
    out_ref[...] = (own_out[...] + o_recv[1].astype(F32) + o_recv[2].astype(F32)).astype(BF16)
    down_step(0)

    def finish(h, carry):
        mem = after[h, :width].astype(BF16)
        key = k_ref[:, lanes(h)].astype(F32)
        value = v_ref[:, lanes(h)]
        grad_kfeat = nt(value, mem) + after[h, width : width + 1]
        gk_ref[:, lanes(h)] = (gk_att[:, lanes(h)] + grad_kfeat * feature_slope(key)).astype(BF16)
        key_feat = feature(key).astype(BF16)
        gv_ref[:, lanes(h)] = (gv_att[:, lanes(h)] + mm(key_feat, mem)).astype(BF16)
        return carry

    lax.fori_loop(0, heads_here, finish, 0)

    def last_step(h, carry):
        @pl.when(is_mid)
        def _():
            sum_copy(1, h).wait_recv()
            gw_ref[strip(h)] += sum_recv[1, strip(h)].astype(F32)

        @pl.when(is_end)
        def _():
            fin_copy(h).wait_recv()
            gw_ref[strip(h)] += sum_recv[0, strip(h)].astype(F32)

        return carry

    lax.fori_loop(0, heads_here, last_step, 0)
    for copy in (og_pair, og_cross[0], *og_relay, o_far, o_pair, o_cross):
        copy.wait_send()

    @pl.when(is_end)
    def _():
        og_cross[1].wait_send()
        for h in range(heads_here):
            mix_copy(h).wait_send()

    @pl.when(is_mid)
    def _():
        for copy in (*end_pair, *end_relay):
            copy.wait_send()
        for h in range(heads_here):
            sum_copy(0, h).wait_send()
            sum_copy(1, h).wait_send()
            fin_copy(h).wait_send()

    @pl.when(place < 3)
    def _():
        for h in range(heads_here):
            up_copy(h, near).wait_send()

    @pl.when(place > 0)
    def _():
        for h in range(heads_here):
            down_copy(h, near).wait_send()


def settle(*refs):
    sems = refs[-1]
    count = len(refs) // 2
    copies = [
        pltpu.make_async_copy(refs[i], refs[count + i], sems.at[i]) for i in range(count)
    ]
    for copy in copies:
        copy.start()
    for copy in copies:
        copy.wait()


def shards(queries, key_rows, values, memory_in, norm_in, decays, gate_bias, out_weight, out_grad):
    rows, cols = queries.shape
    heads_here, width = memory_in.shape[0], memory_in.shape[1]
    if (
        lax.axis_size("ctx") != 4
        or lax.axis_size("heads") != 4
        or rows != 2 * HALF
        or cols != rows
        or heads_here != 4
        or width != 128
    ):
        return plain(
            queries, key_rows, values, memory_in, norm_in, decays, gate_bias, out_weight, out_grad
        )
    wide = out_weight.shape[1]
    free = pl.BlockSpec(memory_space=pl.ANY)
    small = (heads_here, width + PAD, width)
    half = jax.ShapeDtypeStruct((rows, cols), BF16)
    dma = pltpu.SemaphoreType.DMA
    shapes = (half, half, half, half, jax.ShapeDtypeStruct((cols, cols), F32))
    held = tuple(pltpu.VMEM(x.shape, x.dtype) for x in shapes)
    results = pl.pallas_call(
        fused,
        out_shape=held,
        in_specs=[free] * 9,
        out_specs=(pl.BlockSpec(memory_space=pltpu.VMEM),) * 5,
        scratch_shapes=[
            pltpu.VMEM((rows, cols), BF16),
            pltpu.VMEM((rows, cols), BF16),
            pltpu.VMEM((rows, cols), BF16),
            pltpu.VMEM((heads_here, width, width), F32),
            pltpu.VMEM((heads_here, width), F32),
            pltpu.VMEM((cols, wide), BF16),
            pltpu.SMEM((1, heads_here), F32),
            pltpu.SMEM((1, heads_here), F32),
            pltpu.VMEM((rows, wide), BF16),
            pltpu.VMEM((rows, wide), BF16),
            pltpu.VMEM(small, F32),
            pltpu.VMEM(small, F32),
            pltpu.VMEM(small, F32),
            pltpu.VMEM(small, F32),
            pltpu.VMEM(small, BF16),
            pltpu.VMEM(small, BF16),
            pltpu.VMEM(small, BF16),
            pltpu.VMEM(small, BF16),
            pltpu.VMEM((heads_here, rows, rows), BF16),
            pltpu.VMEM((heads_here, width, rows), F32),
            pltpu.VMEM((rows, cols), F32),
            pltpu.VMEM((rows, cols), F32),
            pltpu.VMEM((rows, cols), F32),
            pltpu.VMEM((rows, cols), BF16),
            pltpu.VMEM((cols, rows), BF16),
            pltpu.VMEM((cols, rows), BF16),
            pltpu.VMEM((rows, cols), F32),
            pltpu.VMEM((rows, cols), F32),
            pltpu.VMEM((rows, cols), F32),
            pltpu.VMEM((2, cols, cols), BF16),
            pltpu.VMEM((2, cols, cols), BF16),
            pltpu.VMEM((cols, cols), BF16),
            pltpu.VMEM((3, rows, cols), BF16),
            pltpu.VMEM((3, rows, cols), BF16),
            dma((5,)), dma((5,)), dma((8,)), dma((8,)), dma((4,)), dma((4,)),
            dma((4,)), dma((4,)), dma((4,)), dma((4,)),
            dma((2, 4)), dma((2, 4)), dma((4,)), dma((4,)),
            dma((3,)), dma((3,)), dma((9,)),
        ],
        compiler_params=pltpu.CompilerParams(
            collective_id=0, has_side_effects=True, vmem_limit_bytes=48 << 20
        ),
    )(
        *(
            pltpu.with_memory_space_constraint(x, pltpu.HBM)
            for x in (
                queries, key_rows, values, memory_in, norm_in, decays,
                gate_bias.reshape(1, heads_here), out_weight, out_grad,
            )
        )
    )
    results = [pltpu.with_memory_space_constraint(x, pltpu.VMEM) for x in results]
    return pl.pallas_call(
        settle,
        out_shape=shapes,
        in_specs=[pl.BlockSpec(memory_space=pltpu.VMEM)] * 5,
        out_specs=(free,) * 5,
        scratch_shapes=[dma((5,))],
    )(*results)


def solution(mesh):
    return jax.shard_map(
        shards,
        mesh=mesh,
        in_specs=(
            P(("groups", "ctx"), "heads"),
            P(("groups", "ctx"), "heads"),
            P(("groups", "ctx"), "heads"),
            P(("groups", "heads"), None, None),
            P(("groups", "heads"), None),
            P(("groups", "ctx"), "heads"),
            P("heads"),
            P("heads", None),
            P(("groups", "ctx"), "heads"),
        ),
        out_specs=(
            P(("groups", "ctx"), "heads"),
            P(("groups", "ctx"), "heads"),
            P(("groups", "ctx"), "heads"),
            P(("groups", "ctx"), "heads"),
            P(("groups", "heads"), "ctx"),
        ),
        check_vma=False,
    )
```

```python
import math

import jax
import jax.numpy as jnp
from jax import lax
from jax.experimental import pallas as pl
from jax.experimental.pallas import tpu as pltpu
from jax.sharding import PartitionSpec as P

HIGH = lax.Precision.HIGHEST


def shortened(value):

    def short(part):
        return part.astype(jnp.bfloat16) if part.dtype == jnp.float32 else part

    return jax.tree.map(short, value)


def feature(inner):
    return jnp.where(inner > 0, inner + 1.0, jnp.exp(jnp.minimum(inner, 0.0)))


def feature_slope(inner):
    return jnp.where(inner > 0, 1.0, jnp.exp(jnp.minimum(inner, 0.0)))


def gathered_prefix(stacked_gate, stacked_mem, stacked_norm, own_index, count, upward):
    order = jnp.arange(count, dtype=jnp.int32)
    term_pos = order[:, None]
    inner_pos = order[None, :]
    if upward:
        between = (inner_pos > term_pos) & (inner_pos < own_index)
        active = order < own_index
    else:
        between = (inner_pos < term_pos) & (inner_pos > own_index)
        active = order > own_index
    factor = jnp.prod(jnp.where(between[:, :, None], stacked_gate[None, :, :], 1.0), axis=1)
    weight = jnp.where(active[:, None], factor, 0.0)
    total_mem = jnp.einsum("th,thij->hij", weight, stacked_mem, precision=HIGH)
    total_norm = jnp.einsum("th,thi->hi", weight, stacked_norm, precision=HIGH)
    leading = jnp.prod(jnp.where(active[:, None], stacked_gate, 1.0), axis=0)
    return (leading, total_mem, total_norm)


def plain(queries, key_rows, values, memory_in, norm_in, decays, gate_bias, out_weight, out_grad):
    rows = queries.shape[0]
    heads_here = memory_in.shape[0]
    width = memory_in.shape[1]
    scale = 1.0 / math.sqrt(width)
    shape_three = (rows, heads_here, width)
    query_blk = queries.reshape(shape_three)
    key_blk = key_rows.reshape(shape_three)
    value_blk = values.reshape(shape_three)
    gate_now = decays[0]
    key_f = key_blk.astype(jnp.float32)
    key_feat = feature(key_f).astype(jnp.bfloat16)
    upd_mem = jnp.einsum("thi,thj->hij", key_feat, value_blk, preferred_element_type=jnp.float32)
    upd_norm = jnp.sum(key_feat.astype(jnp.float32), axis=0)
    all_gate, all_mem, all_norm = (
        lax.all_gather(gate_now[None].astype(jnp.bfloat16), "ctx", axis=0, tiled=True).astype(
            jnp.float32
        ),
        lax.all_gather(upd_mem[None].astype(jnp.bfloat16), "ctx", axis=0, tiled=True).astype(
            jnp.float32
        ),
        lax.all_gather(upd_norm[None].astype(jnp.bfloat16), "ctx", axis=0, tiled=True).astype(
            jnp.float32
        ),
    )
    leading, prior_mem, prior_norm = gathered_prefix(
        all_gate, all_mem, all_norm, lax.axis_index("ctx"), lax.axis_size("ctx"), True
    )
    state_mem = leading[:, None, None] * memory_in + prior_mem
    state_norm = leading[:, None] * norm_in + prior_norm
    query_f = query_blk.astype(jnp.float32)
    query_feat = feature(query_f)
    numer = jnp.einsum("thi,hij->thj", query_feat, state_mem, precision=HIGH)
    denom = jnp.einsum("thi,hi->th", query_feat, state_norm, precision=HIGH)
    recall = numer / denom[..., None]
    scores = (
        jnp.einsum("thd,shd->hts", query_blk, key_blk, preferred_element_type=jnp.float32) * scale
    )
    places = jnp.arange(rows, dtype=jnp.int32)
    causal = (places[:, None] >= places[None, :])[None]
    peak = jnp.max(jnp.where(causal, scores, -jnp.inf), axis=-1, keepdims=True)
    expo = jnp.where(causal, jnp.exp(scores - peak), 0.0)
    probs = expo / jnp.sum(expo, axis=-1, keepdims=True)
    probs_half = probs.astype(jnp.bfloat16)
    local_out = jnp.einsum(
        "hts,shd->thd", probs_half, value_blk, preferred_element_type=jnp.float32
    )
    mix = jax.nn.sigmoid(gate_bias)[None, :, None]
    mixed = (
        (mix * recall + (1.0 - mix) * local_out)
        .astype(jnp.bfloat16)
        .reshape(rows, heads_here * width)
    )
    partial_sum = jnp.dot(mixed, out_weight, preferred_element_type=jnp.float32)
    output = lax.psum_scatter(
        partial_sum.astype(jnp.bfloat16), "heads", scatter_dimension=1, tiled=True
    )
    piece = lax.all_gather(out_grad, "heads", axis=1, tiled=True)
    grad_mix = lax.dot_general(
        piece, out_weight, (((1,), (1,)), ((), ())), preferred_element_type=jnp.float32
    )
    block = lax.dot_general(
        mixed, piece, (((0,), (0,)), ((), ())), preferred_element_type=jnp.float32
    )
    grad_mix, collected = (grad_mix, block)
    grad_weight = lax.psum_scatter(
        collected.astype(jnp.bfloat16), "ctx", scatter_dimension=1, tiled=True
    ).astype(jnp.float32)
    grad_seg = grad_mix.reshape(shape_three)
    grad_recall = mix * grad_seg
    grad_local = ((1.0 - mix) * grad_seg).astype(jnp.bfloat16)
    grad_probs = jnp.einsum(
        "thd,shd->hts", grad_local, value_blk, preferred_element_type=jnp.float32
    )
    grad_value_att = jnp.einsum(
        "hts,thd->shd", probs_half, grad_local, preferred_element_type=jnp.float32
    )
    delta = jnp.sum(probs * grad_probs, axis=-1, keepdims=True)
    grad_scores = (probs * (grad_probs - delta) * scale).astype(jnp.bfloat16)
    grad_query_att = jnp.einsum(
        "hts,shd->thd", grad_scores, key_blk, preferred_element_type=jnp.float32
    )
    grad_key_att = jnp.einsum(
        "hts,thd->shd", grad_scores, query_blk, preferred_element_type=jnp.float32
    )
    grad_numer = grad_recall / denom[..., None]
    grad_denom = -jnp.sum(grad_recall * recall, axis=-1) / denom
    grad_qfeat = (
        jnp.einsum("thj,hij->thi", grad_numer, state_mem, precision=HIGH)
        + grad_denom[..., None] * state_norm[None]
    )
    local_mem = jnp.einsum("thi,thj->hij", query_feat, grad_numer, precision=HIGH)
    local_norm = jnp.einsum("thi,th->hi", query_feat, grad_denom, precision=HIGH)
    grad_query = (
        (grad_query_att + grad_qfeat * feature_slope(query_f))
        .astype(jnp.bfloat16)
        .reshape(rows, heads_here * width)
    )
    back_gate, back_mem, back_norm = (
        lax.all_gather(gate_now[None].astype(jnp.bfloat16), "ctx", axis=0, tiled=True).astype(
            jnp.float32
        ),
        lax.all_gather(shortened(local_mem[None]), "ctx", axis=0, tiled=True),
        lax.all_gather(shortened(local_norm[None]), "ctx", axis=0, tiled=True),
    )
    unused_lead, after_mem, after_norm = gathered_prefix(
        back_gate, back_mem, back_norm, lax.axis_index("ctx"), lax.axis_size("ctx"), False
    )
    value_f = value_blk.astype(jnp.float32)
    grad_kfeat = jnp.einsum("thj,hij->thi", value_f, after_mem, precision=HIGH) + after_norm[None]
    grad_key = (
        (grad_key_att + grad_kfeat * feature_slope(key_f))
        .astype(jnp.bfloat16)
        .reshape(rows, heads_here * width)
    )
    grad_value = (
        (
            grad_value_att
            + jnp.einsum("thi,hij->thj", key_feat.astype(jnp.float32), after_mem, precision=HIGH)
        )
        .astype(jnp.bfloat16)
        .reshape(rows, heads_here * width)
    )
    return (output, grad_query, grad_key, grad_value, grad_weight)


MESH = pl.DeviceIdType.MESH
F32 = jnp.float32
BF16 = jnp.bfloat16
HALF = 256
PAD = 16


def mm(left, right):
    return jnp.dot(left, right, preferred_element_type=F32)


def nt(left, right):
    return lax.dot_general(left, right, (((1,), (1,)), ((), ())), preferred_element_type=F32)


def fused(
    q_in, k_in, v_in, mem_in, norm_in, decay_in, gate_in, w_in, og_ref,
    out_ref, gq_ref, gk_ref, gv_ref, gw_ref,
    q_ref, k_ref, v_ref, mem_ref, norm_ref, w_ref, decay_ref, gate_ref,
    og_all, og_end, upd, state, local, after, up_send, up_recv, down_send, down_recv,
    probs, out_t, recall, own_out, grad_mix, mixed, mixed_t, mixed_end, grad_feat, gk_att, gv_att,
    sum_send, sum_recv, fin_send, o_send, o_recv,
    og_s, og_r, end_s, end_r, mix_s, mix_r, up_s, up_r, down_s, down_r, sum_s, sum_r, fin_s, fin_r,
    o_s, o_r, load_s,
):
    rows, cols = q_ref.shape
    heads_here, width = mem_ref.shape[0], mem_ref.shape[1]
    scale = 1.0 / math.sqrt(width)
    me = lax.axis_index("heads")
    place = lax.axis_index("ctx")
    partner = me + 1 - 2 * lax.rem(me, 2)
    cross = lax.rem(me + 2, 4)
    far = lax.rem(partner + 2, 4)
    is_end = (place == 0) | (place == 3)
    is_mid = (place == 1) | (place == 2)
    near = 1 + lax.div(place, 2)
    edge = 3 * lax.div(place, 2)
    side = lax.div(me, 2)
    holds_outer = (me == 0) | (me == 3)
    holds_inner = (me == 1) | (me == 2)
    beside = 3 * side == edge
    across = 3 * side != edge
    ours = (3 * side, 1 + side)
    theirs = (3 - 3 * side, 2 - side)
    part = pl.ds(pl.multiple_of(lax.rem(me, 2) * HALF, HALF), HALF)

    def lanes(h):
        return pl.ds(pl.multiple_of(h * width, width), width)

    def block(j):
        return pl.ds(pl.multiple_of(j * cols, cols), cols)

    def send(src, dst, s, r, **where):
        return pltpu.make_async_remote_copy(
            src_ref=src, dst_ref=dst, send_sem=s, recv_sem=r, device_id=where, device_id_type=MESH
        )

    def mix_of(h):
        return 1.0 / (1.0 + jnp.exp(-jnp.full((1, width), gate_ref[0, h], F32)))

    loads = [
        pltpu.make_async_copy(src, dst, load_s.at[i])
        for i, (src, dst) in enumerate(
            (
                (k_in, k_ref), (v_in, v_ref), (q_in, q_ref), (mem_in, mem_ref),
                (norm_in, norm_ref), (w_in, w_ref), (og_ref, og_all.at[:, block(me)]),
                (decay_in, decay_ref), (gate_in, gate_ref),
            )
        )
    ]
    for i in (6, 0, 1, 2, 3, 4, 7, 8, 5):
        loads[i].start()

    barrier = pltpu.get_barrier_semaphore()
    for peer in (partner, cross):
        pl.semaphore_signal(barrier, inc=1, device_id={"heads": peer}, device_id_type=MESH)
    for step in (-1, 1):

        @pl.when((place + step >= 0) & (place + step <= 3))
        def _():
            pl.semaphore_signal(
                barrier, inc=1, device_id={"ctx": place + step}, device_id_type=MESH
            )

    def piece(ref, j):
        return ref.at[part, block(j)]

    own_block = og_all.at[:, block(me)]
    og_pair = send(own_block, own_block, og_s.at[0], og_r.at[0], heads=partner)
    og_inner = send(
        piece(og_all, ours[1]), piece(og_all, ours[1]), og_s.at[1], og_r.at[1], heads=cross
    )

    def fine(ref, j, i):
        start = lax.rem(me, 2) * HALF + i * (HALF // 2)
        return ref.at[pl.ds(pl.multiple_of(start, HALF // 2), HALF // 2), block(j)]

    og_outer = [
        send(fine(og_all, ours[0], i), fine(og_all, ours[0], i), og_s.at[5 + i], og_r.at[5 + i],
             heads=cross)
        for i in range(2)
    ]
    og_relay = [
        send(piece(og_all, theirs[i]), piece(og_all, theirs[i]), og_s.at[3 + i], og_r.at[3 + i],
             heads=partner)
        for i in range(2)
    ]
    lead = piece(og_end, 3 - edge)
    inner = piece(og_end, ours[1])
    inner_far = piece(og_end, theirs[1])
    ship_lead = [
        send(fine(og_all, 3 - edge, i), fine(og_end, 3 - edge, i), end_s.at[6 * i], end_r.at[6 * i],
             ctx=near)
        for i in range(2)
    ]
    ship_inner = send(piece(og_all, ours[1]), inner, end_s.at[1], end_r.at[1], ctx=near)
    lead_pair = send(lead, lead, end_s.at[2], end_r.at[2], heads=partner)
    inner_pair = send(inner, inner, end_s.at[3], end_r.at[3], heads=partner)
    inner_cross = send(inner, inner, end_s.at[4], end_r.at[4], heads=cross)
    inner_relay = send(inner_far, inner_far, end_s.at[5], end_r.at[5], heads=partner)

    def strip(h):
        return pl.ds(pl.multiple_of(h * width, width), width)

    def mix_copy(h):
        return send(
            mixed_t.at[strip(h)], mixed_end.at[strip(h)], mix_s.at[h], mix_r.at[h], ctx=near
        )

    def sum_copy(i, h):
        return send(
            sum_send.at[i, strip(h)], sum_recv.at[i, strip(h)], sum_s.at[i, h], sum_r.at[i, h],
            ctx=3 - near,
        )

    def fin_copy(h):
        return send(
            fin_send.at[strip(h)], sum_recv.at[0, strip(h)], fin_s.at[h], fin_r.at[h], ctx=edge
        )

    loads[0].wait()
    loads[1].wait()

    def update(h, carry):
        key_feat = feature(k_ref[:, lanes(h)].astype(F32)).astype(BF16)
        upd[h, :width] = mm(key_feat.T, v_ref[:, lanes(h)])
        total = jnp.sum(key_feat.astype(F32), axis=0, keepdims=True)
        upd[h, width:] = jnp.broadcast_to(total, (PAD, width))
        return carry

    lax.fori_loop(0, heads_here, update, 0)

    def up_copy(h, target):
        return send(up_send.at[h], up_recv.at[h], up_s.at[h], up_r.at[h], ctx=target)

    def up_step(index):
        @pl.when(place == index)
        def _():
            for h in range(heads_here):
                if index == 0:
                    state[h, :width] = mem_ref[h]
                    state[h, width:] = jnp.broadcast_to(norm_ref[h : h + 1, :], (PAD, width))
                else:
                    up_copy(h, index - 1).wait_recv()
                    state[h] = up_recv[h].astype(F32)
                if index < 3:
                    up_send[h] = (decay_ref[0, h] * state[h] + upd[h]).astype(BF16)
                    up_copy(h, index + 1).start()

    def down_copy(h, target):
        return send(down_send.at[h], down_recv.at[h], down_s.at[h], down_r.at[h], ctx=target)

    def down_step(index):
        @pl.when(place == index)
        def _():
            if index == 3:
                after[...] = jnp.zeros_like(after)
            for h in range(heads_here):
                if index < 3:
                    down_copy(h, index + 1).wait_recv()
                    after[h] = down_recv[h].astype(F32)
                if index > 0:
                    down_send[h] = (decay_ref[0, h] * after[h] + local[h]).astype(BF16)
                    down_copy(h, index - 1).start()

    keep = lax.broadcasted_iota(jnp.int32, (HALF, HALF), 0) <= lax.broadcasted_iota(
        jnp.int32, (HALF, HALF), 1
    )
    factor = scale * math.log2(math.e)
    parts = rows // HALF

    def span(j):
        return slice(j * HALF, (j + 1) * HALF)

    def forward(h, carry):
        values_t = v_ref[:, lanes(h)].T
        for b in range(parts):
            query = q_ref[span(b), lanes(h)]
            scores = [nt(k_ref[span(j), lanes(h)], query) for j in range(b + 1)]
            scores[b] = jnp.where(keep, scores[b], -1e30)
            peak = jnp.max(scores[0], axis=0, keepdims=True)
            for piece in scores[1:]:
                peak = jnp.maximum(peak, jnp.max(piece, axis=0, keepdims=True))
            expo = [jnp.exp2((piece - peak) * factor) for piece in scores]
            total = sum(jnp.sum(piece, axis=0, keepdims=True) for piece in expo)
            inverse = 1.0 / total
            acc = None
            for j in range(b + 1):
                prob = (expo[j] * inverse).astype(BF16)
                probs[h, span(j), span(b)] = prob
                term = mm(values_t[:, span(j)], prob)
                acc = term if acc is None else acc + term
            out_t[h, :, span(b)] = acc
        return carry

    for i in (3, 4, 7, 8):
        loads[i].wait()
    pl.semaphore_wait(barrier, 3 + is_mid.astype(jnp.int32))
    up_step(0)
    loads[6].wait()
    og_pair.start()

    def launch():
        for copy in og_outer:
            copy.start()

        @pl.when(is_end & across)
        def _():
            for copy in ship_lead:
                copy.start()

    @pl.when(holds_outer)
    def _():
        launch()

    loads[2].wait()
    lax.fori_loop(0, 1, forward, 0)
    og_pair.wait_recv()

    @pl.when(holds_inner)
    def _():
        launch()

    og_inner.start()

    @pl.when(is_end)
    def _():
        ship_inner.start()

    lax.fori_loop(1, 2, forward, 0)
    up_step(1)
    lax.fori_loop(2, heads_here, forward, 0)
    up_step(2)
    for i in range(2):
        og_outer[i].wait_recv()

        @pl.when(is_end & beside)
        def _():
            ship_lead[i].start()

    og_relay[0].start()

    def pass_lead():
        for copy in ship_lead:
            copy.wait_recv()
        lead_pair.start()

    def pass_inner():
        ship_inner.wait_recv()
        inner_cross.start()
        inner_pair.start()

    @pl.when(is_mid & across)
    def _():
        pass_lead()

    @pl.when(is_mid & beside)
    def _():
        pass_inner()

    up_step(3)

    def recall_step(h, carry):
        mem = state[h, :width].astype(BF16)
        norm = state[h, width : width + 1]
        query_feat = feature(q_ref[:, lanes(h)].astype(F32))
        inverse = 1.0 / jnp.sum(query_feat * norm, axis=1, keepdims=True)
        recalled = mm(query_feat.astype(BF16), mem) * inverse
        recall[:, lanes(h)] = recalled
        mix = mix_of(h)
        both = (mix * recalled + (1.0 - mix) * out_t[h].T).astype(BF16)
        mixed[:, lanes(h)] = both
        mixed_t[strip(h), :] = both.T

        @pl.when(is_end & (h < 2))
        def _():
            mix_copy(h).start()

        return carry

    lax.fori_loop(0, heads_here, recall_step, 0)
    loads[5].wait()
    o_far = send(o_send.at[0], o_recv.at[0], o_s.at[0], o_r.at[0], heads=partner)
    o_pair = send(o_send.at[1], o_recv.at[1], o_s.at[1], o_r.at[1], heads=partner)
    o_cross = send(o_send.at[2], o_recv.at[2], o_s.at[2], o_r.at[2], heads=cross)
    o_send[0] = mm(mixed[...], w_ref[:, block(far)]).astype(BF16)
    o_far.start()
    o_send[1] = mm(mixed[...], w_ref[:, block(partner)]).astype(BF16)
    o_pair.start()
    value = mm(mixed[...], w_ref[:, block(cross)])
    o_far.wait_recv()
    o_send[2] = (value + o_recv[0].astype(F32)).astype(BF16)
    own_out[...] = mm(mixed[...], w_ref[:, block(me)])

    def both_terms(h, j):
        return mm(mixed_t[strip(h), :], og_all[:, block(j)]) + mm(
            mixed_end[strip(h), :], og_end[:, block(j)]
        )

    def sum_step(i, j):
        def step(h):
            if i == 0:
                mix_copy(h).wait_recv()
            sum_send[i, strip(h)] = both_terms(h, j).astype(BF16)
            sum_copy(i, h).start()

        return step

    @pl.when(is_end)
    def _():
        o_cross.start()

    og_inner.wait_recv()
    og_relay[1].start()

    @pl.when(is_mid & across)
    def _():
        pass_inner()

    @pl.when(is_mid & beside)
    def _():
        pass_lead()

    @pl.when(is_mid)
    def _():
        o_cross.start()

    og_relay[0].wait_recv()
    og_relay[1].wait_recv()

    def grad_block(j, carry):
        here = pl.ds(pl.multiple_of(j * HALF, HALF), HALF)
        grad_mix[:, here] = nt(og_all[...], w_ref[here, :])
        return carry

    lax.fori_loop(0, cols // HALF, grad_block, 0)

    def memory_step(h, carry):
        mem = state[h, :width].astype(BF16)
        norm = state[h, width : width + 1]
        query = q_ref[:, lanes(h)].astype(F32)
        query_feat = feature(query)
        inverse = 1.0 / jnp.sum(query_feat * norm, axis=1, keepdims=True)
        grad_recall = mix_of(h) * grad_mix[:, lanes(h)]
        grad_numer = (grad_recall * inverse).astype(BF16)
        grad_denom = -jnp.sum(grad_recall * recall[:, lanes(h)], axis=1, keepdims=True) * inverse
        grad_feat[:, lanes(h)] = (nt(grad_numer, mem) + grad_denom * norm) * feature_slope(query)
        local[h, :width] = mm(query_feat.astype(BF16).T, grad_numer)
        total = jnp.sum(query_feat * grad_denom, axis=0, keepdims=True)
        local[h, width:] = jnp.broadcast_to(total, (PAD, width))
        return carry

    @pl.when(is_mid)
    def _():
        lead_pair.wait_recv()
        sum_step(0, 3 - edge)(0)

    lax.fori_loop(0, heads_here, memory_step, 0)
    down_step(3)

    @pl.when(is_end)
    def _():
        for h in range(2, heads_here):
            mix_copy(h).start()


    @pl.when(is_mid)
    def _():
        sum_step(0, 3 - edge)(1)

    down_step(2)

    @pl.when(is_mid)
    def _():
        inner_cross.wait_recv()
        inner_relay.start()
        inner_pair.wait_recv()
        inner_relay.wait_recv()
        for h in range(heads_here):
            sum_step(1, 3 - near)(h)
            if h < 2:
                sum_step(0, 3 - edge)(h + 2)

    down_step(1)
    gw_ref[...] = mm(mixed_t[...], og_all[:, block(place)])

    @pl.when(is_mid)
    def _():
        gw_ref[...] += mm(mixed_end[...], og_end[:, block(place)])

    def backward(h, carry):
        mix = mix_of(h)
        grad_local = ((1.0 - mix) * grad_mix[:, lanes(h)]).astype(BF16)
        grad_t = grad_local.T
        delta = jnp.sum(grad_t.astype(F32) * out_t[h], axis=0, keepdims=True)
        keys_t = k_ref[:, lanes(h)].T
        for b in range(parts):
            query = q_ref[span(b), lanes(h)]
            acc = None
            for j in range(b + 1):
                prob = probs[h, span(j), span(b)]
                grad_prob = mm(v_ref[span(j), lanes(h)], grad_t[:, span(b)])
                grad_score = (prob.astype(F32) * (grad_prob - delta[:, span(b)]) * scale).astype(
                    BF16
                )
                term = mm(keys_t[:, span(j)], grad_score)
                acc = term if acc is None else acc + term
                key_term = mm(grad_score, query)
                value_term = mm(prob, grad_local[span(b), :])
                if b == j:
                    gk_att[span(j), lanes(h)] = key_term
                    gv_att[span(j), lanes(h)] = value_term
                else:
                    gk_att[span(j), lanes(h)] += key_term
                    gv_att[span(j), lanes(h)] += value_term
            gq_ref[span(b), lanes(h)] = (acc.T + grad_feat[span(b), lanes(h)]).astype(BF16)
        return carry

    def backward_step(h, carry):
        backward(h, carry)

        @pl.when(is_mid)
        def _():
            sum_copy(0, h).wait_recv()
            fin_send[strip(h)] = (
                mm(mixed_t[strip(h), :], og_all[:, block(edge)])
                + sum_recv[0, strip(h)].astype(F32)
            ).astype(BF16)
            fin_copy(h).start()

        return carry

    lax.fori_loop(0, heads_here, backward_step, 0)
    o_pair.wait_recv()
    o_cross.wait_recv()
    out_ref[...] = (own_out[...] + o_recv[1].astype(F32) + o_recv[2].astype(F32)).astype(BF16)
    down_step(0)

    def finish(h, carry):
        mem = after[h, :width].astype(BF16)
        key = k_ref[:, lanes(h)].astype(F32)
        value = v_ref[:, lanes(h)]
        grad_kfeat = nt(value, mem) + after[h, width : width + 1]
        gk_ref[:, lanes(h)] = (gk_att[:, lanes(h)] + grad_kfeat * feature_slope(key)).astype(BF16)
        key_feat = feature(key).astype(BF16)
        gv_ref[:, lanes(h)] = (gv_att[:, lanes(h)] + mm(key_feat, mem)).astype(BF16)
        return carry

    lax.fori_loop(0, heads_here, finish, 0)

    def last_step(h, carry):
        @pl.when(is_mid)
        def _():
            sum_copy(1, h).wait_recv()
            gw_ref[strip(h)] += sum_recv[1, strip(h)].astype(F32)

        @pl.when(is_end)
        def _():
            fin_copy(h).wait_recv()
            gw_ref[strip(h)] += sum_recv[0, strip(h)].astype(F32)

        return carry

    lax.fori_loop(0, heads_here, last_step, 0)
    for copy in (og_pair, og_inner, *og_outer, *og_relay, o_far, o_pair, o_cross):
        copy.wait_send()

    @pl.when(is_end)
    def _():
        for copy in ship_lead:
            copy.wait_send()
        ship_inner.wait_send()
        for h in range(heads_here):
            mix_copy(h).wait_send()

    @pl.when(is_mid)
    def _():
        for copy in (lead_pair, inner_pair, inner_cross, inner_relay):
            copy.wait_send()
        for h in range(heads_here):
            sum_copy(0, h).wait_send()
            sum_copy(1, h).wait_send()
            fin_copy(h).wait_send()

    @pl.when(place < 3)
    def _():
        for h in range(heads_here):
            up_copy(h, near).wait_send()

    @pl.when(place > 0)
    def _():
        for h in range(heads_here):
            down_copy(h, near).wait_send()


def settle(*refs):
    sems = refs[-1]
    count = len(refs) // 2
    copies = [
        pltpu.make_async_copy(refs[i], refs[count + i], sems.at[i]) for i in range(count)
    ]
    for copy in copies:
        copy.start()
    for copy in copies:
        copy.wait()


def shards(queries, key_rows, values, memory_in, norm_in, decays, gate_bias, out_weight, out_grad):
    rows, cols = queries.shape
    heads_here, width = memory_in.shape[0], memory_in.shape[1]
    if (
        lax.axis_size("ctx") != 4
        or lax.axis_size("heads") != 4
        or rows != 2 * HALF
        or cols != rows
        or heads_here != 4
        or width != 128
    ):
        return plain(
            queries, key_rows, values, memory_in, norm_in, decays, gate_bias, out_weight, out_grad
        )
    wide = out_weight.shape[1]
    free = pl.BlockSpec(memory_space=pl.ANY)
    small = (heads_here, width + PAD, width)
    half = jax.ShapeDtypeStruct((rows, cols), BF16)
    dma = pltpu.SemaphoreType.DMA
    shapes = (half, half, half, half, jax.ShapeDtypeStruct((cols, cols), F32))
    held = tuple(pltpu.VMEM(x.shape, x.dtype) for x in shapes)
    results = pl.pallas_call(
        fused,
        out_shape=held,
        in_specs=[free] * 9,
        out_specs=(pl.BlockSpec(memory_space=pltpu.VMEM),) * 5,
        scratch_shapes=[
            pltpu.VMEM((rows, cols), BF16),
            pltpu.VMEM((rows, cols), BF16),
            pltpu.VMEM((rows, cols), BF16),
            pltpu.VMEM((heads_here, width, width), F32),
            pltpu.VMEM((heads_here, width), F32),
            pltpu.VMEM((cols, wide), BF16),
            pltpu.SMEM((1, heads_here), F32),
            pltpu.SMEM((1, heads_here), F32),
            pltpu.VMEM((rows, wide), BF16),
            pltpu.VMEM((rows, wide), BF16),
            pltpu.VMEM(small, F32),
            pltpu.VMEM(small, F32),
            pltpu.VMEM(small, F32),
            pltpu.VMEM(small, F32),
            pltpu.VMEM(small, BF16),
            pltpu.VMEM(small, BF16),
            pltpu.VMEM(small, BF16),
            pltpu.VMEM(small, BF16),
            pltpu.VMEM((heads_here, rows, rows), BF16),
            pltpu.VMEM((heads_here, width, rows), F32),
            pltpu.VMEM((rows, cols), F32),
            pltpu.VMEM((rows, cols), F32),
            pltpu.VMEM((rows, cols), F32),
            pltpu.VMEM((rows, cols), BF16),
            pltpu.VMEM((cols, rows), BF16),
            pltpu.VMEM((cols, rows), BF16),
            pltpu.VMEM((rows, cols), F32),
            pltpu.VMEM((rows, cols), F32),
            pltpu.VMEM((rows, cols), F32),
            pltpu.VMEM((2, cols, cols), BF16),
            pltpu.VMEM((2, cols, cols), BF16),
            pltpu.VMEM((cols, cols), BF16),
            pltpu.VMEM((3, rows, cols), BF16),
            pltpu.VMEM((3, rows, cols), BF16),
            dma((7,)), dma((7,)), dma((7,)), dma((7,)), dma((4,)), dma((4,)),
            dma((4,)), dma((4,)), dma((4,)), dma((4,)),
            dma((2, 4)), dma((2, 4)), dma((4,)), dma((4,)),
            dma((3,)), dma((3,)), dma((9,)),
        ],
        compiler_params=pltpu.CompilerParams(
            collective_id=0, has_side_effects=True, vmem_limit_bytes=48 << 20
        ),
    )(
        *(
            pltpu.with_memory_space_constraint(x, pltpu.HBM)
            for x in (
                queries, key_rows, values, memory_in, norm_in, decays,
                gate_bias.reshape(1, heads_here), out_weight, out_grad,
            )
        )
    )
    results = [pltpu.with_memory_space_constraint(x, pltpu.VMEM) for x in results]
    return pl.pallas_call(
        settle,
        out_shape=shapes,
        in_specs=[pl.BlockSpec(memory_space=pltpu.VMEM)] * 5,
        out_specs=(free,) * 5,
        scratch_shapes=[dma((5,))],
    )(*results)


def solution(mesh):
    return jax.shard_map(
        shards,
        mesh=mesh,
        in_specs=(
            P(("groups", "ctx"), "heads"),
            P(("groups", "ctx"), "heads"),
            P(("groups", "ctx"), "heads"),
            P(("groups", "heads"), None, None),
            P(("groups", "heads"), None),
            P(("groups", "ctx"), "heads"),
            P("heads"),
            P("heads", None),
            P(("groups", "ctx"), "heads"),
        ),
        out_specs=(
            P(("groups", "ctx"), "heads"),
            P(("groups", "ctx"), "heads"),
            P(("groups", "ctx"), "heads"),
            P(("groups", "ctx"), "heads"),
            P(("groups", "heads"), "ctx"),
        ),
        check_vma=False,
    )
```

```python
import math

import jax
import jax.numpy as jnp
from jax import lax
from jax.experimental import pallas as pl
from jax.experimental.pallas import tpu as pltpu
from jax.sharding import PartitionSpec as P

HIGH = lax.Precision.HIGHEST


def shortened(value):

    def short(part):
        return part.astype(jnp.bfloat16) if part.dtype == jnp.float32 else part

    return jax.tree.map(short, value)


def feature(inner):
    return jnp.where(inner > 0, inner + 1.0, jnp.exp(jnp.minimum(inner, 0.0)))


def feature_slope(inner):
    return jnp.where(inner > 0, 1.0, jnp.exp(jnp.minimum(inner, 0.0)))


def gathered_prefix(stacked_gate, stacked_mem, stacked_norm, own_index, count, upward):
    order = jnp.arange(count, dtype=jnp.int32)
    term_pos = order[:, None]
    inner_pos = order[None, :]
    if upward:
        between = (inner_pos > term_pos) & (inner_pos < own_index)
        active = order < own_index
    else:
        between = (inner_pos < term_pos) & (inner_pos > own_index)
        active = order > own_index
    factor = jnp.prod(jnp.where(between[:, :, None], stacked_gate[None, :, :], 1.0), axis=1)
    weight = jnp.where(active[:, None], factor, 0.0)
    total_mem = jnp.einsum("th,thij->hij", weight, stacked_mem, precision=HIGH)
    total_norm = jnp.einsum("th,thi->hi", weight, stacked_norm, precision=HIGH)
    leading = jnp.prod(jnp.where(active[:, None], stacked_gate, 1.0), axis=0)
    return (leading, total_mem, total_norm)


def plain(queries, key_rows, values, memory_in, norm_in, decays, gate_bias, out_weight, out_grad):
    rows = queries.shape[0]
    heads_here = memory_in.shape[0]
    width = memory_in.shape[1]
    scale = 1.0 / math.sqrt(width)
    shape_three = (rows, heads_here, width)
    query_blk = queries.reshape(shape_three)
    key_blk = key_rows.reshape(shape_three)
    value_blk = values.reshape(shape_three)
    gate_now = decays[0]
    key_f = key_blk.astype(jnp.float32)
    key_feat = feature(key_f).astype(jnp.bfloat16)
    upd_mem = jnp.einsum("thi,thj->hij", key_feat, value_blk, preferred_element_type=jnp.float32)
    upd_norm = jnp.sum(key_feat.astype(jnp.float32), axis=0)
    all_gate, all_mem, all_norm = (
        lax.all_gather(gate_now[None].astype(jnp.bfloat16), "ctx", axis=0, tiled=True).astype(
            jnp.float32
        ),
        lax.all_gather(upd_mem[None].astype(jnp.bfloat16), "ctx", axis=0, tiled=True).astype(
            jnp.float32
        ),
        lax.all_gather(upd_norm[None].astype(jnp.bfloat16), "ctx", axis=0, tiled=True).astype(
            jnp.float32
        ),
    )
    leading, prior_mem, prior_norm = gathered_prefix(
        all_gate, all_mem, all_norm, lax.axis_index("ctx"), lax.axis_size("ctx"), True
    )
    state_mem = leading[:, None, None] * memory_in + prior_mem
    state_norm = leading[:, None] * norm_in + prior_norm
    query_f = query_blk.astype(jnp.float32)
    query_feat = feature(query_f)
    numer = jnp.einsum("thi,hij->thj", query_feat, state_mem, precision=HIGH)
    denom = jnp.einsum("thi,hi->th", query_feat, state_norm, precision=HIGH)
    recall = numer / denom[..., None]
    scores = (
        jnp.einsum("thd,shd->hts", query_blk, key_blk, preferred_element_type=jnp.float32) * scale
    )
    places = jnp.arange(rows, dtype=jnp.int32)
    causal = (places[:, None] >= places[None, :])[None]
    peak = jnp.max(jnp.where(causal, scores, -jnp.inf), axis=-1, keepdims=True)
    expo = jnp.where(causal, jnp.exp(scores - peak), 0.0)
    probs = expo / jnp.sum(expo, axis=-1, keepdims=True)
    probs_half = probs.astype(jnp.bfloat16)
    local_out = jnp.einsum(
        "hts,shd->thd", probs_half, value_blk, preferred_element_type=jnp.float32
    )
    mix = jax.nn.sigmoid(gate_bias)[None, :, None]
    mixed = (
        (mix * recall + (1.0 - mix) * local_out)
        .astype(jnp.bfloat16)
        .reshape(rows, heads_here * width)
    )
    partial_sum = jnp.dot(mixed, out_weight, preferred_element_type=jnp.float32)
    output = lax.psum_scatter(
        partial_sum.astype(jnp.bfloat16), "heads", scatter_dimension=1, tiled=True
    )
    piece = lax.all_gather(out_grad, "heads", axis=1, tiled=True)
    grad_mix = lax.dot_general(
        piece, out_weight, (((1,), (1,)), ((), ())), preferred_element_type=jnp.float32
    )
    block = lax.dot_general(
        mixed, piece, (((0,), (0,)), ((), ())), preferred_element_type=jnp.float32
    )
    grad_mix, collected = (grad_mix, block)
    grad_weight = lax.psum_scatter(
        collected.astype(jnp.bfloat16), "ctx", scatter_dimension=1, tiled=True
    ).astype(jnp.float32)
    grad_seg = grad_mix.reshape(shape_three)
    grad_recall = mix * grad_seg
    grad_local = ((1.0 - mix) * grad_seg).astype(jnp.bfloat16)
    grad_probs = jnp.einsum(
        "thd,shd->hts", grad_local, value_blk, preferred_element_type=jnp.float32
    )
    grad_value_att = jnp.einsum(
        "hts,thd->shd", probs_half, grad_local, preferred_element_type=jnp.float32
    )
    delta = jnp.sum(probs * grad_probs, axis=-1, keepdims=True)
    grad_scores = (probs * (grad_probs - delta) * scale).astype(jnp.bfloat16)
    grad_query_att = jnp.einsum(
        "hts,shd->thd", grad_scores, key_blk, preferred_element_type=jnp.float32
    )
    grad_key_att = jnp.einsum(
        "hts,thd->shd", grad_scores, query_blk, preferred_element_type=jnp.float32
    )
    grad_numer = grad_recall / denom[..., None]
    grad_denom = -jnp.sum(grad_recall * recall, axis=-1) / denom
    grad_qfeat = (
        jnp.einsum("thj,hij->thi", grad_numer, state_mem, precision=HIGH)
        + grad_denom[..., None] * state_norm[None]
    )
    local_mem = jnp.einsum("thi,thj->hij", query_feat, grad_numer, precision=HIGH)
    local_norm = jnp.einsum("thi,th->hi", query_feat, grad_denom, precision=HIGH)
    grad_query = (
        (grad_query_att + grad_qfeat * feature_slope(query_f))
        .astype(jnp.bfloat16)
        .reshape(rows, heads_here * width)
    )
    back_gate, back_mem, back_norm = (
        lax.all_gather(gate_now[None].astype(jnp.bfloat16), "ctx", axis=0, tiled=True).astype(
            jnp.float32
        ),
        lax.all_gather(shortened(local_mem[None]), "ctx", axis=0, tiled=True),
        lax.all_gather(shortened(local_norm[None]), "ctx", axis=0, tiled=True),
    )
    unused_lead, after_mem, after_norm = gathered_prefix(
        back_gate, back_mem, back_norm, lax.axis_index("ctx"), lax.axis_size("ctx"), False
    )
    value_f = value_blk.astype(jnp.float32)
    grad_kfeat = jnp.einsum("thj,hij->thi", value_f, after_mem, precision=HIGH) + after_norm[None]
    grad_key = (
        (grad_key_att + grad_kfeat * feature_slope(key_f))
        .astype(jnp.bfloat16)
        .reshape(rows, heads_here * width)
    )
    grad_value = (
        (
            grad_value_att
            + jnp.einsum("thi,hij->thj", key_feat.astype(jnp.float32), after_mem, precision=HIGH)
        )
        .astype(jnp.bfloat16)
        .reshape(rows, heads_here * width)
    )
    return (output, grad_query, grad_key, grad_value, grad_weight)


MESH = pl.DeviceIdType.MESH
F32 = jnp.float32
BF16 = jnp.bfloat16
HALF = 256
PAD = 16


def mm(left, right):
    return jnp.dot(left, right, preferred_element_type=F32)


def nt(left, right):
    return lax.dot_general(left, right, (((1,), (1,)), ((), ())), preferred_element_type=F32)


def fused(
    q_in, k_in, v_in, mem_in, norm_in, decay_in, gate_in, w_in, og_ref,
    out_ref, gq_ref, gk_ref, gv_ref, gw_ref,
    q_ref, k_ref, v_ref, mem_ref, norm_ref, w_ref, decay_ref, gate_ref,
    og_all, og_end, upd, state, local, after, up_send, up_recv, down_send, down_recv,
    probs, out_t, recall, own_out, grad_mix, mixed, mixed_t, mixed_end, grad_feat, gk_att, gv_att,
    sum_send, sum_recv, fin_send, o_send, o_recv,
    og_s, og_r, end_s, end_r, mix_s, mix_r, up_s, up_r, down_s, down_r, sum_s, sum_r, fin_s, fin_r,
    o_s, o_r, load_s,
):
    rows, cols = q_ref.shape
    heads_here, width = mem_ref.shape[0], mem_ref.shape[1]
    scale = 1.0 / math.sqrt(width)
    me = lax.axis_index("heads")
    place = lax.axis_index("ctx")
    partner = me + 1 - 2 * lax.rem(me, 2)
    cross = lax.rem(me + 2, 4)
    far = lax.rem(partner + 2, 4)
    is_end = (place == 0) | (place == 3)
    is_mid = (place == 1) | (place == 2)
    near = 1 + lax.div(place, 2)
    edge = 3 * lax.div(place, 2)
    side = lax.div(me, 2)
    holds_outer = (me == 0) | (me == 3)
    holds_inner = (me == 1) | (me == 2)
    beside = 3 * side == edge
    across = 3 * side != edge
    ours = (3 * side, 1 + side)
    theirs = (3 - 3 * side, 2 - side)
    part = pl.ds(pl.multiple_of(lax.rem(me, 2) * HALF, HALF), HALF)

    def lanes(h):
        return pl.ds(pl.multiple_of(h * width, width), width)

    def block(j):
        return pl.ds(pl.multiple_of(j * cols, cols), cols)

    def send(src, dst, s, r, **where):
        return pltpu.make_async_remote_copy(
            src_ref=src, dst_ref=dst, send_sem=s, recv_sem=r, device_id=where, device_id_type=MESH
        )

    def mix_of(h):
        return 1.0 / (1.0 + jnp.exp(-jnp.full((1, width), gate_ref[0, h], F32)))

    loads = [
        pltpu.make_async_copy(src, dst, load_s.at[i])
        for i, (src, dst) in enumerate(
            (
                (k_in, k_ref), (v_in, v_ref), (q_in, q_ref), (mem_in, mem_ref),
                (norm_in, norm_ref), (w_in, w_ref), (og_ref, og_all.at[:, block(me)]),
                (decay_in, decay_ref), (gate_in, gate_ref),
            )
        )
    ]
    for i in (6, 0, 1, 2, 3, 4, 7, 8, 5):
        loads[i].start()

    barrier = pltpu.get_barrier_semaphore()
    for peer in (partner, cross):
        pl.semaphore_signal(barrier, inc=1, device_id={"heads": peer}, device_id_type=MESH)
    for step in (-1, 1):

        @pl.when((place + step >= 0) & (place + step <= 3))
        def _():
            pl.semaphore_signal(
                barrier, inc=1, device_id={"ctx": place + step}, device_id_type=MESH
            )

    def piece(ref, j):
        return ref.at[part, block(j)]

    own_block = og_all.at[:, block(me)]
    og_pair = send(own_block, own_block, og_s.at[0], og_r.at[0], heads=partner)
    og_inner = send(
        piece(og_all, ours[1]), piece(og_all, ours[1]), og_s.at[1], og_r.at[1], heads=cross
    )

    def fine(ref, j, i):
        start = lax.rem(me, 2) * HALF + i * (HALF // 2)
        return ref.at[pl.ds(pl.multiple_of(start, HALF // 2), HALF // 2), block(j)]

    og_outer = [
        send(fine(og_all, ours[0], i), fine(og_all, ours[0], i), og_s.at[5 + i], og_r.at[5 + i],
             heads=cross)
        for i in range(2)
    ]
    og_relay = [
        send(piece(og_all, theirs[i]), piece(og_all, theirs[i]), og_s.at[3 + i], og_r.at[3 + i],
             heads=partner)
        for i in range(2)
    ]
    lead = piece(og_end, 3 - edge)
    inner = piece(og_end, ours[1])
    inner_far = piece(og_end, theirs[1])
    ship_lead = [
        send(fine(og_all, 3 - edge, i), fine(og_end, 3 - edge, i), end_s.at[6 * i], end_r.at[6 * i],
             ctx=near)
        for i in range(2)
    ]
    ship_inner = send(piece(og_all, ours[1]), inner, end_s.at[1], end_r.at[1], ctx=near)
    lead_pair = send(lead, lead, end_s.at[2], end_r.at[2], heads=partner)
    inner_pair = send(inner, inner, end_s.at[3], end_r.at[3], heads=partner)
    inner_cross = send(inner, inner, end_s.at[4], end_r.at[4], heads=cross)
    inner_relay = send(inner_far, inner_far, end_s.at[5], end_r.at[5], heads=partner)

    def strip(h):
        return pl.ds(pl.multiple_of(h * width, width), width)

    def mix_copy(h):
        return send(
            mixed_t.at[strip(h)], mixed_end.at[strip(h)], mix_s.at[h], mix_r.at[h], ctx=near
        )

    def sum_copy(i, h):
        return send(
            sum_send.at[i, strip(h)], sum_recv.at[i, strip(h)], sum_s.at[i, h], sum_r.at[i, h],
            ctx=3 - near,
        )

    def fin_copy(h):
        return send(
            fin_send.at[strip(h)], sum_recv.at[0, strip(h)], fin_s.at[h], fin_r.at[h], ctx=edge
        )


    def update(h, carry):
        key_feat = feature(k_ref[:, lanes(h)].astype(F32)).astype(BF16)
        upd[h, :width] = mm(key_feat.T, v_ref[:, lanes(h)])
        total = jnp.sum(key_feat.astype(F32), axis=0, keepdims=True)
        upd[h, width:] = jnp.broadcast_to(total, (PAD, width))
        return carry

    pl.semaphore_wait(barrier, 3 + is_mid.astype(jnp.int32))
    loads[6].wait()
    og_pair.start()

    def launch():
        for copy in og_outer:
            copy.start()

        @pl.when(is_end & across)
        def _():
            for copy in ship_lead:
                copy.start()

    @pl.when(holds_outer & (place > 0))
    def _():
        launch()

    loads[0].wait()
    loads[1].wait()
    lax.fori_loop(0, heads_here, update, 0)

    def up_copy(h, target):
        return send(up_send.at[h], up_recv.at[h], up_s.at[h], up_r.at[h], ctx=target)

    def up_step(index):
        @pl.when(place == index)
        def _():
            for h in range(heads_here):
                if index == 0:
                    state[h, :width] = mem_ref[h]
                    state[h, width:] = jnp.broadcast_to(norm_ref[h : h + 1, :], (PAD, width))
                else:
                    up_copy(h, index - 1).wait_recv()
                    state[h] = up_recv[h].astype(F32)
                if index < 3:
                    up_send[h] = (decay_ref[0, h] * state[h] + upd[h]).astype(BF16)
                    up_copy(h, index + 1).start()

    def down_copy(h, target):
        return send(down_send.at[h], down_recv.at[h], down_s.at[h], down_r.at[h], ctx=target)

    def down_step(index):
        @pl.when(place == index)
        def _():
            if index == 3:
                after[...] = jnp.zeros_like(after)
            for h in range(heads_here):
                if index < 3:
                    down_copy(h, index + 1).wait_recv()
                    after[h] = down_recv[h].astype(F32)
                if index > 0:
                    down_send[h] = (decay_ref[0, h] * after[h] + local[h]).astype(BF16)
                    down_copy(h, index - 1).start()

    keep = lax.broadcasted_iota(jnp.int32, (HALF, HALF), 0) <= lax.broadcasted_iota(
        jnp.int32, (HALF, HALF), 1
    )
    factor = scale * math.log2(math.e)
    parts = rows // HALF

    def span(j):
        return slice(j * HALF, (j + 1) * HALF)

    def forward(h, carry):
        values_t = v_ref[:, lanes(h)].T
        for b in range(parts):
            query = q_ref[span(b), lanes(h)]
            scores = [nt(k_ref[span(j), lanes(h)], query) for j in range(b + 1)]
            scores[b] = jnp.where(keep, scores[b], -1e30)
            peak = jnp.max(scores[0], axis=0, keepdims=True)
            for piece in scores[1:]:
                peak = jnp.maximum(peak, jnp.max(piece, axis=0, keepdims=True))
            expo = [jnp.exp2((piece - peak) * factor) for piece in scores]
            total = sum(jnp.sum(piece, axis=0, keepdims=True) for piece in expo)
            inverse = 1.0 / total
            acc = None
            for j in range(b + 1):
                prob = (expo[j] * inverse).astype(BF16)
                probs[h, span(j), span(b)] = prob
                term = mm(values_t[:, span(j)], prob)
                acc = term if acc is None else acc + term
            out_t[h, :, span(b)] = acc
        return carry

    for i in (3, 4, 7, 8):
        loads[i].wait()
    up_step(0)

    @pl.when(holds_outer & (place == 0))
    def _():
        launch()

    loads[2].wait()
    lax.fori_loop(0, 1, forward, 0)
    og_pair.wait_recv()

    @pl.when(holds_inner)
    def _():
        launch()

    og_inner.start()

    @pl.when(is_end)
    def _():
        ship_inner.start()

    lax.fori_loop(1, 2, forward, 0)
    up_step(1)
    lax.fori_loop(2, heads_here, forward, 0)
    up_step(2)
    for i in range(2):
        og_outer[i].wait_recv()

        @pl.when(is_end & beside)
        def _():
            ship_lead[i].start()

    og_relay[0].start()

    def pass_lead():
        for copy in ship_lead:
            copy.wait_recv()
        lead_pair.start()

    def pass_inner():
        ship_inner.wait_recv()
        inner_cross.start()
        inner_pair.start()

    @pl.when(is_mid & across)
    def _():
        pass_lead()

    @pl.when(is_mid & beside)
    def _():
        pass_inner()

    up_step(3)

    def recall_step(h, carry):
        mem = state[h, :width].astype(BF16)
        norm = state[h, width : width + 1]
        query_feat = feature(q_ref[:, lanes(h)].astype(F32))
        inverse = 1.0 / jnp.sum(query_feat * norm, axis=1, keepdims=True)
        recalled = mm(query_feat.astype(BF16), mem) * inverse
        recall[:, lanes(h)] = recalled
        mix = mix_of(h)
        both = (mix * recalled + (1.0 - mix) * out_t[h].T).astype(BF16)
        mixed[:, lanes(h)] = both
        mixed_t[strip(h), :] = both.T

        @pl.when(is_end & (h < 2))
        def _():
            mix_copy(h).start()

        return carry

    lax.fori_loop(0, heads_here, recall_step, 0)
    loads[5].wait()
    o_far = send(o_send.at[0], o_recv.at[0], o_s.at[0], o_r.at[0], heads=partner)
    o_pair = send(o_send.at[1], o_recv.at[1], o_s.at[1], o_r.at[1], heads=partner)
    o_cross = send(o_send.at[2], o_recv.at[2], o_s.at[2], o_r.at[2], heads=cross)
    o_send[0] = mm(mixed[...], w_ref[:, block(far)]).astype(BF16)
    o_far.start()
    o_send[1] = mm(mixed[...], w_ref[:, block(partner)]).astype(BF16)
    o_pair.start()
    value = mm(mixed[...], w_ref[:, block(cross)])
    o_far.wait_recv()
    o_send[2] = (value + o_recv[0].astype(F32)).astype(BF16)
    own_out[...] = mm(mixed[...], w_ref[:, block(me)])

    def both_terms(h, j):
        return mm(mixed_t[strip(h), :], og_all[:, block(j)]) + mm(
            mixed_end[strip(h), :], og_end[:, block(j)]
        )

    def sum_step(i, j):
        def step(h):
            if i == 0:
                mix_copy(h).wait_recv()
            sum_send[i, strip(h)] = both_terms(h, j).astype(BF16)
            sum_copy(i, h).start()

        return step

    @pl.when(is_end)
    def _():
        o_cross.start()

    og_inner.wait_recv()
    og_relay[1].start()

    @pl.when(is_mid & across)
    def _():
        pass_inner()

    @pl.when(is_mid & beside)
    def _():
        pass_lead()

    @pl.when(is_mid)
    def _():
        o_cross.start()

    og_relay[0].wait_recv()
    og_relay[1].wait_recv()

    def grad_block(j, carry):
        here = pl.ds(pl.multiple_of(j * HALF, HALF), HALF)
        grad_mix[:, here] = nt(og_all[...], w_ref[here, :])
        return carry

    lax.fori_loop(0, cols // HALF, grad_block, 0)

    def memory_step(h, carry):
        mem = state[h, :width].astype(BF16)
        norm = state[h, width : width + 1]
        query = q_ref[:, lanes(h)].astype(F32)
        query_feat = feature(query)
        inverse = 1.0 / jnp.sum(query_feat * norm, axis=1, keepdims=True)
        grad_recall = mix_of(h) * grad_mix[:, lanes(h)]
        grad_numer = (grad_recall * inverse).astype(BF16)
        grad_denom = -jnp.sum(grad_recall * recall[:, lanes(h)], axis=1, keepdims=True) * inverse
        grad_feat[:, lanes(h)] = (nt(grad_numer, mem) + grad_denom * norm) * feature_slope(query)
        local[h, :width] = mm(query_feat.astype(BF16).T, grad_numer)
        total = jnp.sum(query_feat * grad_denom, axis=0, keepdims=True)
        local[h, width:] = jnp.broadcast_to(total, (PAD, width))
        return carry

    @pl.when(is_mid)
    def _():
        lead_pair.wait_recv()
        sum_step(0, 3 - edge)(0)

    lax.fori_loop(0, heads_here, memory_step, 0)
    down_step(3)

    @pl.when(is_end)
    def _():
        for h in range(2, heads_here):
            mix_copy(h).start()


    @pl.when(is_mid)
    def _():
        sum_step(0, 3 - edge)(1)
        inner_cross.wait_recv()
        inner_relay.start()

    down_step(2)

    @pl.when(is_mid)
    def _():
        inner_pair.wait_recv()
        inner_relay.wait_recv()
        for h in range(heads_here):
            sum_step(1, 3 - near)(h)
            if h < 2:
                sum_step(0, 3 - edge)(h + 2)

    down_step(1)
    gw_ref[...] = mm(mixed_t[...], og_all[:, block(place)])

    @pl.when(is_mid)
    def _():
        gw_ref[...] += mm(mixed_end[...], og_end[:, block(place)])

    def backward(h, carry):
        mix = mix_of(h)
        grad_local = ((1.0 - mix) * grad_mix[:, lanes(h)]).astype(BF16)
        grad_t = grad_local.T
        delta = jnp.sum(grad_t.astype(F32) * out_t[h], axis=0, keepdims=True)
        keys_t = k_ref[:, lanes(h)].T
        for b in range(parts):
            query = q_ref[span(b), lanes(h)]
            acc = None
            for j in range(b + 1):
                prob = probs[h, span(j), span(b)]
                grad_prob = mm(v_ref[span(j), lanes(h)], grad_t[:, span(b)])
                grad_score = (prob.astype(F32) * (grad_prob - delta[:, span(b)]) * scale).astype(
                    BF16
                )
                term = mm(keys_t[:, span(j)], grad_score)
                acc = term if acc is None else acc + term
                key_term = mm(grad_score, query)
                value_term = mm(prob, grad_local[span(b), :])
                if b == j:
                    gk_att[span(j), lanes(h)] = key_term
                    gv_att[span(j), lanes(h)] = value_term
                else:
                    gk_att[span(j), lanes(h)] += key_term
                    gv_att[span(j), lanes(h)] += value_term
            gq_ref[span(b), lanes(h)] = (acc.T + grad_feat[span(b), lanes(h)]).astype(BF16)
        return carry

    def backward_step(h, carry):
        backward(h, carry)

        @pl.when(is_mid)
        def _():
            sum_copy(0, h).wait_recv()
            fin_send[strip(h)] = (
                mm(mixed_t[strip(h), :], og_all[:, block(edge)])
                + sum_recv[0, strip(h)].astype(F32)
            ).astype(BF16)
            fin_copy(h).start()

        return carry

    lax.fori_loop(0, heads_here, backward_step, 0)
    o_pair.wait_recv()
    o_cross.wait_recv()
    out_ref[...] = (own_out[...] + o_recv[1].astype(F32) + o_recv[2].astype(F32)).astype(BF16)
    down_step(0)

    def finish(h, carry):
        mem = after[h, :width].astype(BF16)
        key = k_ref[:, lanes(h)].astype(F32)
        value = v_ref[:, lanes(h)]
        grad_kfeat = nt(value, mem) + after[h, width : width + 1]
        gk_ref[:, lanes(h)] = (gk_att[:, lanes(h)] + grad_kfeat * feature_slope(key)).astype(BF16)
        key_feat = feature(key).astype(BF16)
        gv_ref[:, lanes(h)] = (gv_att[:, lanes(h)] + mm(key_feat, mem)).astype(BF16)
        return carry

    lax.fori_loop(0, heads_here, finish, 0)

    def last_step(h, carry):
        @pl.when(is_mid)
        def _():
            sum_copy(1, h).wait_recv()
            gw_ref[strip(h)] += sum_recv[1, strip(h)].astype(F32)

        @pl.when(is_end)
        def _():
            fin_copy(h).wait_recv()
            gw_ref[strip(h)] += sum_recv[0, strip(h)].astype(F32)

        return carry

    lax.fori_loop(0, heads_here, last_step, 0)
    for copy in (og_pair, og_inner, *og_outer, *og_relay, o_far, o_pair, o_cross):
        copy.wait_send()

    @pl.when(is_end)
    def _():
        for copy in ship_lead:
            copy.wait_send()
        ship_inner.wait_send()
        for h in range(heads_here):
            mix_copy(h).wait_send()

    @pl.when(is_mid)
    def _():
        for copy in (lead_pair, inner_pair, inner_cross, inner_relay):
            copy.wait_send()
        for h in range(heads_here):
            sum_copy(0, h).wait_send()
            sum_copy(1, h).wait_send()
            fin_copy(h).wait_send()

    @pl.when(place < 3)
    def _():
        for h in range(heads_here):
            up_copy(h, near).wait_send()

    @pl.when(place > 0)
    def _():
        for h in range(heads_here):
            down_copy(h, near).wait_send()


def settle(*refs):
    sems = refs[-1]
    count = len(refs) // 2
    copies = [
        pltpu.make_async_copy(refs[i], refs[count + i], sems.at[i]) for i in range(count)
    ]
    for copy in copies:
        copy.start()
    for copy in copies:
        copy.wait()


def shards(queries, key_rows, values, memory_in, norm_in, decays, gate_bias, out_weight, out_grad):
    rows, cols = queries.shape
    heads_here, width = memory_in.shape[0], memory_in.shape[1]
    if (
        lax.axis_size("ctx") != 4
        or lax.axis_size("heads") != 4
        or rows != 2 * HALF
        or cols != rows
        or heads_here != 4
        or width != 128
    ):
        return plain(
            queries, key_rows, values, memory_in, norm_in, decays, gate_bias, out_weight, out_grad
        )
    wide = out_weight.shape[1]
    free = pl.BlockSpec(memory_space=pl.ANY)
    small = (heads_here, width + PAD, width)
    half = jax.ShapeDtypeStruct((rows, cols), BF16)
    dma = pltpu.SemaphoreType.DMA
    shapes = (half, half, half, half, jax.ShapeDtypeStruct((cols, cols), F32))
    held = tuple(pltpu.VMEM(x.shape, x.dtype) for x in shapes)
    results = pl.pallas_call(
        fused,
        out_shape=held,
        in_specs=[free] * 9,
        out_specs=(pl.BlockSpec(memory_space=pltpu.VMEM),) * 5,
        scratch_shapes=[
            pltpu.VMEM((rows, cols), BF16),
            pltpu.VMEM((rows, cols), BF16),
            pltpu.VMEM((rows, cols), BF16),
            pltpu.VMEM((heads_here, width, width), F32),
            pltpu.VMEM((heads_here, width), F32),
            pltpu.VMEM((cols, wide), BF16),
            pltpu.SMEM((1, heads_here), F32),
            pltpu.SMEM((1, heads_here), F32),
            pltpu.VMEM((rows, wide), BF16),
            pltpu.VMEM((rows, wide), BF16),
            pltpu.VMEM(small, F32),
            pltpu.VMEM(small, F32),
            pltpu.VMEM(small, F32),
            pltpu.VMEM(small, F32),
            pltpu.VMEM(small, BF16),
            pltpu.VMEM(small, BF16),
            pltpu.VMEM(small, BF16),
            pltpu.VMEM(small, BF16),
            pltpu.VMEM((heads_here, rows, rows), BF16),
            pltpu.VMEM((heads_here, width, rows), F32),
            pltpu.VMEM((rows, cols), F32),
            pltpu.VMEM((rows, cols), F32),
            pltpu.VMEM((rows, cols), F32),
            pltpu.VMEM((rows, cols), BF16),
            pltpu.VMEM((cols, rows), BF16),
            pltpu.VMEM((cols, rows), BF16),
            pltpu.VMEM((rows, cols), F32),
            pltpu.VMEM((rows, cols), F32),
            pltpu.VMEM((rows, cols), F32),
            pltpu.VMEM((2, cols, cols), BF16),
            pltpu.VMEM((2, cols, cols), BF16),
            pltpu.VMEM((cols, cols), BF16),
            pltpu.VMEM((3, rows, cols), BF16),
            pltpu.VMEM((3, rows, cols), BF16),
            dma((7,)), dma((7,)), dma((7,)), dma((7,)), dma((4,)), dma((4,)),
            dma((4,)), dma((4,)), dma((4,)), dma((4,)),
            dma((2, 4)), dma((2, 4)), dma((4,)), dma((4,)),
            dma((3,)), dma((3,)), dma((9,)),
        ],
        compiler_params=pltpu.CompilerParams(
            collective_id=0, has_side_effects=True, vmem_limit_bytes=48 << 20
        ),
    )(
        *(
            pltpu.with_memory_space_constraint(x, pltpu.HBM)
            for x in (
                queries, key_rows, values, memory_in, norm_in, decays,
                gate_bias.reshape(1, heads_here), out_weight, out_grad,
            )
        )
    )
    results = [pltpu.with_memory_space_constraint(x, pltpu.VMEM) for x in results]
    return pl.pallas_call(
        settle,
        out_shape=shapes,
        in_specs=[pl.BlockSpec(memory_space=pltpu.VMEM)] * 5,
        out_specs=(free,) * 5,
        scratch_shapes=[dma((5,))],
    )(*results)


def solution(mesh):
    return jax.shard_map(
        shards,
        mesh=mesh,
        in_specs=(
            P(("groups", "ctx"), "heads"),
            P(("groups", "ctx"), "heads"),
            P(("groups", "ctx"), "heads"),
            P(("groups", "heads"), None, None),
            P(("groups", "heads"), None),
            P(("groups", "ctx"), "heads"),
            P("heads"),
            P("heads", None),
            P(("groups", "ctx"), "heads"),
        ),
        out_specs=(
            P(("groups", "ctx"), "heads"),
            P(("groups", "ctx"), "heads"),
            P(("groups", "ctx"), "heads"),
            P(("groups", "ctx"), "heads"),
            P(("groups", "heads"), "ctx"),
        ),
        check_vma=False,
    )
```

```python
import math

import jax
import jax.numpy as jnp
from jax import lax
from jax.experimental import pallas as pl
from jax.experimental.pallas import tpu as pltpu
from jax.sharding import PartitionSpec as P

HIGH = lax.Precision.HIGHEST


def shortened(value):

    def short(part):
        return part.astype(jnp.bfloat16) if part.dtype == jnp.float32 else part

    return jax.tree.map(short, value)


def feature(inner):
    return jnp.where(inner > 0, inner + 1.0, jnp.exp(jnp.minimum(inner, 0.0)))


def feature_slope(inner):
    return jnp.where(inner > 0, 1.0, jnp.exp(jnp.minimum(inner, 0.0)))


def gathered_prefix(stacked_gate, stacked_mem, stacked_norm, own_index, count, upward):
    order = jnp.arange(count, dtype=jnp.int32)
    term_pos = order[:, None]
    inner_pos = order[None, :]
    if upward:
        between = (inner_pos > term_pos) & (inner_pos < own_index)
        active = order < own_index
    else:
        between = (inner_pos < term_pos) & (inner_pos > own_index)
        active = order > own_index
    factor = jnp.prod(jnp.where(between[:, :, None], stacked_gate[None, :, :], 1.0), axis=1)
    weight = jnp.where(active[:, None], factor, 0.0)
    total_mem = jnp.einsum("th,thij->hij", weight, stacked_mem, precision=HIGH)
    total_norm = jnp.einsum("th,thi->hi", weight, stacked_norm, precision=HIGH)
    leading = jnp.prod(jnp.where(active[:, None], stacked_gate, 1.0), axis=0)
    return (leading, total_mem, total_norm)


def plain(queries, key_rows, values, memory_in, norm_in, decays, gate_bias, out_weight, out_grad):
    rows = queries.shape[0]
    heads_here = memory_in.shape[0]
    width = memory_in.shape[1]
    scale = 1.0 / math.sqrt(width)
    shape_three = (rows, heads_here, width)
    query_blk = queries.reshape(shape_three)
    key_blk = key_rows.reshape(shape_three)
    value_blk = values.reshape(shape_three)
    gate_now = decays[0]
    key_f = key_blk.astype(jnp.float32)
    key_feat = feature(key_f).astype(jnp.bfloat16)
    upd_mem = jnp.einsum("thi,thj->hij", key_feat, value_blk, preferred_element_type=jnp.float32)
    upd_norm = jnp.sum(key_feat.astype(jnp.float32), axis=0)
    all_gate, all_mem, all_norm = (
        lax.all_gather(gate_now[None].astype(jnp.bfloat16), "ctx", axis=0, tiled=True).astype(
            jnp.float32
        ),
        lax.all_gather(upd_mem[None].astype(jnp.bfloat16), "ctx", axis=0, tiled=True).astype(
            jnp.float32
        ),
        lax.all_gather(upd_norm[None].astype(jnp.bfloat16), "ctx", axis=0, tiled=True).astype(
            jnp.float32
        ),
    )
    leading, prior_mem, prior_norm = gathered_prefix(
        all_gate, all_mem, all_norm, lax.axis_index("ctx"), lax.axis_size("ctx"), True
    )
    state_mem = leading[:, None, None] * memory_in + prior_mem
    state_norm = leading[:, None] * norm_in + prior_norm
    query_f = query_blk.astype(jnp.float32)
    query_feat = feature(query_f)
    numer = jnp.einsum("thi,hij->thj", query_feat, state_mem, precision=HIGH)
    denom = jnp.einsum("thi,hi->th", query_feat, state_norm, precision=HIGH)
    recall = numer / denom[..., None]
    scores = (
        jnp.einsum("thd,shd->hts", query_blk, key_blk, preferred_element_type=jnp.float32) * scale
    )
    places = jnp.arange(rows, dtype=jnp.int32)
    causal = (places[:, None] >= places[None, :])[None]
    peak = jnp.max(jnp.where(causal, scores, -jnp.inf), axis=-1, keepdims=True)
    expo = jnp.where(causal, jnp.exp(scores - peak), 0.0)
    probs = expo / jnp.sum(expo, axis=-1, keepdims=True)
    probs_half = probs.astype(jnp.bfloat16)
    local_out = jnp.einsum(
        "hts,shd->thd", probs_half, value_blk, preferred_element_type=jnp.float32
    )
    mix = jax.nn.sigmoid(gate_bias)[None, :, None]
    mixed = (
        (mix * recall + (1.0 - mix) * local_out)
        .astype(jnp.bfloat16)
        .reshape(rows, heads_here * width)
    )
    partial_sum = jnp.dot(mixed, out_weight, preferred_element_type=jnp.float32)
    output = lax.psum_scatter(
        partial_sum.astype(jnp.bfloat16), "heads", scatter_dimension=1, tiled=True
    )
    piece = lax.all_gather(out_grad, "heads", axis=1, tiled=True)
    grad_mix = lax.dot_general(
        piece, out_weight, (((1,), (1,)), ((), ())), preferred_element_type=jnp.float32
    )
    block = lax.dot_general(
        mixed, piece, (((0,), (0,)), ((), ())), preferred_element_type=jnp.float32
    )
    grad_mix, collected = (grad_mix, block)
    grad_weight = lax.psum_scatter(
        collected.astype(jnp.bfloat16), "ctx", scatter_dimension=1, tiled=True
    ).astype(jnp.float32)
    grad_seg = grad_mix.reshape(shape_three)
    grad_recall = mix * grad_seg
    grad_local = ((1.0 - mix) * grad_seg).astype(jnp.bfloat16)
    grad_probs = jnp.einsum(
        "thd,shd->hts", grad_local, value_blk, preferred_element_type=jnp.float32
    )
    grad_value_att = jnp.einsum(
        "hts,thd->shd", probs_half, grad_local, preferred_element_type=jnp.float32
    )
    delta = jnp.sum(probs * grad_probs, axis=-1, keepdims=True)
    grad_scores = (probs * (grad_probs - delta) * scale).astype(jnp.bfloat16)
    grad_query_att = jnp.einsum(
        "hts,shd->thd", grad_scores, key_blk, preferred_element_type=jnp.float32
    )
    grad_key_att = jnp.einsum(
        "hts,thd->shd", grad_scores, query_blk, preferred_element_type=jnp.float32
    )
    grad_numer = grad_recall / denom[..., None]
    grad_denom = -jnp.sum(grad_recall * recall, axis=-1) / denom
    grad_qfeat = (
        jnp.einsum("thj,hij->thi", grad_numer, state_mem, precision=HIGH)
        + grad_denom[..., None] * state_norm[None]
    )
    local_mem = jnp.einsum("thi,thj->hij", query_feat, grad_numer, precision=HIGH)
    local_norm = jnp.einsum("thi,th->hi", query_feat, grad_denom, precision=HIGH)
    grad_query = (
        (grad_query_att + grad_qfeat * feature_slope(query_f))
        .astype(jnp.bfloat16)
        .reshape(rows, heads_here * width)
    )
    back_gate, back_mem, back_norm = (
        lax.all_gather(gate_now[None].astype(jnp.bfloat16), "ctx", axis=0, tiled=True).astype(
            jnp.float32
        ),
        lax.all_gather(shortened(local_mem[None]), "ctx", axis=0, tiled=True),
        lax.all_gather(shortened(local_norm[None]), "ctx", axis=0, tiled=True),
    )
    unused_lead, after_mem, after_norm = gathered_prefix(
        back_gate, back_mem, back_norm, lax.axis_index("ctx"), lax.axis_size("ctx"), False
    )
    value_f = value_blk.astype(jnp.float32)
    grad_kfeat = jnp.einsum("thj,hij->thi", value_f, after_mem, precision=HIGH) + after_norm[None]
    grad_key = (
        (grad_key_att + grad_kfeat * feature_slope(key_f))
        .astype(jnp.bfloat16)
        .reshape(rows, heads_here * width)
    )
    grad_value = (
        (
            grad_value_att
            + jnp.einsum("thi,hij->thj", key_feat.astype(jnp.float32), after_mem, precision=HIGH)
        )
        .astype(jnp.bfloat16)
        .reshape(rows, heads_here * width)
    )
    return (output, grad_query, grad_key, grad_value, grad_weight)


MESH = pl.DeviceIdType.MESH
F32 = jnp.float32
BF16 = jnp.bfloat16
HALF = 256
PAD = 16


def mm(left, right):
    return jnp.dot(left, right, preferred_element_type=F32)


def nt(left, right):
    return lax.dot_general(left, right, (((1,), (1,)), ((), ())), preferred_element_type=F32)


def fused(
    q_in, k_in, v_in, mem_in, norm_in, decay_in, gate_in, w_in, og_ref,
    out_ref, gq_ref, gk_ref, gv_ref, gw_ref,
    q_ref, k_ref, v_ref, mem_ref, norm_ref, w_ref, decay_ref, gate_ref,
    og_all, og_end, upd, state, local, after, up_send, up_recv, down_send, down_recv,
    probs, out_t, recall, own_out, grad_mix, mixed, mixed_t, mixed_end, grad_feat, gk_att, gv_att,
    sum_send, sum_recv, fin_send, o_send, o_recv,
    og_s, og_r, end_s, end_r, mix_s, mix_r, up_s, up_r, down_s, down_r, sum_s, sum_r, fin_s, fin_r,
    o_s, o_r, load_s,
):
    rows, cols = q_ref.shape
    heads_here, width = mem_ref.shape[0], mem_ref.shape[1]
    scale = 1.0 / math.sqrt(width)
    me = lax.axis_index("heads")
    place = lax.axis_index("ctx")
    partner = me + 1 - 2 * lax.rem(me, 2)
    cross = lax.rem(me + 2, 4)
    far = lax.rem(partner + 2, 4)
    is_end = (place == 0) | (place == 3)
    is_mid = (place == 1) | (place == 2)
    near = 1 + lax.div(place, 2)
    edge = 3 * lax.div(place, 2)
    side = lax.div(me, 2)
    holds_outer = (me == 0) | (me == 3)
    holds_inner = (me == 1) | (me == 2)
    beside = 3 * side == edge
    across = 3 * side != edge
    ours = (3 * side, 1 + side)
    theirs = (3 - 3 * side, 2 - side)
    part = pl.ds(pl.multiple_of(lax.rem(me, 2) * HALF, HALF), HALF)

    def lanes(h):
        return pl.ds(pl.multiple_of(h * width, width), width)

    def block(j):
        return pl.ds(pl.multiple_of(j * cols, cols), cols)

    def send(src, dst, s, r, **where):
        return pltpu.make_async_remote_copy(
            src_ref=src, dst_ref=dst, send_sem=s, recv_sem=r, device_id=where, device_id_type=MESH
        )

    def mix_of(h):
        return 1.0 / (1.0 + jnp.exp(-jnp.full((1, width), gate_ref[0, h], F32)))

    loads = [
        pltpu.make_async_copy(src, dst, load_s.at[i])
        for i, (src, dst) in enumerate(
            (
                (k_in, k_ref), (v_in, v_ref), (q_in, q_ref), (mem_in, mem_ref),
                (norm_in, norm_ref), (w_in, w_ref), (og_ref, og_all.at[:, block(me)]),
                (decay_in, decay_ref), (gate_in, gate_ref),
            )
        )
    ]
    for i in (6, 0, 1, 2, 3, 4, 7, 8, 5):
        loads[i].start()

    barrier = pltpu.get_barrier_semaphore()
    for peer in (partner, cross):
        pl.semaphore_signal(barrier, inc=1, device_id={"heads": peer}, device_id_type=MESH)
    for step in (-1, 1):

        @pl.when((place + step >= 0) & (place + step <= 3))
        def _():
            pl.semaphore_signal(
                barrier, inc=1, device_id={"ctx": place + step}, device_id_type=MESH
            )

    def piece(ref, j):
        return ref.at[part, block(j)]

    own_block = og_all.at[:, block(me)]
    og_pair = send(own_block, own_block, og_s.at[0], og_r.at[0], heads=partner)
    og_inner = send(
        piece(og_all, ours[1]), piece(og_all, ours[1]), og_s.at[1], og_r.at[1], heads=cross
    )

    def fine(ref, j, i):
        start = lax.rem(me, 2) * HALF + i * (HALF // 2)
        return ref.at[pl.ds(pl.multiple_of(start, HALF // 2), HALF // 2), block(j)]

    og_outer = [
        send(fine(og_all, ours[0], i), fine(og_all, ours[0], i), og_s.at[5 + i], og_r.at[5 + i],
             heads=cross)
        for i in range(2)
    ]
    og_relay = [
        send(piece(og_all, theirs[i]), piece(og_all, theirs[i]), og_s.at[3 + i], og_r.at[3 + i],
             heads=partner)
        for i in range(2)
    ]
    lead = piece(og_end, 3 - edge)
    inner = piece(og_end, ours[1])
    inner_far = piece(og_end, theirs[1])
    ship_lead = [
        send(fine(og_all, 3 - edge, i), fine(og_end, 3 - edge, i), end_s.at[6 * i], end_r.at[6 * i],
             ctx=near)
        for i in range(2)
    ]
    ship_inner = send(piece(og_all, ours[1]), inner, end_s.at[1], end_r.at[1], ctx=near)
    lead_pair = send(lead, lead, end_s.at[2], end_r.at[2], heads=partner)
    inner_pair = send(inner, inner, end_s.at[3], end_r.at[3], heads=partner)
    inner_cross = send(inner, inner, end_s.at[4], end_r.at[4], heads=cross)
    inner_relay = send(inner_far, inner_far, end_s.at[5], end_r.at[5], heads=partner)

    def strip(h):
        return pl.ds(pl.multiple_of(h * width, width), width)

    def mix_copy(h):
        return send(
            mixed_t.at[strip(h)], mixed_end.at[strip(h)], mix_s.at[h], mix_r.at[h], ctx=near
        )

    def sum_copy(i, h):
        return send(
            sum_send.at[i, strip(h)], sum_recv.at[i, strip(h)], sum_s.at[i, h], sum_r.at[i, h],
            ctx=3 - near,
        )

    def fin_copy(h):
        return send(
            fin_send.at[strip(h)], sum_recv.at[0, strip(h)], fin_s.at[h], fin_r.at[h], ctx=edge
        )


    def update(h, carry):
        key_feat = feature(k_ref[:, lanes(h)].astype(F32)).astype(BF16)
        upd[h, :width] = mm(key_feat.T, v_ref[:, lanes(h)])
        total = jnp.sum(key_feat.astype(F32), axis=0, keepdims=True)
        upd[h, width:] = jnp.broadcast_to(total, (PAD, width))
        return carry

    pl.semaphore_wait(barrier, 3 + is_mid.astype(jnp.int32))
    loads[6].wait()
    og_pair.start()

    def launch():
        for copy in og_outer:
            copy.start()

        @pl.when(is_end & across)
        def _():
            for copy in ship_lead:
                copy.start()

    @pl.when(holds_outer & (place > 0))
    def _():
        launch()

    loads[0].wait()
    loads[1].wait()
    lax.fori_loop(0, heads_here, update, 0)

    def up_copy(h, target):
        return send(up_send.at[h], up_recv.at[h], up_s.at[h], up_r.at[h], ctx=target)

    def up_step(index):
        @pl.when(place == index)
        def _():
            for h in range(heads_here):
                if index == 0:
                    state[h, :width] = mem_ref[h]
                    state[h, width:] = jnp.broadcast_to(norm_ref[h : h + 1, :], (PAD, width))
                else:
                    up_copy(h, index - 1).wait_recv()
                    state[h] = up_recv[h].astype(F32)
                if index < 3:
                    up_send[h] = (decay_ref[0, h] * state[h] + upd[h]).astype(BF16)
                    up_copy(h, index + 1).start()

    def down_copy(h, target):
        return send(down_send.at[h], down_recv.at[h], down_s.at[h], down_r.at[h], ctx=target)

    def down_step(index):
        @pl.when(place == index)
        def _():
            if index == 3:
                after[...] = jnp.zeros_like(after)
            for h in range(heads_here):
                if index < 3:
                    down_copy(h, index + 1).wait_recv()
                    after[h] = down_recv[h].astype(F32)
                if index > 0:
                    down_send[h] = (decay_ref[0, h] * after[h] + local[h]).astype(BF16)
                    down_copy(h, index - 1).start()

    keep = lax.broadcasted_iota(jnp.int32, (HALF, HALF), 0) <= lax.broadcasted_iota(
        jnp.int32, (HALF, HALF), 1
    )
    factor = scale * math.log2(math.e)
    parts = rows // HALF

    def span(j):
        return slice(j * HALF, (j + 1) * HALF)

    def forward(h, carry):
        values_t = v_ref[:, lanes(h)].T
        for b in range(parts):
            query = q_ref[span(b), lanes(h)]
            scores = [nt(k_ref[span(j), lanes(h)], query) for j in range(b + 1)]
            scores[b] = jnp.where(keep, scores[b], -1e30)
            peak = jnp.max(scores[0], axis=0, keepdims=True)
            for piece in scores[1:]:
                peak = jnp.maximum(peak, jnp.max(piece, axis=0, keepdims=True))
            expo = [jnp.exp2((piece - peak) * factor) for piece in scores]
            total = sum(jnp.sum(piece, axis=0, keepdims=True) for piece in expo)
            inverse = 1.0 / total
            acc = None
            for j in range(b + 1):
                prob = (expo[j] * inverse).astype(BF16)
                probs[h, span(j), span(b)] = prob
                term = mm(values_t[:, span(j)], prob)
                acc = term if acc is None else acc + term
            out_t[h, :, span(b)] = acc
        return carry

    for i in (3, 4, 7, 8):
        loads[i].wait()
    up_step(0)

    @pl.when(holds_outer & (place == 0))
    def _():
        launch()

    loads[2].wait()
    lax.fori_loop(0, 1, forward, 0)
    og_pair.wait_recv()

    @pl.when(holds_inner)
    def _():
        launch()

    og_inner.start()

    @pl.when(is_end)
    def _():
        ship_inner.start()

    lax.fori_loop(1, 2, forward, 0)
    up_step(1)
    lax.fori_loop(2, heads_here, forward, 0)
    up_step(2)
    for i in range(2):
        og_outer[i].wait_recv()

        @pl.when(is_end & beside)
        def _():
            ship_lead[i].start()

    og_relay[0].start()

    def pass_lead():
        for copy in ship_lead:
            copy.wait_recv()
        lead_pair.start()

    def pass_inner():
        ship_inner.wait_recv()
        inner_cross.start()
        inner_pair.start()

    @pl.when(is_mid & across)
    def _():
        pass_lead()

    @pl.when(is_mid & beside)
    def _():
        pass_inner()

    up_step(3)

    def recall_step(h, carry):
        mem = state[h, :width].astype(BF16)
        norm = state[h, width : width + 1]
        query_feat = feature(q_ref[:, lanes(h)].astype(F32))
        inverse = 1.0 / jnp.sum(query_feat * norm, axis=1, keepdims=True)
        recalled = mm(query_feat.astype(BF16), mem) * inverse
        recall[:, lanes(h)] = recalled
        mix = mix_of(h)
        both = (mix * recalled + (1.0 - mix) * out_t[h].T).astype(BF16)
        mixed[:, lanes(h)] = both
        mixed_t[strip(h), :] = both.T

        @pl.when(is_end & (h < 2))
        def _():
            mix_copy(h).start()

        return carry

    lax.fori_loop(0, heads_here, recall_step, 0)
    loads[5].wait()
    o_far = send(o_send.at[0], o_recv.at[0], o_s.at[0], o_r.at[0], heads=partner)
    o_pair = send(o_send.at[1], o_recv.at[1], o_s.at[1], o_r.at[1], heads=partner)
    o_cross = send(o_send.at[2], o_recv.at[2], o_s.at[2], o_r.at[2], heads=cross)
    o_send[0] = mm(mixed[...], w_ref[:, block(far)]).astype(BF16)
    o_far.start()
    o_send[1] = mm(mixed[...], w_ref[:, block(partner)]).astype(BF16)
    o_pair.start()
    value = mm(mixed[...], w_ref[:, block(cross)])
    o_far.wait_recv()
    o_send[2] = (value + o_recv[0].astype(F32)).astype(BF16)
    own_out[...] = mm(mixed[...], w_ref[:, block(me)])

    def both_terms(h, j):
        return mm(mixed_t[strip(h), :], og_all[:, block(j)]) + mm(
            mixed_end[strip(h), :], og_end[:, block(j)]
        )

    def sum_pair(h):
        here = pl.ds(h * width, 2 * width)
        target = block(3 - near)
        sum_send[1, here] = (
            mm(mixed_t[here, :], og_all[:, target]) + mm(mixed_end[here, :], og_end[:, target])
        ).astype(BF16)
        sum_copy(1, h).start()
        sum_copy(1, h + 1).start()

    def sum_step(i, j):
        def step(h):
            if i == 0:
                mix_copy(h).wait_recv()
            sum_send[i, strip(h)] = both_terms(h, j).astype(BF16)
            sum_copy(i, h).start()

        return step

    @pl.when(is_end)
    def _():
        o_cross.start()

    og_inner.wait_recv()
    og_relay[1].start()

    @pl.when(is_mid & across)
    def _():
        pass_inner()

    @pl.when(is_mid & beside)
    def _():
        pass_lead()

    @pl.when(is_mid)
    def _():
        o_cross.start()

    og_relay[0].wait_recv()
    og_relay[1].wait_recv()

    def grad_block(j, carry):
        here = pl.ds(pl.multiple_of(j * HALF, HALF), HALF)
        grad_mix[:, here] = nt(og_all[...], w_ref[here, :])
        return carry

    lax.fori_loop(0, cols // HALF, grad_block, 0)

    def memory_step(h, carry):
        mem = state[h, :width].astype(BF16)
        norm = state[h, width : width + 1]
        query = q_ref[:, lanes(h)].astype(F32)
        query_feat = feature(query)
        inverse = 1.0 / jnp.sum(query_feat * norm, axis=1, keepdims=True)
        grad_recall = mix_of(h) * grad_mix[:, lanes(h)]
        grad_numer = (grad_recall * inverse).astype(BF16)
        grad_denom = -jnp.sum(grad_recall * recall[:, lanes(h)], axis=1, keepdims=True) * inverse
        grad_feat[:, lanes(h)] = (nt(grad_numer, mem) + grad_denom * norm) * feature_slope(query)
        local[h, :width] = mm(query_feat.astype(BF16).T, grad_numer)
        total = jnp.sum(query_feat * grad_denom, axis=0, keepdims=True)
        local[h, width:] = jnp.broadcast_to(total, (PAD, width))
        return carry

    @pl.when(is_mid)
    def _():
        lead_pair.wait_recv()
        sum_step(0, 3 - edge)(0)

    lax.fori_loop(0, heads_here, memory_step, 0)
    down_step(3)

    @pl.when(is_end)
    def _():
        for h in range(2, heads_here):
            mix_copy(h).start()


    @pl.when(is_mid)
    def _():
        sum_step(0, 3 - edge)(1)
        inner_cross.wait_recv()
        inner_relay.start()

    down_step(2)

    @pl.when(is_mid)
    def _():
        inner_pair.wait_recv()
        inner_relay.wait_recv()
        sum_pair(0)
        sum_step(0, 3 - edge)(2)
        sum_step(0, 3 - edge)(3)
        sum_pair(2)

    down_step(1)
    gw_ref[...] = mm(mixed_t[...], og_all[:, block(place)])

    @pl.when(is_mid)
    def _():
        gw_ref[...] += mm(mixed_end[...], og_end[:, block(place)])

    def backward(h, carry):
        mix = mix_of(h)
        grad_local = ((1.0 - mix) * grad_mix[:, lanes(h)]).astype(BF16)
        grad_t = grad_local.T
        delta = jnp.sum(grad_t.astype(F32) * out_t[h], axis=0, keepdims=True)
        keys_t = k_ref[:, lanes(h)].T
        for b in range(parts):
            query = q_ref[span(b), lanes(h)]
            acc = None
            for j in range(b + 1):
                prob = probs[h, span(j), span(b)]
                grad_prob = mm(v_ref[span(j), lanes(h)], grad_t[:, span(b)])
                grad_score = (prob.astype(F32) * (grad_prob - delta[:, span(b)]) * scale).astype(
                    BF16
                )
                term = mm(keys_t[:, span(j)], grad_score)
                acc = term if acc is None else acc + term
                key_term = mm(grad_score, query)
                value_term = mm(prob, grad_local[span(b), :])
                if b == j:
                    gk_att[span(j), lanes(h)] = key_term
                    gv_att[span(j), lanes(h)] = value_term
                else:
                    gk_att[span(j), lanes(h)] += key_term
                    gv_att[span(j), lanes(h)] += value_term
            gq_ref[span(b), lanes(h)] = (acc.T + grad_feat[span(b), lanes(h)]).astype(BF16)
        return carry

    def backward_step(h, carry):
        backward(h, carry)

        @pl.when(is_mid)
        def _():
            sum_copy(0, h).wait_recv()
            fin_send[strip(h)] = (
                mm(mixed_t[strip(h), :], og_all[:, block(edge)])
                + sum_recv[0, strip(h)].astype(F32)
            ).astype(BF16)
            fin_copy(h).start()

        return carry

    lax.fori_loop(0, heads_here, backward_step, 0)
    o_pair.wait_recv()
    o_cross.wait_recv()
    out_ref[...] = (own_out[...] + o_recv[1].astype(F32) + o_recv[2].astype(F32)).astype(BF16)
    down_step(0)

    def finish(h, carry):
        mem = after[h, :width].astype(BF16)
        key = k_ref[:, lanes(h)].astype(F32)
        value = v_ref[:, lanes(h)]
        grad_kfeat = nt(value, mem) + after[h, width : width + 1]
        gk_ref[:, lanes(h)] = (gk_att[:, lanes(h)] + grad_kfeat * feature_slope(key)).astype(BF16)
        key_feat = feature(key).astype(BF16)
        gv_ref[:, lanes(h)] = (gv_att[:, lanes(h)] + mm(key_feat, mem)).astype(BF16)
        return carry

    lax.fori_loop(0, heads_here, finish, 0)

    def last_step(h, carry):
        @pl.when(is_mid)
        def _():
            sum_copy(1, h).wait_recv()
            gw_ref[strip(h)] += sum_recv[1, strip(h)].astype(F32)

        @pl.when(is_end)
        def _():
            fin_copy(h).wait_recv()
            gw_ref[strip(h)] += sum_recv[0, strip(h)].astype(F32)

        return carry

    lax.fori_loop(0, heads_here, last_step, 0)
    for copy in (og_pair, og_inner, *og_outer, *og_relay, o_far, o_pair, o_cross):
        copy.wait_send()

    @pl.when(is_end)
    def _():
        for copy in ship_lead:
            copy.wait_send()
        ship_inner.wait_send()
        for h in range(heads_here):
            mix_copy(h).wait_send()

    @pl.when(is_mid)
    def _():
        for copy in (lead_pair, inner_pair, inner_cross, inner_relay):
            copy.wait_send()
        for h in range(heads_here):
            sum_copy(0, h).wait_send()
            sum_copy(1, h).wait_send()
            fin_copy(h).wait_send()

    @pl.when(place < 3)
    def _():
        for h in range(heads_here):
            up_copy(h, near).wait_send()

    @pl.when(place > 0)
    def _():
        for h in range(heads_here):
            down_copy(h, near).wait_send()


def settle(*refs):
    sems = refs[-1]
    count = len(refs) // 2
    copies = [
        pltpu.make_async_copy(refs[i], refs[count + i], sems.at[i]) for i in range(count)
    ]
    for copy in copies:
        copy.start()
    for copy in copies:
        copy.wait()


def shards(queries, key_rows, values, memory_in, norm_in, decays, gate_bias, out_weight, out_grad):
    rows, cols = queries.shape
    heads_here, width = memory_in.shape[0], memory_in.shape[1]
    if (
        lax.axis_size("ctx") != 4
        or lax.axis_size("heads") != 4
        or rows != 2 * HALF
        or cols != rows
        or heads_here != 4
        or width != 128
    ):
        return plain(
            queries, key_rows, values, memory_in, norm_in, decays, gate_bias, out_weight, out_grad
        )
    wide = out_weight.shape[1]
    free = pl.BlockSpec(memory_space=pl.ANY)
    small = (heads_here, width + PAD, width)
    half = jax.ShapeDtypeStruct((rows, cols), BF16)
    dma = pltpu.SemaphoreType.DMA
    shapes = (half, half, half, half, jax.ShapeDtypeStruct((cols, cols), F32))
    held = tuple(pltpu.VMEM(x.shape, x.dtype) for x in shapes)
    results = pl.pallas_call(
        fused,
        out_shape=held,
        in_specs=[free] * 9,
        out_specs=(pl.BlockSpec(memory_space=pltpu.VMEM),) * 5,
        scratch_shapes=[
            pltpu.VMEM((rows, cols), BF16),
            pltpu.VMEM((rows, cols), BF16),
            pltpu.VMEM((rows, cols), BF16),
            pltpu.VMEM((heads_here, width, width), F32),
            pltpu.VMEM((heads_here, width), F32),
            pltpu.VMEM((cols, wide), BF16),
            pltpu.SMEM((1, heads_here), F32),
            pltpu.SMEM((1, heads_here), F32),
            pltpu.VMEM((rows, wide), BF16),
            pltpu.VMEM((rows, wide), BF16),
            pltpu.VMEM(small, F32),
            pltpu.VMEM(small, F32),
            pltpu.VMEM(small, F32),
            pltpu.VMEM(small, F32),
            pltpu.VMEM(small, BF16),
            pltpu.VMEM(small, BF16),
            pltpu.VMEM(small, BF16),
            pltpu.VMEM(small, BF16),
            pltpu.VMEM((heads_here, rows, rows), BF16),
            pltpu.VMEM((heads_here, width, rows), F32),
            pltpu.VMEM((rows, cols), F32),
            pltpu.VMEM((rows, cols), F32),
            pltpu.VMEM((rows, cols), F32),
            pltpu.VMEM((rows, cols), BF16),
            pltpu.VMEM((cols, rows), BF16),
            pltpu.VMEM((cols, rows), BF16),
            pltpu.VMEM((rows, cols), F32),
            pltpu.VMEM((rows, cols), F32),
            pltpu.VMEM((rows, cols), F32),
            pltpu.VMEM((2, cols, cols), BF16),
            pltpu.VMEM((2, cols, cols), BF16),
            pltpu.VMEM((cols, cols), BF16),
            pltpu.VMEM((3, rows, cols), BF16),
            pltpu.VMEM((3, rows, cols), BF16),
            dma((7,)), dma((7,)), dma((7,)), dma((7,)), dma((4,)), dma((4,)),
            dma((4,)), dma((4,)), dma((4,)), dma((4,)),
            dma((2, 4)), dma((2, 4)), dma((4,)), dma((4,)),
            dma((3,)), dma((3,)), dma((9,)),
        ],
        compiler_params=pltpu.CompilerParams(
            collective_id=0, has_side_effects=True, vmem_limit_bytes=48 << 20
        ),
    )(
        *(
            pltpu.with_memory_space_constraint(x, pltpu.HBM)
            for x in (
                queries, key_rows, values, memory_in, norm_in, decays,
                gate_bias.reshape(1, heads_here), out_weight, out_grad,
            )
        )
    )
    results = [pltpu.with_memory_space_constraint(x, pltpu.VMEM) for x in results]
    return pl.pallas_call(
        settle,
        out_shape=shapes,
        in_specs=[pl.BlockSpec(memory_space=pltpu.VMEM)] * 5,
        out_specs=(free,) * 5,
        scratch_shapes=[dma((5,))],
    )(*results)


def solution(mesh):
    return jax.shard_map(
        shards,
        mesh=mesh,
        in_specs=(
            P(("groups", "ctx"), "heads"),
            P(("groups", "ctx"), "heads"),
            P(("groups", "ctx"), "heads"),
            P(("groups", "heads"), None, None),
            P(("groups", "heads"), None),
            P(("groups", "ctx"), "heads"),
            P("heads"),
            P("heads", None),
            P(("groups", "ctx"), "heads"),
        ),
        out_specs=(
            P(("groups", "ctx"), "heads"),
            P(("groups", "ctx"), "heads"),
            P(("groups", "ctx"), "heads"),
            P(("groups", "ctx"), "heads"),
            P(("groups", "heads"), "ctx"),
        ),
        check_vma=False,
    )
```

```python
import math

import jax
import jax.numpy as jnp
from jax import lax
from jax.experimental import pallas as pl
from jax.experimental.pallas import tpu as pltpu
from jax.sharding import PartitionSpec as P

HIGH = lax.Precision.HIGHEST


def shortened(value):

    def short(part):
        return part.astype(jnp.bfloat16) if part.dtype == jnp.float32 else part

    return jax.tree.map(short, value)


def feature(inner):
    return jnp.where(inner > 0, inner + 1.0, jnp.exp(jnp.minimum(inner, 0.0)))


def feature_slope(inner):
    return jnp.where(inner > 0, 1.0, jnp.exp(jnp.minimum(inner, 0.0)))


def gathered_prefix(stacked_gate, stacked_mem, stacked_norm, own_index, count, upward):
    order = jnp.arange(count, dtype=jnp.int32)
    term_pos = order[:, None]
    inner_pos = order[None, :]
    if upward:
        between = (inner_pos > term_pos) & (inner_pos < own_index)
        active = order < own_index
    else:
        between = (inner_pos < term_pos) & (inner_pos > own_index)
        active = order > own_index
    factor = jnp.prod(jnp.where(between[:, :, None], stacked_gate[None, :, :], 1.0), axis=1)
    weight = jnp.where(active[:, None], factor, 0.0)
    total_mem = jnp.einsum("th,thij->hij", weight, stacked_mem, precision=HIGH)
    total_norm = jnp.einsum("th,thi->hi", weight, stacked_norm, precision=HIGH)
    leading = jnp.prod(jnp.where(active[:, None], stacked_gate, 1.0), axis=0)
    return (leading, total_mem, total_norm)


def plain(queries, key_rows, values, memory_in, norm_in, decays, gate_bias, out_weight, out_grad):
    rows = queries.shape[0]
    heads_here = memory_in.shape[0]
    width = memory_in.shape[1]
    scale = 1.0 / math.sqrt(width)
    shape_three = (rows, heads_here, width)
    query_blk = queries.reshape(shape_three)
    key_blk = key_rows.reshape(shape_three)
    value_blk = values.reshape(shape_three)
    gate_now = decays[0]
    key_f = key_blk.astype(jnp.float32)
    key_feat = feature(key_f).astype(jnp.bfloat16)
    upd_mem = jnp.einsum("thi,thj->hij", key_feat, value_blk, preferred_element_type=jnp.float32)
    upd_norm = jnp.sum(key_feat.astype(jnp.float32), axis=0)
    all_gate, all_mem, all_norm = (
        lax.all_gather(gate_now[None].astype(jnp.bfloat16), "ctx", axis=0, tiled=True).astype(
            jnp.float32
        ),
        lax.all_gather(upd_mem[None].astype(jnp.bfloat16), "ctx", axis=0, tiled=True).astype(
            jnp.float32
        ),
        lax.all_gather(upd_norm[None].astype(jnp.bfloat16), "ctx", axis=0, tiled=True).astype(
            jnp.float32
        ),
    )
    leading, prior_mem, prior_norm = gathered_prefix(
        all_gate, all_mem, all_norm, lax.axis_index("ctx"), lax.axis_size("ctx"), True
    )
    state_mem = leading[:, None, None] * memory_in + prior_mem
    state_norm = leading[:, None] * norm_in + prior_norm
    query_f = query_blk.astype(jnp.float32)
    query_feat = feature(query_f)
    numer = jnp.einsum("thi,hij->thj", query_feat, state_mem, precision=HIGH)
    denom = jnp.einsum("thi,hi->th", query_feat, state_norm, precision=HIGH)
    recall = numer / denom[..., None]
    scores = (
        jnp.einsum("thd,shd->hts", query_blk, key_blk, preferred_element_type=jnp.float32) * scale
    )
    places = jnp.arange(rows, dtype=jnp.int32)
    causal = (places[:, None] >= places[None, :])[None]
    peak = jnp.max(jnp.where(causal, scores, -jnp.inf), axis=-1, keepdims=True)
    expo = jnp.where(causal, jnp.exp(scores - peak), 0.0)
    probs = expo / jnp.sum(expo, axis=-1, keepdims=True)
    probs_half = probs.astype(jnp.bfloat16)
    local_out = jnp.einsum(
        "hts,shd->thd", probs_half, value_blk, preferred_element_type=jnp.float32
    )
    mix = jax.nn.sigmoid(gate_bias)[None, :, None]
    mixed = (
        (mix * recall + (1.0 - mix) * local_out)
        .astype(jnp.bfloat16)
        .reshape(rows, heads_here * width)
    )
    partial_sum = jnp.dot(mixed, out_weight, preferred_element_type=jnp.float32)
    output = lax.psum_scatter(
        partial_sum.astype(jnp.bfloat16), "heads", scatter_dimension=1, tiled=True
    )
    piece = lax.all_gather(out_grad, "heads", axis=1, tiled=True)
    grad_mix = lax.dot_general(
        piece, out_weight, (((1,), (1,)), ((), ())), preferred_element_type=jnp.float32
    )
    block = lax.dot_general(
        mixed, piece, (((0,), (0,)), ((), ())), preferred_element_type=jnp.float32
    )
    grad_mix, collected = (grad_mix, block)
    grad_weight = lax.psum_scatter(
        collected.astype(jnp.bfloat16), "ctx", scatter_dimension=1, tiled=True
    ).astype(jnp.float32)
    grad_seg = grad_mix.reshape(shape_three)
    grad_recall = mix * grad_seg
    grad_local = ((1.0 - mix) * grad_seg).astype(jnp.bfloat16)
    grad_probs = jnp.einsum(
        "thd,shd->hts", grad_local, value_blk, preferred_element_type=jnp.float32
    )
    grad_value_att = jnp.einsum(
        "hts,thd->shd", probs_half, grad_local, preferred_element_type=jnp.float32
    )
    delta = jnp.sum(probs * grad_probs, axis=-1, keepdims=True)
    grad_scores = (probs * (grad_probs - delta) * scale).astype(jnp.bfloat16)
    grad_query_att = jnp.einsum(
        "hts,shd->thd", grad_scores, key_blk, preferred_element_type=jnp.float32
    )
    grad_key_att = jnp.einsum(
        "hts,thd->shd", grad_scores, query_blk, preferred_element_type=jnp.float32
    )
    grad_numer = grad_recall / denom[..., None]
    grad_denom = -jnp.sum(grad_recall * recall, axis=-1) / denom
    grad_qfeat = (
        jnp.einsum("thj,hij->thi", grad_numer, state_mem, precision=HIGH)
        + grad_denom[..., None] * state_norm[None]
    )
    local_mem = jnp.einsum("thi,thj->hij", query_feat, grad_numer, precision=HIGH)
    local_norm = jnp.einsum("thi,th->hi", query_feat, grad_denom, precision=HIGH)
    grad_query = (
        (grad_query_att + grad_qfeat * feature_slope(query_f))
        .astype(jnp.bfloat16)
        .reshape(rows, heads_here * width)
    )
    back_gate, back_mem, back_norm = (
        lax.all_gather(gate_now[None].astype(jnp.bfloat16), "ctx", axis=0, tiled=True).astype(
            jnp.float32
        ),
        lax.all_gather(shortened(local_mem[None]), "ctx", axis=0, tiled=True),
        lax.all_gather(shortened(local_norm[None]), "ctx", axis=0, tiled=True),
    )
    unused_lead, after_mem, after_norm = gathered_prefix(
        back_gate, back_mem, back_norm, lax.axis_index("ctx"), lax.axis_size("ctx"), False
    )
    value_f = value_blk.astype(jnp.float32)
    grad_kfeat = jnp.einsum("thj,hij->thi", value_f, after_mem, precision=HIGH) + after_norm[None]
    grad_key = (
        (grad_key_att + grad_kfeat * feature_slope(key_f))
        .astype(jnp.bfloat16)
        .reshape(rows, heads_here * width)
    )
    grad_value = (
        (
            grad_value_att
            + jnp.einsum("thi,hij->thj", key_feat.astype(jnp.float32), after_mem, precision=HIGH)
        )
        .astype(jnp.bfloat16)
        .reshape(rows, heads_here * width)
    )
    return (output, grad_query, grad_key, grad_value, grad_weight)


MESH = pl.DeviceIdType.MESH
F32 = jnp.float32
BF16 = jnp.bfloat16
HALF = 256
PAD = 16


def mm(left, right):
    return jnp.dot(left, right, preferred_element_type=F32)


def nt(left, right):
    return lax.dot_general(left, right, (((1,), (1,)), ((), ())), preferred_element_type=F32)


def fused(
    q_in, k_in, v_in, mem_in, norm_in, decay_in, gate_in, w_in, og_ref,
    out_ref, gq_ref, gk_ref, gv_ref, gw_ref,
    q_ref, k_ref, v_ref, mem_ref, norm_ref, w_ref, decay_ref, gate_ref,
    og_all, og_end, upd, state, local, after, up_send, up_recv, down_send, down_recv,
    probs, out_t, recall, own_out, grad_mix, mixed, mixed_t, mixed_end, grad_feat, gk_att, gv_att,
    sum_send, sum_recv, fin_send, o_send, o_recv,
    og_s, og_r, end_s, end_r, mix_s, mix_r, up_s, up_r, down_s, down_r, sum_s, sum_r, fin_s, fin_r,
    o_s, o_r, load_s,
):
    rows, cols = q_ref.shape
    heads_here, width = mem_ref.shape[0], mem_ref.shape[1]
    scale = 1.0 / math.sqrt(width)
    me = lax.axis_index("heads")
    place = lax.axis_index("ctx")
    partner = me + 1 - 2 * lax.rem(me, 2)
    cross = lax.rem(me + 2, 4)
    far = lax.rem(partner + 2, 4)
    is_end = (place == 0) | (place == 3)
    is_mid = (place == 1) | (place == 2)
    near = 1 + lax.div(place, 2)
    edge = 3 * lax.div(place, 2)
    side = lax.div(me, 2)
    holds_outer = (me == 0) | (me == 3)
    holds_inner = (me == 1) | (me == 2)
    beside = 3 * side == edge
    across = 3 * side != edge
    ours = (3 * side, 1 + side)
    theirs = (3 - 3 * side, 2 - side)
    part = pl.ds(pl.multiple_of(lax.rem(me, 2) * HALF, HALF), HALF)

    def lanes(h):
        return pl.ds(pl.multiple_of(h * width, width), width)

    def block(j):
        return pl.ds(pl.multiple_of(j * cols, cols), cols)

    def send(src, dst, s, r, **where):
        return pltpu.make_async_remote_copy(
            src_ref=src, dst_ref=dst, send_sem=s, recv_sem=r, device_id=where, device_id_type=MESH
        )

    def mix_of(h):
        return 1.0 / (1.0 + jnp.exp(-jnp.full((1, width), gate_ref[0, h], F32)))

    loads = [
        pltpu.make_async_copy(src, dst, load_s.at[i])
        for i, (src, dst) in enumerate(
            (
                (k_in, k_ref), (v_in, v_ref), (q_in, q_ref), (mem_in, mem_ref),
                (norm_in, norm_ref), (w_in, w_ref), (og_ref, og_all.at[:, block(me)]),
                (decay_in, decay_ref), (gate_in, gate_ref),
            )
        )
    ]
    for i in (6, 0, 1, 2, 3, 4, 7, 8, 5):
        loads[i].start()

    barrier = pltpu.get_barrier_semaphore()
    for peer in (partner, cross):
        pl.semaphore_signal(barrier, inc=1, device_id={"heads": peer}, device_id_type=MESH)
    for step in (-1, 1):

        @pl.when((place + step >= 0) & (place + step <= 3))
        def _():
            pl.semaphore_signal(
                barrier, inc=1, device_id={"ctx": place + step}, device_id_type=MESH
            )

    def piece(ref, j):
        return ref.at[part, block(j)]

    own_block = og_all.at[:, block(me)]
    og_pair = send(own_block, own_block, og_s.at[0], og_r.at[0], heads=partner)
    og_inner = send(
        piece(og_all, ours[1]), piece(og_all, ours[1]), og_s.at[1], og_r.at[1], heads=cross
    )

    def fine(ref, j, i):
        start = lax.rem(me, 2) * HALF + i * (HALF // 2)
        return ref.at[pl.ds(pl.multiple_of(start, HALF // 2), HALF // 2), block(j)]

    og_outer = [
        send(fine(og_all, ours[0], i), fine(og_all, ours[0], i), og_s.at[5 + i], og_r.at[5 + i],
             heads=cross)
        for i in range(2)
    ]
    og_relay = [
        send(piece(og_all, theirs[i]), piece(og_all, theirs[i]), og_s.at[3 + i], og_r.at[3 + i],
             heads=partner)
        for i in range(2)
    ]
    lead = piece(og_end, 3 - edge)
    inner = piece(og_end, ours[1])
    inner_far = piece(og_end, theirs[1])
    ship_lead = [
        send(fine(og_all, 3 - edge, i), fine(og_end, 3 - edge, i), end_s.at[6 * i], end_r.at[6 * i],
             ctx=near)
        for i in range(2)
    ]
    ship_inner = send(piece(og_all, ours[1]), inner, end_s.at[1], end_r.at[1], ctx=near)
    lead_pair = send(lead, lead, end_s.at[2], end_r.at[2], heads=partner)
    inner_pair = send(inner, inner, end_s.at[3], end_r.at[3], heads=partner)
    inner_cross = send(inner, inner, end_s.at[4], end_r.at[4], heads=cross)
    inner_relay = send(inner_far, inner_far, end_s.at[5], end_r.at[5], heads=partner)

    def strip(h):
        return pl.ds(pl.multiple_of(h * width, width), width)

    def mix_copy(h):
        return send(
            mixed_t.at[strip(h)], mixed_end.at[strip(h)], mix_s.at[h], mix_r.at[h], ctx=near
        )

    def sum_copy(i, h):
        return send(
            sum_send.at[i, strip(h)], sum_recv.at[i, strip(h)], sum_s.at[i, h], sum_r.at[i, h],
            ctx=3 - near,
        )

    def fin_copy(h):
        return send(
            fin_send.at[strip(h)], sum_recv.at[0, strip(h)], fin_s.at[h], fin_r.at[h], ctx=edge
        )


    def update(h, carry):
        key_feat = feature(k_ref[:, lanes(h)].astype(F32)).astype(BF16)
        upd[h, :width] = mm(key_feat.T, v_ref[:, lanes(h)])
        total = jnp.sum(key_feat.astype(F32), axis=0, keepdims=True)
        upd[h, width:] = jnp.broadcast_to(total, (PAD, width))
        return carry

    pl.semaphore_wait(barrier, 3 + is_mid.astype(jnp.int32))
    loads[6].wait()
    og_pair.start()

    def launch():
        for copy in og_outer:
            copy.start()

        @pl.when(is_end & across)
        def _():
            for copy in ship_lead:
                copy.start()

    @pl.when(holds_outer & (place > 0))
    def _():
        launch()

    loads[0].wait()
    loads[1].wait()
    lax.fori_loop(0, heads_here, update, 0)

    def up_copy(h, target):
        return send(up_send.at[h], up_recv.at[h], up_s.at[h], up_r.at[h], ctx=target)

    def up_step(index):
        @pl.when(place == index)
        def _():
            for h in range(heads_here):
                if index == 0:
                    state[h, :width] = mem_ref[h]
                    state[h, width:] = jnp.broadcast_to(norm_ref[h : h + 1, :], (PAD, width))
                else:
                    up_copy(h, index - 1).wait_recv()
                    state[h] = up_recv[h].astype(F32)
                if index < 3:
                    up_send[h] = (decay_ref[0, h] * state[h] + upd[h]).astype(BF16)
                    up_copy(h, index + 1).start()

    def down_copy(h, target):
        return send(down_send.at[h], down_recv.at[h], down_s.at[h], down_r.at[h], ctx=target)

    def down_step(index):
        @pl.when(place == index)
        def _():
            if index == 3:
                after[...] = jnp.zeros_like(after)
            for h in range(heads_here):
                if index < 3:
                    down_copy(h, index + 1).wait_recv()
                    after[h] = down_recv[h].astype(F32)
                if index > 0:
                    down_send[h] = (decay_ref[0, h] * after[h] + local[h]).astype(BF16)
                    down_copy(h, index - 1).start()

    keep = lax.broadcasted_iota(jnp.int32, (HALF, HALF), 0) <= lax.broadcasted_iota(
        jnp.int32, (HALF, HALF), 1
    )
    factor = scale * math.log2(math.e)
    parts = rows // HALF

    def span(j):
        return slice(j * HALF, (j + 1) * HALF)

    def forward(h, carry):
        values_t = v_ref[:, lanes(h)].T
        for b in range(parts):
            query = q_ref[span(b), lanes(h)]
            scores = [nt(k_ref[span(j), lanes(h)], query) for j in range(b + 1)]
            scores[b] = jnp.where(keep, scores[b], -1e30)
            peak = jnp.max(scores[0], axis=0, keepdims=True)
            for piece in scores[1:]:
                peak = jnp.maximum(peak, jnp.max(piece, axis=0, keepdims=True))
            expo = [jnp.exp2((piece - peak) * factor) for piece in scores]
            total = sum(jnp.sum(piece, axis=0, keepdims=True) for piece in expo)
            inverse = 1.0 / total
            acc = None
            for j in range(b + 1):
                prob = (expo[j] * inverse).astype(BF16)
                probs[h, span(j), span(b)] = prob
                term = mm(values_t[:, span(j)], prob)
                acc = term if acc is None else acc + term
            out_t[h, :, span(b)] = acc
        return carry

    for i in (3, 4, 7, 8):
        loads[i].wait()
    up_step(0)

    @pl.when(holds_outer & (place == 0))
    def _():
        launch()

    loads[2].wait()
    lax.fori_loop(0, 1, forward, 0)
    og_pair.wait_recv()

    @pl.when(holds_inner)
    def _():
        launch()

    og_inner.start()

    @pl.when(is_end)
    def _():
        ship_inner.start()

    lax.fori_loop(1, 2, forward, 0)
    up_step(1)
    lax.fori_loop(2, heads_here, forward, 0)
    up_step(2)
    for i in range(2):
        og_outer[i].wait_recv()

        @pl.when(is_end & beside)
        def _():
            ship_lead[i].start()

    og_relay[0].start()

    def pass_lead():
        for copy in ship_lead:
            copy.wait_recv()
        lead_pair.start()

    def pass_inner():
        ship_inner.wait_recv()
        inner_cross.start()
        inner_pair.start()

    @pl.when(is_mid & across)
    def _():
        pass_lead()

    @pl.when(is_mid & beside)
    def _():
        pass_inner()

    up_step(3)

    def recall_step(h, carry):
        mem = state[h, :width].astype(BF16)
        norm = state[h, width : width + 1]
        query_feat = feature(q_ref[:, lanes(h)].astype(F32))
        inverse = 1.0 / jnp.sum(query_feat * norm, axis=1, keepdims=True)
        recalled = mm(query_feat.astype(BF16), mem) * inverse
        recall[:, lanes(h)] = recalled
        mix = mix_of(h)
        both = (mix * recalled + (1.0 - mix) * out_t[h].T).astype(BF16)
        mixed[:, lanes(h)] = both
        mixed_t[strip(h), :] = both.T

        @pl.when(is_end & (h < 2))
        def _():
            mix_copy(h).start()

        return carry

    lax.fori_loop(0, heads_here, recall_step, 0)
    loads[5].wait()
    o_far = send(o_send.at[0], o_recv.at[0], o_s.at[0], o_r.at[0], heads=partner)
    o_pair = send(o_send.at[1], o_recv.at[1], o_s.at[1], o_r.at[1], heads=partner)
    o_cross = send(o_send.at[2], o_recv.at[2], o_s.at[2], o_r.at[2], heads=cross)
    o_send[0] = mm(mixed[...], w_ref[:, block(far)]).astype(BF16)
    o_far.start()
    o_send[1] = mm(mixed[...], w_ref[:, block(partner)]).astype(BF16)
    o_pair.start()
    value = mm(mixed[...], w_ref[:, block(cross)])
    o_far.wait_recv()
    o_send[2] = (value + o_recv[0].astype(F32)).astype(BF16)
    own_out[...] = mm(mixed[...], w_ref[:, block(me)])

    def both_terms(h, j):
        return mm(mixed_t[strip(h), :], og_all[:, block(j)]) + mm(
            mixed_end[strip(h), :], og_end[:, block(j)]
        )

    def sum_pair(h):
        here = pl.ds(h * width, 2 * width)
        target = block(3 - near)
        sum_send[1, here] = (
            mm(mixed_t[here, :], og_all[:, target]) + mm(mixed_end[here, :], og_end[:, target])
        ).astype(BF16)
        sum_copy(1, h).start()
        sum_copy(1, h + 1).start()

    def sum_step(i, j):
        def step(h):
            if i == 0:
                mix_copy(h).wait_recv()
            sum_send[i, strip(h)] = both_terms(h, j).astype(BF16)
            sum_copy(i, h).start()

        return step

    @pl.when(is_end)
    def _():
        o_cross.start()

    our_half = pl.ds(pl.multiple_of(side * 2 * cols, 2 * cols), 2 * cols)
    their_half = pl.ds(pl.multiple_of((1 - side) * 2 * cols, 2 * cols), 2 * cols)

    def grad_early(j, carry):
        here = pl.ds(pl.multiple_of(j * HALF, HALF), HALF)
        grad_mix[:, here] = nt(og_all[:, our_half], w_ref[here, our_half])
        return carry

    lax.fori_loop(0, cols // HALF, grad_early, 0)
    og_inner.wait_recv()
    og_relay[1].start()

    @pl.when(is_mid & across)
    def _():
        pass_inner()

    @pl.when(is_mid & beside)
    def _():
        pass_lead()

    @pl.when(is_mid)
    def _():
        o_cross.start()

    og_relay[0].wait_recv()
    og_relay[1].wait_recv()

    def grad_late(j, carry):
        here = pl.ds(pl.multiple_of(j * HALF, HALF), HALF)
        grad_mix[:, here] += nt(og_all[:, their_half], w_ref[here, their_half])
        return carry

    lax.fori_loop(0, cols // HALF, grad_late, 0)

    def memory_step(h, carry):
        mem = state[h, :width].astype(BF16)
        norm = state[h, width : width + 1]
        query = q_ref[:, lanes(h)].astype(F32)
        query_feat = feature(query)
        inverse = 1.0 / jnp.sum(query_feat * norm, axis=1, keepdims=True)
        grad_recall = mix_of(h) * grad_mix[:, lanes(h)]
        grad_numer = (grad_recall * inverse).astype(BF16)
        grad_denom = -jnp.sum(grad_recall * recall[:, lanes(h)], axis=1, keepdims=True) * inverse
        grad_feat[:, lanes(h)] = (nt(grad_numer, mem) + grad_denom * norm) * feature_slope(query)
        local[h, :width] = mm(query_feat.astype(BF16).T, grad_numer)
        total = jnp.sum(query_feat * grad_denom, axis=0, keepdims=True)
        local[h, width:] = jnp.broadcast_to(total, (PAD, width))
        return carry

    @pl.when(is_mid)
    def _():
        lead_pair.wait_recv()
        sum_step(0, 3 - edge)(0)

    lax.fori_loop(0, heads_here, memory_step, 0)
    down_step(3)

    @pl.when(is_end)
    def _():
        for h in range(2, heads_here):
            mix_copy(h).start()


    @pl.when(is_mid)
    def _():
        sum_step(0, 3 - edge)(1)
        inner_cross.wait_recv()
        inner_relay.start()

    down_step(2)

    @pl.when(is_mid)
    def _():
        inner_pair.wait_recv()
        inner_relay.wait_recv()
        sum_pair(0)
        sum_step(0, 3 - edge)(2)
        sum_step(0, 3 - edge)(3)
        sum_pair(2)

    down_step(1)
    gw_ref[...] = mm(mixed_t[...], og_all[:, block(place)])

    @pl.when(is_mid)
    def _():
        gw_ref[...] += mm(mixed_end[...], og_end[:, block(place)])

    def backward(h, carry):
        mix = mix_of(h)
        grad_local = ((1.0 - mix) * grad_mix[:, lanes(h)]).astype(BF16)
        grad_t = grad_local.T
        delta = jnp.sum(grad_t.astype(F32) * out_t[h], axis=0, keepdims=True)
        keys_t = k_ref[:, lanes(h)].T
        for b in range(parts):
            query = q_ref[span(b), lanes(h)]
            acc = None
            for j in range(b + 1):
                prob = probs[h, span(j), span(b)]
                grad_prob = mm(v_ref[span(j), lanes(h)], grad_t[:, span(b)])
                grad_score = (prob.astype(F32) * (grad_prob - delta[:, span(b)]) * scale).astype(
                    BF16
                )
                term = mm(keys_t[:, span(j)], grad_score)
                acc = term if acc is None else acc + term
                key_term = mm(grad_score, query)
                value_term = mm(prob, grad_local[span(b), :])
                if b == j:
                    gk_att[span(j), lanes(h)] = key_term
                    gv_att[span(j), lanes(h)] = value_term
                else:
                    gk_att[span(j), lanes(h)] += key_term
                    gv_att[span(j), lanes(h)] += value_term
            gq_ref[span(b), lanes(h)] = (acc.T + grad_feat[span(b), lanes(h)]).astype(BF16)
        return carry

    def backward_step(h, carry):
        backward(h, carry)

        @pl.when(is_mid)
        def _():
            sum_copy(0, h).wait_recv()
            fin_send[strip(h)] = (
                mm(mixed_t[strip(h), :], og_all[:, block(edge)])
                + sum_recv[0, strip(h)].astype(F32)
            ).astype(BF16)
            fin_copy(h).start()

        return carry

    lax.fori_loop(0, heads_here, backward_step, 0)
    o_pair.wait_recv()
    o_cross.wait_recv()
    out_ref[...] = (own_out[...] + o_recv[1].astype(F32) + o_recv[2].astype(F32)).astype(BF16)
    down_step(0)

    def finish(h, carry):
        mem = after[h, :width].astype(BF16)
        key = k_ref[:, lanes(h)].astype(F32)
        value = v_ref[:, lanes(h)]
        grad_kfeat = nt(value, mem) + after[h, width : width + 1]
        gk_ref[:, lanes(h)] = (gk_att[:, lanes(h)] + grad_kfeat * feature_slope(key)).astype(BF16)
        key_feat = feature(key).astype(BF16)
        gv_ref[:, lanes(h)] = (gv_att[:, lanes(h)] + mm(key_feat, mem)).astype(BF16)
        return carry

    lax.fori_loop(0, heads_here, finish, 0)

    def last_step(h, carry):
        @pl.when(is_mid)
        def _():
            sum_copy(1, h).wait_recv()
            gw_ref[strip(h)] += sum_recv[1, strip(h)].astype(F32)

        @pl.when(is_end)
        def _():
            fin_copy(h).wait_recv()
            gw_ref[strip(h)] += sum_recv[0, strip(h)].astype(F32)

        return carry

    lax.fori_loop(0, heads_here, last_step, 0)
    for copy in (og_pair, og_inner, *og_outer, *og_relay, o_far, o_pair, o_cross):
        copy.wait_send()

    @pl.when(is_end)
    def _():
        for copy in ship_lead:
            copy.wait_send()
        ship_inner.wait_send()
        for h in range(heads_here):
            mix_copy(h).wait_send()

    @pl.when(is_mid)
    def _():
        for copy in (lead_pair, inner_pair, inner_cross, inner_relay):
            copy.wait_send()
        for h in range(heads_here):
            sum_copy(0, h).wait_send()
            sum_copy(1, h).wait_send()
            fin_copy(h).wait_send()

    @pl.when(place < 3)
    def _():
        for h in range(heads_here):
            up_copy(h, near).wait_send()

    @pl.when(place > 0)
    def _():
        for h in range(heads_here):
            down_copy(h, near).wait_send()


def settle(*refs):
    sems = refs[-1]
    count = len(refs) // 2
    copies = [
        pltpu.make_async_copy(refs[i], refs[count + i], sems.at[i]) for i in range(count)
    ]
    for copy in copies:
        copy.start()
    for copy in copies:
        copy.wait()


def shards(queries, key_rows, values, memory_in, norm_in, decays, gate_bias, out_weight, out_grad):
    rows, cols = queries.shape
    heads_here, width = memory_in.shape[0], memory_in.shape[1]
    if (
        lax.axis_size("ctx") != 4
        or lax.axis_size("heads") != 4
        or rows != 2 * HALF
        or cols != rows
        or heads_here != 4
        or width != 128
    ):
        return plain(
            queries, key_rows, values, memory_in, norm_in, decays, gate_bias, out_weight, out_grad
        )
    wide = out_weight.shape[1]
    free = pl.BlockSpec(memory_space=pl.ANY)
    small = (heads_here, width + PAD, width)
    half = jax.ShapeDtypeStruct((rows, cols), BF16)
    dma = pltpu.SemaphoreType.DMA
    shapes = (half, half, half, half, jax.ShapeDtypeStruct((cols, cols), F32))
    held = tuple(pltpu.VMEM(x.shape, x.dtype) for x in shapes)
    results = pl.pallas_call(
        fused,
        out_shape=held,
        in_specs=[free] * 9,
        out_specs=(pl.BlockSpec(memory_space=pltpu.VMEM),) * 5,
        scratch_shapes=[
            pltpu.VMEM((rows, cols), BF16),
            pltpu.VMEM((rows, cols), BF16),
            pltpu.VMEM((rows, cols), BF16),
            pltpu.VMEM((heads_here, width, width), F32),
            pltpu.VMEM((heads_here, width), F32),
            pltpu.VMEM((cols, wide), BF16),
            pltpu.SMEM((1, heads_here), F32),
            pltpu.SMEM((1, heads_here), F32),
            pltpu.VMEM((rows, wide), BF16),
            pltpu.VMEM((rows, wide), BF16),
            pltpu.VMEM(small, F32),
            pltpu.VMEM(small, F32),
            pltpu.VMEM(small, F32),
            pltpu.VMEM(small, F32),
            pltpu.VMEM(small, BF16),
            pltpu.VMEM(small, BF16),
            pltpu.VMEM(small, BF16),
            pltpu.VMEM(small, BF16),
            pltpu.VMEM((heads_here, rows, rows), BF16),
            pltpu.VMEM((heads_here, width, rows), F32),
            pltpu.VMEM((rows, cols), F32),
            pltpu.VMEM((rows, cols), F32),
            pltpu.VMEM((rows, cols), F32),
            pltpu.VMEM((rows, cols), BF16),
            pltpu.VMEM((cols, rows), BF16),
            pltpu.VMEM((cols, rows), BF16),
            pltpu.VMEM((rows, cols), F32),
            pltpu.VMEM((rows, cols), F32),
            pltpu.VMEM((rows, cols), F32),
            pltpu.VMEM((2, cols, cols), BF16),
            pltpu.VMEM((2, cols, cols), BF16),
            pltpu.VMEM((cols, cols), BF16),
            pltpu.VMEM((3, rows, cols), BF16),
            pltpu.VMEM((3, rows, cols), BF16),
            dma((7,)), dma((7,)), dma((7,)), dma((7,)), dma((4,)), dma((4,)),
            dma((4,)), dma((4,)), dma((4,)), dma((4,)),
            dma((2, 4)), dma((2, 4)), dma((4,)), dma((4,)),
            dma((3,)), dma((3,)), dma((9,)),
        ],
        compiler_params=pltpu.CompilerParams(
            collective_id=0, has_side_effects=True, vmem_limit_bytes=48 << 20
        ),
    )(
        *(
            pltpu.with_memory_space_constraint(x, pltpu.HBM)
            for x in (
                queries, key_rows, values, memory_in, norm_in, decays,
                gate_bias.reshape(1, heads_here), out_weight, out_grad,
            )
        )
    )
    results = [pltpu.with_memory_space_constraint(x, pltpu.VMEM) for x in results]
    return pl.pallas_call(
        settle,
        out_shape=shapes,
        in_specs=[pl.BlockSpec(memory_space=pltpu.VMEM)] * 5,
        out_specs=(free,) * 5,
        scratch_shapes=[dma((5,))],
    )(*results)


def solution(mesh):
    return jax.shard_map(
        shards,
        mesh=mesh,
        in_specs=(
            P(("groups", "ctx"), "heads"),
            P(("groups", "ctx"), "heads"),
            P(("groups", "ctx"), "heads"),
            P(("groups", "heads"), None, None),
            P(("groups", "heads"), None),
            P(("groups", "ctx"), "heads"),
            P("heads"),
            P("heads", None),
            P(("groups", "ctx"), "heads"),
        ),
        out_specs=(
            P(("groups", "ctx"), "heads"),
            P(("groups", "ctx"), "heads"),
            P(("groups", "ctx"), "heads"),
            P(("groups", "ctx"), "heads"),
            P(("groups", "heads"), "ctx"),
        ),
        check_vma=False,
    )
```
